32 devices in a mesh: member: 4 (over y, core), lon: 4 (over z), lat: 2 (over x).
Axes of the slice: x: 2, y: 2, z: 4, core: 2. Of those that a mesh axis runs over, the one named last changes fastest.
Arguments:
- member_state: float32 [4, 16, 256, 1536], P('member', None, 'lat', 'lon'), may hold values from -12 to 12
- column_depth: float32 [256, 1536], P('lat', 'lon'), may hold values from 0.5 to 2
- rotation: float32 [256, 1536], P('lat', 'lon'), may hold values from -0.2 to 0.2
- diffusivity: float32 [5, 256, 1536], P(None, 'lat', 'lon'), may hold values from 0.02 to 0.2
- ocean_mask: int32 [256, 1536], P('lat', 'lon'), may hold values from 0 to 1, as said below
- region_id: int32 [256, 1536], P('lat', 'lon'), may hold values from 0 to 15, as said below
- target_rms: float32 [16], replicated, may hold values from 0.2 to 1
Outputs:
- bred_state: float32 [4, 16, 256, 1536], P('member', None, 'lat', 'lon')
- growth_rms: float32 [4, 16], P('member')
The draws below stay inside these ranges and needn't reach their ends.
Inputs may be any that keep to these rules, and one draw needn't show every extreme that they name: `ocean_mask`: 1 marks an ocean cell. `region_id`: every region id holds ocean cells.
All inputs are finite; a program needn't handle non-finite values.
Results may differ from the reference program's by a relative error of at most 0.0003.
Values sent between devices are 32-bit elements; how exact they have to be, the bound alone decides.
A program may use at most 64 MiB of HBM per device.

```python
import math
import jax
import jax.numpy as jnp
from jax import lax

LEV = 5
STEPS = 2
SECTORS = 8
MEMBERS = 4
CHANNELS = 16
REGIONS = 16
NLAT = 256
NLON = 1536


def draw_member_state(key, part):
    keys = jax.random.split(key, 2)
    shape = (MEMBERS, CHANNELS, NLAT, NLON)
    ramp = jnp.exp(math.log(3.0) * jnp.arange(NLON).astype(jnp.float32) / NLON)[None, None, None, :]
    rows = jnp.exp(jax.random.uniform(keys[0], (1, 1, NLAT, 1), jnp.float32, 0.0, math.log(3.3)))
    scale = 0.3 * rows * ramp
    return jax.random.truncated_normal(keys[1], -4.0, 4.0, shape, jnp.float32) * scale


def draw_ocean_mask(key, part):
    coins = jax.random.randint(key, (NLAT, NLON), 0, 4)
    rows = jnp.arange(NLAT)[:, None]
    ocean = jnp.where(coins > 0, 1, 0)
    edge = (rows == 0) | (rows == NLAT - 1)
    return jnp.where(edge, 1, ocean).astype(jnp.int32)


def draw_region_id(key, part):
    keys = jax.random.split(key, 2)
    offset = jax.random.randint(keys[0], (NLAT, 1), 0, SECTORS)
    columns = jnp.arange(NLON)[None, :]
    block_width = max(NLON // (4 * SECTORS), 1)
    sector = (columns // block_width + offset) % SECTORS
    bound = jax.random.randint(keys[1], (1, NLON), NLAT // 4, 3 * NLAT // 4 + 1)
    rows = jnp.arange(NLAT)[:, None]
    return (sector * 2 + jnp.where(rows >= bound, 1, 0)).astype(jnp.int32)


def block_scale(own_key, dims, cuts, low, top_value):
    level, own = 1.0, jax.random.fold_in(own_key, 6)
    for dim, shards_of in cuts:
        steps = jnp.exp(jax.random.uniform(jax.random.fold_in(own, dim), (shards_of,), jnp.float32, low / len(cuts), top_value / len(cuts)))
        level = level * jnp.repeat(steps, dims[dim] // shards_of).reshape([-1 if axis == dim else 1 for axis in range(len(dims))])
    return level


def setup_inputs(seed: int = 0) -> dict:
    key_list = jax.random.split(jax.random.key(seed), 8)
    return {
        "member_state": draw_member_state(jax.random.fold_in(key_list[7], 71), 0),
        "column_depth": jnp.clip(jnp.exp(math.log(2.0) - 1.3862944 * jax.random.uniform(key_list[1], (NLAT, NLON), jnp.float32) ** block_scale(key_list[1], (NLAT, NLON), ((0, 2), (1, 4)), -0.2, 0.2)), 0.5, 2.0),
        "rotation": jnp.clip(jax.random.uniform(key_list[2], (NLAT, NLON), jnp.float32, -0.2, 0.2) * block_scale(key_list[2], (NLAT, NLON), ((0, 2), (1, 4)), -0.4, 0.0), -0.2, 0.2),
        "diffusivity": jnp.clip(jnp.exp(math.log(0.2) - 2.3025851 * jax.random.uniform(key_list[3], (LEV, NLAT, NLON), jnp.float32) ** block_scale(key_list[3], (LEV, NLAT, NLON), ((1, 2), (2, 4)), -0.2, 0.2)), 0.02, 0.2),
        "ocean_mask": draw_ocean_mask(jax.random.fold_in(key_list[7], 71), 0),
        "region_id": draw_region_id(jax.random.fold_in(key_list[7], 71), 0),
        "target_rms": jnp.clip(jnp.exp(jax.random.uniform(key_list[6], (REGIONS,), jnp.float32, math.log(0.2), math.log(1.0))), 0.2, 1.0),
    }


divergence_gain = 0.25
pressure_gain = 0.25
buoyancy_gain = 0.1
advection_gain = 0.05
epsilon = 1e-06

def neighbours(field):
    east_side = jnp.roll(field, -1, axis=-1)
    west_side = jnp.roll(field, 1, axis=-1)
    zero_row = jnp.zeros_like(field[..., :1, :])
    north_side = jnp.concatenate([field[..., 1:, :], zero_row], axis=-2)
    south_side = jnp.concatenate([zero_row, field[..., :-1, :]], axis=-2)
    return (east_side, west_side, north_side, south_side)

def advance(state, column_depth, rotation, diffusivity, ocean_float):
    east_side, west_side, north_side, south_side = neighbours(state)
    zonal_diff = east_side - west_side
    merid_diff = north_side - south_side
    laplacian = east_side + west_side + north_side + south_side - 4.0 * state
    surface = state[:, 0]
    zonal_flow = state[:, 1:1 + LEV]
    merid_flow = state[:, 1 + LEV:1 + 2 * LEV]
    heat_field = state[:, 1 + 2 * LEV:]
    divergence = lax.optimization_barrier(jnp.mean(zonal_diff[:, 1:1 + LEV], axis=1)) + lax.optimization_barrier(jnp.mean(merid_diff[:, 1 + LEV:1 + 2 * LEV], axis=1))
    new_surface = ocean_float * (surface - divergence_gain * column_depth * divergence)
    s_east, s_west, s_north, s_south = neighbours(new_surface)
    slope_east = (s_east - s_west)[:, None]
    slope_north = (s_north - s_south)[:, None]
    heat_east = zonal_diff[:, 1 + 2 * LEV:]
    heat_north = merid_diff[:, 1 + 2 * LEV:]
    new_zonal = ocean_float * (zonal_flow + rotation * merid_flow - pressure_gain * slope_east - buoyancy_gain * heat_east + diffusivity * laplacian[:, 1:1 + LEV])
    new_merid = ocean_float * (merid_flow - rotation * zonal_flow - pressure_gain * slope_north - buoyancy_gain * heat_north + diffusivity * laplacian[:, 1 + LEV:1 + 2 * LEV])
    new_heat = ocean_float * (heat_field + diffusivity * laplacian[:, 1 + 2 * LEV:] - advection_gain * (new_zonal * heat_east + new_merid * heat_north))
    return jnp.concatenate([new_surface[:, None], new_zonal, new_merid, new_heat], axis=1)

def reference(member_state, column_depth, rotation, diffusivity, ocean_mask, region_id, target_rms):
    ocean_float = ocean_mask.astype(jnp.float32)
    state = member_state
    for step_index in range(STEPS):
        state = advance(state, column_depth, rotation, diffusivity, ocean_float)
    control = state[0:1]
    difference = state - control
    cell_sum = ocean_float * lax.optimization_barrier(jnp.sum(difference * difference, axis=1))
    labels = jnp.arange(REGIONS).astype(jnp.int32)
    onehot = (region_id[None] == labels[:, None, None]).astype(jnp.float32)
    squares = jnp.einsum('rji,mji->mr', onehot, cell_sum, precision=lax.Precision.HIGHEST)
    counts = jnp.einsum('rji,ji->r', onehot, ocean_float, precision=lax.Precision.HIGHEST)
    growth = jnp.sqrt(squares / (counts * CHANNELS) + epsilon)
    factor = target_rms[None] / growth
    cell_factor = jnp.einsum('mr,rji->mji', factor, onehot, precision=lax.Precision.HIGHEST)
    bred = control + cell_factor[:, None] * difference
    return (bred, growth)
```

```python
import functools

import jax
import jax.numpy as jnp
from jax import lax
from jax.experimental import pallas as pl
from jax.experimental.pallas import tpu as pltpu
from jax.sharding import PartitionSpec as P

LEV = 5
STEPS = 2
MARGIN = 2 * STEPS
TILE = 8
LANES = 128
FIRST_ROWS = 4
SEND_AT = 5
MIDS_EARLY = 12
RIMS_EARLY = 12
KERNEL_BYTES = 56 * 2**20
WRITE_BYTES = 16 * 2**20

divergence_gain = 0.25
pressure_gain = 0.25
buoyancy_gain = 0.1
advection_gain = 0.05
epsilon = 1e-06

MESH = pl.DeviceIdType.MESH


def cycle_kernel(
    sizes,
    state_in, depth_in, rotation_in, diffusivity_in, mask_in, region_in, target_in,
    bred, growth_out,
    field, middle, surface_one, surface_two,
    own_mid, own_rim, control_mid, control_rim, lent_mid, lent_rim,
    pack, from_east, from_west, send_north, send_south, from_north, from_south,
    mask, region, squares, lent_squares, counts, gathered, loan_out, loan, value, factor,
    in_sem, halo_send, halo_recv, pair_send, pair_recv, next_send, next_recv,
    lend_send, lend_recv, loan_send, loan_recv, sum_send, sum_recv, go,
):
    members, lons, lats = sizes
    channels, rows, columns = state_in.shape
    regions = squares.shape[0]
    fields = field.shape[0]
    groups = pack.shape[0]
    slots = columns // LANES
    halo = slots
    tiles = rows // TILE
    tall = rows + 2 * TILE
    clients = members // 2 - 1
    DEPTH, ROT, OCEAN, DIFF = channels, channels + 1, channels + 2, channels + 3
    mids = list(range(1, slots - 1))
    rims = [0, slots - 1]
    half = TILE // 2
    first_tiles = min(FIRST_ROWS, tiles)
    mids_early = min(MIDS_EARLY, tiles)
    rims_early = min(RIMS_EARLY, tiles)

    me = lax.axis_index("member")
    lon = lax.axis_index("lon")
    lat = lax.axis_index("lat")
    core = lax.rem(me, 2)
    client = me // 2 - 1

    down = 2 * lat >= lats
    step = jnp.where(down, -1, 1)
    has_north = lat < lats - 1
    has_south = lat > 0

    def tile_of(order):
        return jnp.where(down, tiles - 1 - order, order)

    def tall_of(order):
        return jnp.where(down, tiles + 1 - order, order)

    def at(dlat, dlon, member=None):
        return {
            "member": me if member is None else member,
            "lon": lax.rem(lon + dlon + lons, lons),
            "lat": lax.rem(lat + dlat + lats, lats),
        }

    def to_member(other):
        return {"member": other, "lon": lon, "lat": lat}

    even = core == 0
    has_pair = even & (me + 1 < members)
    has_next = even & (me + 2 < members)
    parent = jnp.where(even, me - 2, me - 1)
    lender = core
    peers = [(a, b) for a in range(lats) for b in range(lons) if (a, b) != (0, 0)]
    peers.sort(key=lambda p: -(p[0] + min(p[1], lons - p[1]) + p[1]))

    first_rows = first_tiles * TILE
    other_rows = rows - first_rows
    first_row = pl.multiple_of(jnp.where(down, rows - first_rows, 0), TILE)
    other_row = pl.multiple_of(jnp.where(down, 0, first_rows), TILE)

    def loads(index, row, count):
        src = pl.ds(row, count)
        dst = pl.ds(pl.multiple_of(row + TILE, TILE), count)
        copies = []
        for c in range(slots):
            part = slice(c * LANES, (c + 1) * LANES)
            copies += [
                (state_in.at[:, src, part], field.at[0:channels, c, dst, :]),
                (depth_in.at[src, part], field.at[DEPTH, c, dst, :]),
                (rotation_in.at[src, part], field.at[ROT, c, dst, :]),
                (diffusivity_in.at[:, src, part], field.at[DIFF:fields, c, dst, :]),
            ]
        copies.append((mask_in.at[src, :], mask.at[src, :]))
        return [pltpu.make_async_copy(a, b, in_sem.at[index, n]) for n, (a, b) in enumerate(copies)]

    load_first = loads(0, first_row, first_rows)
    load_region = pltpu.make_async_copy(region_in, region, in_sem.at[2, 0])
    for load in load_first:
        load.start()

    barrier = pltpu.get_barrier_semaphore()

    def greet(device):
        pl.semaphore_signal(barrier, inc=1, device_id=device, device_id_type=MESH)

    client_members = list(range(2, members, 2))

    @pl.when(me == 0)
    def _():
        greet(to_member(1))
        for a, b in peers:
            greet(at(a, b, 1))
        for other in client_members:
            greet(to_member(other))

    @pl.when(me > 0)
    def _():
        for a, b in peers:
            greet(at(a, b))
        greet(to_member(parent))

    @pl.when(me == 1)
    def _():
        for other in client_members:
            greet(to_member(other + 1))

    @pl.when(me > 1)
    def _():
        greet(to_member(lender))

    @pl.when(me == 0)
    def _():
        pl.semaphore_wait(barrier, 1 + (1 if members > 2 else 0) + clients)

    def all_here():
        @pl.when(me == 0)
        def _():
            pl.semaphore_wait(go, 1)

        @pl.when(me > 1)
        def _():
            pl.semaphore_wait(
                barrier,
                len(peers) + 1 + has_pair.astype(jnp.int32) + has_next.astype(jnp.int32),
            )

    @pl.when(me == 1)
    def _():
        pl.semaphore_wait(barrier, 2 * len(peers) + 1 + clients)
        pl.semaphore_signal(go, inc=1, device_id=to_member(0), device_id_type=MESH)

    lane = lax.broadcasted_iota(jnp.int32, (TILE, LANES), 1)
    zero_tile = jnp.zeros((TILE, LANES), jnp.float32)
    low_lanes = lane < LANES // 2

    for load in load_first:
        load.wait()
    load_other = loads(1, other_row, other_rows) if other_rows else []
    for load in load_other + [load_region]:
        load.start()

    def make_ocean(t, carry):
        r = pl.multiple_of(t * TILE, TILE)
        for c in range(slots):
            field[OCEAN, c, pl.ds(pl.multiple_of(r + TILE, TILE), TILE), :] = mask[
                pl.ds(r, TILE), c * LANES : (c + 1) * LANES
            ].astype(jnp.float32)
        return carry

    lax.fori_loop(first_row // TILE, first_row // TILE + first_tiles, make_ocean, 0)

    def remote(src, dst, index, device):
        return pltpu.make_async_remote_copy(
            src_ref=src, dst_ref=dst, send_sem=halo_send.at[index], recv_sem=halo_recv.at[index],
            device_id=device, device_id_type=MESH,
        )

    whole = slice(TILE, TILE + rows)
    last = slice(rows - TILE, rows)
    first = slice(0, TILE)
    above = slice(rows + TILE, rows + 2 * TILE)
    north = [
        remote(send_north, from_south, 0, at(1, 0)),
        remote(pack.at[:, last, :], from_west.at[:, first, :], 4, at(1, 1)),
        remote(pack.at[:, last, :], from_east.at[:, first, :], 5, at(1, -1)),
    ]
    south = [
        remote(send_south, from_north, 1, at(-1, 0)),
        remote(pack.at[:, first, :], from_west.at[:, above, :], 6, at(-1, 1)),
        remote(pack.at[:, first, :], from_east.at[:, above, :], 7, at(-1, -1)),
    ]
    sideways = [
        remote(pack, from_west.at[:, whole, :], 2, at(0, 1)),
        remote(pack, from_east.at[:, whole, :], 3, at(0, -1)),
    ]

    def pack_tile(t, carry):
        r = pl.multiple_of(t * TILE, TILE)
        now = pl.ds(pl.multiple_of(r + TILE, TILE), TILE)
        packed = [zero_tile] * groups
        for f in range(fields):
            g, s = divmod(f * 2 * MARGIN, LANES)
            edges = jnp.where(low_lanes, field[f, 0, now, :], field[f, slots - 1, now, :])
            here = (lane >= s) & (lane < s + 2 * MARGIN)
            packed[g] = jnp.where(here, pltpu.roll(edges, s + MARGIN, 1), packed[g])
        for g in range(groups):
            pack[g, pl.ds(r, TILE), :] = packed[g]
        return carry

    def pack_halos():
        for load in load_other + [load_region]:
            load.wait()
        if other_rows:
            lax.fori_loop(other_row // TILE, other_row // TILE + other_rows // TILE, make_ocean, 0)
        for k in range(fields // 2):
            for c in range(slots):
                send_north[k, c, 0:half, :] = field[2 * k, c, rows + half : rows + TILE, :]
                send_north[k, c, half:TILE, :] = field[2 * k + 1, c, rows + half : rows + TILE, :]
                send_south[k, c, 0:half, :] = field[2 * k, c, TILE : TILE + half, :]
                send_south[k, c, half:TILE, :] = field[2 * k + 1, c, TILE : TILE + half, :]
        lax.fori_loop(0, tiles, pack_tile, 0)

    def send_halos():
        all_here()

        @pl.when(has_north)
        def _():
            for copy in north:
                copy.start()

        @pl.when(has_south)
        def _():
            for copy in south:
                copy.start()

        for copy in sideways:
            copy.start()

    def south_rows():
        @pl.when(has_south)
        def _():
            north[0].wait_recv()

        @pl.when(jnp.logical_not(has_south))
        def _():
            from_south[...] = jnp.zeros_like(from_south)

        for k in range(fields // 2):
            for c in range(slots):
                field[2 * k, c, half:TILE, :] = from_south[k, c, 0:half, :]
                field[2 * k + 1, c, half:TILE, :] = from_south[k, c, half:TILE, :]
                field[2 * k, c, 0:half, :] = from_south[k, c, 0:half, :]
                field[2 * k + 1, c, 0:half, :] = from_south[k, c, half:TILE, :]

    def north_rows():
        @pl.when(has_north)
        def _():
            south[0].wait_recv()

        @pl.when(jnp.logical_not(has_north))
        def _():
            from_north[...] = jnp.zeros_like(from_north)

        base = rows + TILE
        for k in range(fields // 2):
            for c in range(slots):
                field[2 * k, c, base : base + half, :] = from_north[k, c, 0:half, :]
                field[2 * k + 1, c, base : base + half, :] = from_north[k, c, half:TILE, :]
                field[2 * k, c, base + half : base + TILE, :] = from_north[k, c, 0:half, :]
                field[2 * k + 1, c, base + half : base + TILE, :] = from_north[k, c, half:TILE, :]

    def join_middle(order):
        now = pl.ds(pl.multiple_of(tall_of(order) * TILE, TILE), TILE)
        for f in range(fields):
            field[f, halo, now, :] = jnp.where(low_lanes, field[f, slots - 1, now, :], field[f, 0, now, :])

    easterly = lax.rem(lane, 2 * MARGIN) >= MARGIN

    def join_halo(order):
        now = pl.ds(pl.multiple_of(tall_of(order) * TILE, TILE), TILE)
        both = [jnp.where(easterly, from_east[g, now, :], from_west[g, now, :]) for g in range(groups)]
        for f in range(fields):
            g, s = divmod(f * 2 * MARGIN, LANES)
            field[f, halo, now, :] = pltpu.roll(both[g], LANES - s - MARGIN, 1)

    class Ring:
        def __init__(self, ring, todo):
            self.todo = todo
            size = len(ring)
            place = {c: i for i, c in enumerate(ring)}
            self.east = {c: ring[(place[c] + 1) % size] for c in todo}
            self.west = {c: ring[(place[c] - 1) % size] for c in todo}
            self.used = sorted(set(todo) | set(self.east.values()) | set(self.west.values()))

        def sides(self, q):
            to_east = {c: pltpu.roll(q[c], LANES - 1, 1) for c in {*self.todo, *self.east.values()}}
            to_west = {c: pltpu.roll(q[c], 1, 1) for c in {*self.todo, *self.west.values()}}
            e = {c: jnp.where(lane == LANES - 1, to_east[self.east[c]], to_east[c]) for c in self.todo}
            w = {c: jnp.where(lane == 0, to_west[self.west[c]], to_west[c]) for c in self.todo}
            return e, w

    def surface_rows(src, dst, ring, r):
        now, above_r, below_r = pl.ds(r, TILE), pl.ds(r + 1, TILE), pl.ds(r - 1, TILE)

        def add_up(base, c, where):
            total = src[base, c, where, :]
            for k in range(1, LEV):
                total = total + src[base + k, c, where, :]
            return total

        e, w = ring.sides({c: add_up(1, c, now) for c in ring.used})
        for c in ring.todo:
            n, s = add_up(1 + LEV, c, above_r), add_up(1 + LEV, c, below_r)
            divergence = (e[c] - w[c]) + (n - s)
            dst[c, now, :] = field[OCEAN, c, now, :] * (
                src[0, c, now, :] - (divergence_gain / LEV) * field[DEPTH, c, now, :] * divergence
            )

    def update_rows(src, surface, ring, r, write):
        now, above_r, below_r = pl.ds(r, TILE), pl.ds(r + 1, TILE), pl.ds(r - 1, TILE)
        h = {c: surface[c, now, :] for c in ring.used}
        e, w = ring.sides(h)
        slope_east, slope_north = {}, {}
        for c in ring.todo:
            slope_east[c] = pressure_gain * (e[c] - w[c])
            slope_north[c] = pressure_gain * (surface[c, above_r, :] - surface[c, below_r, :])
            write(0, c, h[c])
        for k in range(LEV):
            iu, iv, ic = 1 + k, 1 + LEV + k, 1 + 2 * LEV + k
            u = {c: src[iu, c, now, :] for c in ring.used}
            v = {c: src[iv, c, now, :] for c in ring.used}
            t = {c: src[ic, c, now, :] for c in ring.used}
            ue, uw = ring.sides(u)
            ve, vw = ring.sides(v)
            te, tw = ring.sides(t)
            for c in ring.todo:
                ocean = field[OCEAN, c, now, :]
                rotation = field[ROT, c, now, :]
                mixing = field[DIFF + k, c, now, :]
                tn, ts = src[ic, c, above_r, :], src[ic, c, below_r, :]
                heat_east, heat_north = te[c] - tw[c], tn - ts
                around_u = (ue[c] + uw[c]) + (src[iu, c, above_r, :] + src[iu, c, below_r, :])
                around_v = (ve[c] + vw[c]) + (src[iv, c, above_r, :] + src[iv, c, below_r, :])
                around_t = (te[c] + tw[c]) + (tn + ts)
                new_u = ocean * (
                    u[c] + rotation * v[c] - slope_east[c] - buoyancy_gain * heat_east
                    + mixing * (around_u - 4.0 * u[c])
                )
                new_v = ocean * (
                    v[c] - rotation * u[c] - slope_north[c] - buoyancy_gain * heat_north
                    + mixing * (around_v - 4.0 * v[c])
                )
                new_t = ocean * (
                    t[c] + mixing * (around_t - 4.0 * t[c])
                    - advection_gain * (new_u * heat_east + new_v * heat_north)
                )
                write(iu, c, new_u)
                write(iv, c, new_v)
                write(ic, c, new_t)

    def run_pass(join, one, two, own, own_slots, at_order, leave):
        def body(i, carry):
            j = i - 1
            at_order(j)
            join(j + 2)
            r = jnp.where(down, rows - TILE * j, TILE + TILE * j)
            surface_rows(field, surface_one, one, r + 3 * step)
            r_one = r + 2 * step

            def middle_write(channel, c, new):
                middle[channel, c, pl.ds(r_one, TILE), :] = new

            update_rows(field, surface_one, one, r_one, middle_write)
            surface_rows(middle, surface_two, one, r + step)

            @pl.when(j >= 0)
            def _():
                t = tile_of(j)

                def last_write(channel, c, new):
                    own[t, channel, own_slots[c]] = new

                update_rows(
                    middle, surface_two, two, pl.multiple_of(r, TILE), last_write
                )
                leave(j, t)

            return carry

        lax.fori_loop(0, tiles + 1, body, 0)

    def pair_copy(ref, kind, t):
        return pltpu.make_async_remote_copy(
            src_ref=ref.at[t], dst_ref=ref.at[t],
            send_sem=pair_send.at[kind, t], recv_sem=pair_recv.at[kind, t],
            device_id=to_member(me + 1), device_id_type=MESH,
        )

    def next_copy(ref, kind, t):
        return pltpu.make_async_remote_copy(
            src_ref=ref.at[t], dst_ref=ref.at[t],
            send_sem=next_send.at[kind, t], recv_sem=next_recv.at[kind, t],
            device_id=to_member(me + 2), device_id_type=MESH,
        )

    def lend_copy(own, lent, kind, early, which, order):
        return pltpu.make_async_remote_copy(
            src_ref=own.at[tile_of(order)], dst_ref=lent.at[which, order - early],
            send_sem=lend_send.at[kind, which, order - early],
            recv_sem=lend_recv.at[kind, which, order - early],
            device_id=to_member(lender), device_id_type=MESH,
        )

    def leave_mid(order, t):
        @pl.when(me == 0)
        def _():
            for k in range(channels):
                for n in range(len(mids)):
                    control_mid[t, k, n] = own_mid[t, k, n]
            pair_copy(control_mid, 0, t).start()

            @pl.when(has_next & (order < mids_early))
            def _():
                next_copy(control_mid, 0, t).start()

        @pl.when((me > 1) & (order >= mids_early))
        def _():
            lend_copy(own_mid, lent_mid, 0, mids_early, client, order).start()

    def leave_rim(order, t):
        @pl.when(me == 0)
        def _():
            for k in range(channels):
                for n in range(len(rims)):
                    control_rim[t, k, n] = own_rim[t, k, n]
            pair_copy(control_rim, 1, t).start()

            @pl.when(has_next)
            def _():
                next_copy(control_rim, 1, t).start()

        @pl.when((me > 1) & (order >= rims_early))
        def _():
            lend_copy(own_rim, lent_rim, 1, rims_early, client, order).start()

    def start_rows():
        @pl.when(down)
        def _():
            north_rows()

        @pl.when(jnp.logical_not(down))
        def _():
            south_rows()

    def end_rows():
        @pl.when(down)
        def _():
            south_rows()

        @pl.when(jnp.logical_not(down))
        def _():
            north_rows()

    load_at = min(first_tiles - 1, tiles - 1)
    send_at = max(load_at, min(SEND_AT, tiles - 2))

    def events_mid(j):
        if lats <= 2:
            @pl.when(j == load_at)
            def _():
                pack_halos()

            @pl.when(j == send_at)
            def _():
                send_halos()

        @pl.when(j == tiles - 1)
        def _():
            end_rows()

    if lats > 2:
        pack_halos()
        send_halos()
    start_rows()
    join_middle(0)
    ring_mid = mids + [halo]
    run_pass(
        join_middle, Ring(ring_mid, ring_mid), Ring(ring_mid, mids),
        own_mid, {c: n for n, c in enumerate(mids)}, events_mid, leave_mid,
    )

    for copy in sideways:
        copy.wait_recv()

    @pl.when(has_north)
    def _():
        for copy in south[1:]:
            copy.wait_recv()

    @pl.when(has_south)
    def _():
        for copy in north[1:]:
            copy.wait_recv()

    @pl.when(jnp.logical_not(has_north))
    def _():
        for g in range(groups):
            from_east[g, above, :] = zero_tile
            from_west[g, above, :] = zero_tile

    @pl.when(jnp.logical_not(has_south))
    def _():
        for g in range(groups):
            from_east[g, first, :] = zero_tile
            from_west[g, first, :] = zero_tile

    join_halo(0)
    ring_all = list(range(slots)) + [halo]
    run_pass(
        join_halo, Ring(ring_all, [slots - 1, halo, 0]), Ring(ring_all, rims),
        own_rim, {c: n for n, c in enumerate(rims)}, lambda j: None, leave_rim,
    )

    @pl.when((me == 0) & has_next)
    def _():
        def body(order, carry):
            next_copy(control_mid, 0, tile_of(order)).start()
            return carry

        lax.fori_loop(mids_early, tiles, body, 0)

    def clear(ref):
        for k in range(regions):
            ref[k] = zero_tile

    def ids_at(t, c):
        return region[pl.ds(pl.multiple_of(t * TILE, TILE), TILE), c * LANES : (c + 1) * LANES]

    def ocean_at(t, c):
        return field[OCEAN, c, pl.ds(pl.multiple_of(t * TILE + TILE, TILE), TILE), :]

    def add_regions(ref, items):
        for k in range(regions):
            total = ref[k]
            for ids, amount in items:
                total = total + jnp.where(ids == k, amount, 0.0)
            ref[k] = total

    def compare(ref, mine, its, t, part):
        items = []
        for n, c in enumerate(part):
            total = None
            for k in range(channels):
                d = mine(k, n) - its(k, n)
                total = d * d if total is None else total + d * d
            items.append((ids_at(t, c), ocean_at(t, c) * total))
        add_regions(ref, items)

    def share(which):
        for p, (a, b) in enumerate(peers):
            pltpu.make_async_remote_copy(
                src_ref=gathered.at[which, 0], dst_ref=gathered.at[which, p + 1],
                send_sem=sum_send.at[which, p], recv_sem=sum_recv.at[which, p],
                device_id=at(a, b), device_id_type=MESH,
            ).start()

    def collect(which):
        for p, (a, b) in enumerate(peers):
            pltpu.make_async_remote_copy(
                src_ref=gathered.at[which, 0], dst_ref=gathered.at[which, p + 1],
                send_sem=sum_send.at[which, p], recv_sem=sum_recv.at[which, p],
                device_id=at(a, b), device_id_type=MESH,
            ).wait()
        total = gathered[which, 0]
        for p in range(len(peers)):
            total = total + gathered[which, p + 1]
        return jnp.sum(total, axis=1, keepdims=True)

    clear(squares)
    clear(counts)

    def count(t, carry):
        add_regions(counts, [(ids_at(t, c), ocean_at(t, c)) for c in range(slots)])
        return carry

    lax.fori_loop(0, tiles, count, 0)
    gathered[0, 0] = jnp.sum(counts[...], axis=1)
    share(0)

    kinds = [
        (0, own_mid, control_mid, lent_mid, mids, mids_early),
        (1, own_rim, control_rim, lent_rim, rims, rims_early),
    ]

    def take(kind, order):
        _, own, control, _, part, _ = kinds[kind]
        t = tile_of(order)

        @pl.when(even)
        def _():
            next_copy(control, kind, t).wait_recv()

            @pl.when(has_pair)
            def _():
                pair_copy(control, kind, t).start()

            @pl.when(has_next)
            def _():
                next_copy(control, kind, t).start()

        @pl.when(jnp.logical_not(even))
        def _():
            pair_copy(control, kind, t).wait_recv()

    def weigh(kind, order):
        _, own, control, _, part, _ = kinds[kind]
        t = tile_of(order)
        compare(squares, lambda k, n: own[t, k, n], lambda k, n: control[t, k, n], t, part)

    def loop(begin, end, *actions):
        def body(order, carry):
            for action in actions:
                action(order)
            return carry

        lax.fori_loop(begin, end, body, 0)

    @pl.when(me > 0)
    def _():
        late_mids = jnp.where(me == 1, tiles, mids_early)
        late_rims = jnp.where(me == 1, tiles, rims_early)
        loop(0, mids_early, lambda o: take(0, o), lambda o: weigh(0, o))
        loop(0, late_rims, lambda o: take(1, o), lambda o: weigh(1, o))
        loop(mids_early, late_mids, lambda o: take(0, o), lambda o: weigh(0, o))

    def loan_copy(other, which):
        return pltpu.make_async_remote_copy(
            src_ref=loan_out.at[which], dst_ref=loan,
            send_sem=loan_send.at[which], recv_sem=loan_recv,
            device_id=to_member(other), device_id_type=MESH,
        )

    def lend(which, other):
        clear(lent_squares)
        for kind, own, control, lent, part, early in kinds:
            def body(order, carry):
                lend_copy(own, lent, kind, early, which, order).wait_recv()
                t = tile_of(order)
                compare(
                    lent_squares,
                    lambda k, n: lent[which, order - early, k, n],
                    lambda k, n: control[t, k, n], t, part,
                )
                return carry

            lax.fori_loop(early, tiles, body, 0)
        loan_out[which] = jnp.sum(lent_squares[...], axis=1)
        loan_copy(other, which).start()

    gathered[1, 0] = jnp.sum(squares[...], axis=1)

    @pl.when(me < 2)
    def _():
        for which in range(clients):
            lend(which, 2 * which + 2 + core)

    @pl.when(me > 1)
    def _():
        loan_copy(me, 0).wait_recv()
        gathered[1, 0] = gathered[1, 0] + loan[...]

    share(1)
    count_sum = collect(0)
    square_sum = collect(1)
    growth = jnp.sqrt(square_sum / (count_sum * channels) + epsilon)
    growth_wide = jnp.broadcast_to(growth, (regions, LANES))
    growth_out[...] = growth_wide
    for k in range(regions):
        value[k] = jnp.broadcast_to(target_in[k] / growth_wide[k : k + 1, :], (TILE, LANES))

    def make_factor(t, carry):
        for c in range(slots):
            ids = ids_at(t, c)
            total = zero_tile
            for k in range(regions):
                total = jnp.where(ids == k, value[k], total)
            factor[t, c] = total
        return carry

    lax.fori_loop(0, tiles, make_factor, 0)

    def breed(kind, order):
        _, own, control, _, part, _ = kinds[kind]
        t = tile_of(order)
        now = pl.ds(pl.multiple_of(t * TILE, TILE), TILE)
        for n, c in enumerate(part):
            scale = factor[t, c]
            for k in range(channels):
                base = control[t, k, n]
                bred[k, now, c * LANES : (c + 1) * LANES] = base + scale * (own[t, k, n] - base)

    def take_late(kind, order):
        @pl.when(me > 1)
        def _():
            take(kind, order)

    loop(0, mids_early, lambda o: breed(0, o))
    loop(0, rims_early, lambda o: breed(1, o))
    loop(rims_early, tiles, lambda o: take_late(1, o), lambda o: breed(1, o))
    loop(mids_early, tiles, lambda o: take_late(0, o), lambda o: breed(0, o))

    for copy in sideways:
        copy.wait_send()

    @pl.when(has_north)
    def _():
        for copy in north:
            copy.wait_send()

    @pl.when(has_south)
    def _():
        for copy in south:
            copy.wait_send()

    def finish(t, carry):
        for kind, own, control, lent, part, early in kinds:
            @pl.when(has_pair)
            def _():
                pair_copy(control, kind, t).wait_send()

            @pl.when(has_next)
            def _():
                next_copy(control, kind, t).wait_send()

        return carry

    lax.fori_loop(0, tiles, finish, 0)

    @pl.when(me < 2)
    def _():
        for which in range(clients):
            loan_copy(2 * which + 2 + core, which).wait_send()

    @pl.when(me > 1)
    def _():
        for kind, own, control, lent, part, early in kinds:
            loop(early, tiles, lambda o: lend_copy(own, lent, kind, early, client, o).wait_send())


def write_kernel(bred_in, growth_in, bred, growth, out_sem):
    channels = bred_in.shape[0]
    copies = [
        pltpu.make_async_copy(bred_in.at[k], bred.at[k], out_sem.at[k]) for k in range(channels)
    ]
    for copy in copies:
        copy.start()
    shape = growth_in.shape
    diagonal = lax.broadcasted_iota(jnp.int32, shape, 0) == lax.broadcasted_iota(jnp.int32, shape, 1)
    line = jnp.sum(jnp.where(diagonal, growth_in[...], 0.0), axis=0, keepdims=True)
    growth[...] = line[:, 0 : growth.shape[1]]
    for copy in copies:
        copy.wait()


def per_device(
    sizes, member_state, column_depth, rotation, diffusivity, ocean_mask, region_id, target_rms
):
    members, lons, lats = sizes
    _, channels, rows, columns = member_state.shape
    regions = target_rms.shape[0]
    fields = channels + 3 + LEV
    tall = rows + 2 * TILE
    tiles = rows // TILE
    slots = columns // LANES
    group = lons * lats
    groups = -(-fields * 2 * MARGIN // LANES)
    clients = max(members // 2 - 1, 1)
    late_mids = max(tiles - MIDS_EARLY, 1)
    late_rims = max(tiles - RIMS_EARLY, 1)
    late = max(late_mids, late_rims)
    f32 = jnp.float32
    anywhere = pl.BlockSpec(memory_space=pl.ANY)
    resident = pl.BlockSpec(memory_space=pltpu.VMEM)
    piece_mid = (channels, slots - 2, TILE, LANES)
    piece_rim = (channels, 2, TILE, LANES)
    bred, growth_wide = pl.pallas_call(
        functools.partial(cycle_kernel, sizes),
        out_shape=(
            pltpu.VMEM((channels, rows, columns), f32),
            pltpu.VMEM((regions, LANES), f32),
        ),
        in_specs=[anywhere] * 6 + [pl.BlockSpec(memory_space=pltpu.SMEM)],
        out_specs=(resident,) * 2,
        scratch_shapes=[
            pltpu.VMEM((fields, slots + 1, tall, LANES), f32),
            pltpu.VMEM((channels, slots + 1, tall, LANES), f32),
            pltpu.VMEM((slots + 1, tall, LANES), f32),
            pltpu.VMEM((slots + 1, tall, LANES), f32),
            pltpu.VMEM((tiles,) + piece_mid, f32),
            pltpu.VMEM((tiles,) + piece_rim, f32),
            pltpu.VMEM((tiles,) + piece_mid, f32),
            pltpu.VMEM((tiles,) + piece_rim, f32),
            pltpu.VMEM((clients, late_mids) + piece_mid, f32),
            pltpu.VMEM((clients, late_rims) + piece_rim, f32),
            pltpu.VMEM((groups, rows, LANES), f32),
            pltpu.VMEM((groups, tall, LANES), f32),
            pltpu.VMEM((groups, tall, LANES), f32),
            pltpu.VMEM((fields // 2, slots, TILE, LANES), f32),
            pltpu.VMEM((fields // 2, slots, TILE, LANES), f32),
            pltpu.VMEM((fields // 2, slots, TILE, LANES), f32),
            pltpu.VMEM((fields // 2, slots, TILE, LANES), f32),
            pltpu.VMEM((rows, columns), jnp.int32),
            pltpu.VMEM((rows, columns), jnp.int32),
            pltpu.VMEM((regions, TILE, LANES), f32),
            pltpu.VMEM((regions, TILE, LANES), f32),
            pltpu.VMEM((regions, TILE, LANES), f32),
            pltpu.VMEM((2, group, regions, LANES), f32),
            pltpu.VMEM((clients, regions, LANES), f32),
            pltpu.VMEM((regions, LANES), f32),
            pltpu.VMEM((regions, TILE, LANES), f32),
            pltpu.VMEM((tiles, slots, TILE, LANES), f32),
            pltpu.SemaphoreType.DMA((3, 4 * slots + 1)),
            pltpu.SemaphoreType.DMA((8,)),
            pltpu.SemaphoreType.DMA((8,)),
            pltpu.SemaphoreType.DMA((2, tiles)),
            pltpu.SemaphoreType.DMA((2, tiles)),
            pltpu.SemaphoreType.DMA((2, tiles)),
            pltpu.SemaphoreType.DMA((2, tiles)),
            pltpu.SemaphoreType.DMA((2, clients, late)),
            pltpu.SemaphoreType.DMA((2, clients, late)),
            pltpu.SemaphoreType.DMA((clients,)),
            pltpu.SemaphoreType.DMA,
            pltpu.SemaphoreType.DMA((2, group - 1)),
            pltpu.SemaphoreType.DMA((2, group - 1)),
            pltpu.SemaphoreType.REGULAR,
        ],
        compiler_params=pltpu.CompilerParams(
            collective_id=0, has_side_effects=True, vmem_limit_bytes=KERNEL_BYTES
        ),
    )(
        member_state.reshape(channels, rows, columns),
        column_depth, rotation, diffusivity, ocean_mask, region_id, target_rms,
    )
    bred, growth = pl.pallas_call(
        write_kernel,
        out_shape=(
            jax.ShapeDtypeStruct((channels, rows, columns), f32),
            jax.ShapeDtypeStruct((1, regions), f32),
        ),
        in_specs=[resident, resident],
        out_specs=(anywhere, resident),
        scratch_shapes=[pltpu.SemaphoreType.DMA((channels,))],
        compiler_params=pltpu.CompilerParams(vmem_limit_bytes=WRITE_BYTES),
    )(bred, growth_wide)
    return (bred[None], growth)


def solution(mesh):
    sizes = (mesh.shape["member"], mesh.shape["lon"], mesh.shape["lat"])
    return jax.shard_map(
        functools.partial(per_device, sizes),
        mesh=mesh,
        in_specs=(
            P("member", None, "lat", "lon"),
            P("lat", "lon"),
            P("lat", "lon"),
            P(None, "lat", "lon"),
            P("lat", "lon"),
            P("lat", "lon"),
            P(),
        ),
        out_specs=(P("member", None, "lat", "lon"), P("member", None)),
        check_vma=False,
    )
```

```python
import functools

import jax
import jax.numpy as jnp
from jax import lax
from jax.experimental import pallas as pl
from jax.experimental.pallas import tpu as pltpu
from jax.sharding import PartitionSpec as P

LEV = 5
STEPS = 2
MARGIN = 2 * STEPS
TILE = 8
LANES = 128
FIRST_ROWS = 4
SEND_AT = 5
MIDS_EARLY = 12
RIMS_EARLY = 12
KERNEL_BYTES = 56 * 2**20
WRITE_BYTES = 16 * 2**20

divergence_gain = 0.25
pressure_gain = 0.25
buoyancy_gain = 0.1
advection_gain = 0.05
epsilon = 1e-06

MESH = pl.DeviceIdType.MESH


def cycle_kernel(
    sizes,
    state_in, depth_in, rotation_in, diffusivity_in, mask_in, region_in, target_in,
    bred, growth_out,
    field, middle, surface_one, surface_two,
    own_mid, own_rim, control_mid, control_rim, lent_mid, lent_rim,
    send_east, send_west, from_east, from_west, send_north, send_south, from_north, from_south,
    mask, region, squares, lent_squares, counts, gathered, loan_out, loan, value, factor,
    in_sem, halo_send, halo_recv, pair_send, pair_recv, next_send, next_recv,
    lend_send, lend_recv, loan_send, loan_recv, sum_send, sum_recv, go,
):
    members, lons, lats = sizes
    channels, rows, columns = state_in.shape
    regions = squares.shape[0]
    fields = field.shape[0]
    slots = columns // LANES
    halo = slots
    tiles = rows // TILE
    tall = rows + 2 * TILE
    clients = members - 2
    DEPTH, ROT, OCEAN, DIFF = channels, channels + 1, channels + 2, channels + 3
    mids = list(range(1, slots - 1))
    rims = [0, slots - 1]
    half = TILE // 2
    first_tiles = min(FIRST_ROWS, tiles)
    mids_early = min(MIDS_EARLY, tiles)
    rims_early = min(RIMS_EARLY, tiles)

    me = lax.axis_index("member")
    lon = lax.axis_index("lon")
    lat = lax.axis_index("lat")
    core = lax.rem(me, 2)
    client = me - 2

    down = 2 * lat >= lats
    has_north = lat < lats - 1
    has_south = lat > 0

    def tile_of(order):
        return jnp.where(down, tiles - 1 - order, order)

    def tall_of(order, back=False):
        return jnp.where(down ^ back, tiles + 1 - order, order)

    def at(dlat, dlon, member=None):
        return {
            "member": me if member is None else member,
            "lon": lax.rem(lon + dlon + lons, lons),
            "lat": lax.rem(lat + dlat + lats, lats),
        }

    def to_member(other):
        return {"member": other, "lon": lon, "lat": lat}

    even = core == 0
    has_pair = even & (me + 1 < members)
    has_next = even & (me + 2 < members)
    parent = jnp.where(even, me - 2, me - 1)
    lender = 1
    peers = [(a, b) for a in range(lats) for b in range(lons) if (a, b) != (0, 0)]
    peers.sort(key=lambda p: -(p[0] + min(p[1], lons - p[1]) + p[1]))

    first_rows = first_tiles * TILE
    other_rows = rows - first_rows
    first_row = pl.multiple_of(jnp.where(down, rows - first_rows, 0), TILE)
    other_row = pl.multiple_of(jnp.where(down, 0, first_rows), TILE)

    def loads(index, row, count):
        src = pl.ds(row, count)
        dst = pl.ds(pl.multiple_of(row + TILE, TILE), count)
        copies = []
        for c in range(slots):
            part = slice(c * LANES, (c + 1) * LANES)
            copies += [
                (state_in.at[:, src, part], field.at[0:channels, c, dst, :]),
                (depth_in.at[src, part], field.at[DEPTH, c, dst, :]),
                (rotation_in.at[src, part], field.at[ROT, c, dst, :]),
                (diffusivity_in.at[:, src, part], field.at[DIFF:fields, c, dst, :]),
            ]
        copies.append((mask_in.at[src, :], mask.at[src, :]))
        return [pltpu.make_async_copy(a, b, in_sem.at[index, n]) for n, (a, b) in enumerate(copies)]

    load_first = loads(0, first_row, first_rows)
    load_region = pltpu.make_async_copy(region_in, region, in_sem.at[2, 0])
    for load in load_first:
        load.start()

    barrier = pltpu.get_barrier_semaphore()

    def greet(device):
        pl.semaphore_signal(barrier, inc=1, device_id=device, device_id_type=MESH)

    @pl.when(me == 0)
    def _():
        greet(to_member(1))
        for a, b in peers:
            greet(at(a, b, 1))

    @pl.when(me > 0)
    def _():
        for a, b in peers:
            greet(at(a, b))
        greet(to_member(parent))

    @pl.when(me == 1)
    def _():
        for other in range(2, members):
            greet(to_member(other))

    @pl.when(me > 1)
    def _():
        greet(to_member(lender))

    @pl.when(me == 0)
    def _():
        pl.semaphore_wait(barrier, 2 if members > 2 else 1)

    def all_here():
        @pl.when(me == 0)
        def _():
            pl.semaphore_wait(go, 1)

        @pl.when(me > 1)
        def _():
            pl.semaphore_wait(
                barrier,
                len(peers) + 1 + has_pair.astype(jnp.int32) + has_next.astype(jnp.int32),
            )

    @pl.when(me == 1)
    def _():
        pl.semaphore_wait(barrier, 2 * len(peers) + 1 + clients)
        pl.semaphore_signal(go, inc=1, device_id=to_member(0), device_id_type=MESH)

    lane = lax.broadcasted_iota(jnp.int32, (TILE, LANES), 1)
    zero_tile = jnp.zeros((TILE, LANES), jnp.float32)
    low_lanes = lane < LANES // 2
    easterly = lax.rem(lane, 2 * MARGIN) >= MARGIN

    for load in load_first:
        load.wait()
    load_other = loads(1, other_row, other_rows) if other_rows else []
    for load in load_other + [load_region]:
        load.start()

    def make_ocean(t, carry):
        r = pl.multiple_of(t * TILE, TILE)
        for c in range(slots):
            field[OCEAN, c, pl.ds(pl.multiple_of(r + TILE, TILE), TILE), :] = mask[
                pl.ds(r, TILE), c * LANES : (c + 1) * LANES
            ].astype(jnp.float32)
        return carry

    lax.fori_loop(first_row // TILE, first_row // TILE + first_tiles, make_ocean, 0)

    def remote(src, dst, index, device):
        return pltpu.make_async_remote_copy(
            src_ref=src, dst_ref=dst, send_sem=halo_send.at[index], recv_sem=halo_recv.at[index],
            device_id=device, device_id_type=MESH,
        )

    whole = slice(TILE, TILE + rows)
    last = slice(rows - TILE, rows)
    first = slice(0, TILE)
    above = slice(rows + TILE, rows + 2 * TILE)
    north = [
        remote(send_north, from_south, 0, at(1, 0)),
        remote(send_east.at[last], from_west.at[first], 4, at(1, 1)),
        remote(send_west.at[last], from_east.at[first], 5, at(1, -1)),
    ]
    south = [
        remote(send_south, from_north, 1, at(-1, 0)),
        remote(send_east.at[first], from_west.at[above], 6, at(-1, 1)),
        remote(send_west.at[first], from_east.at[above], 7, at(-1, -1)),
    ]
    sideways = [
        remote(send_east, from_west.at[whole], 2, at(0, 1)),
        remote(send_west, from_east.at[whole], 3, at(0, -1)),
    ]

    def pack_tile(t, carry):
        r = pl.multiple_of(t * TILE, TILE)
        now = pl.ds(pl.multiple_of(r + TILE, TILE), TILE)
        packed = [zero_tile] * 2
        for f in range(fields):
            g, s = divmod(f * 2 * MARGIN, LANES)
            edges = jnp.where(low_lanes, field[f, 0, now, :], field[f, slots - 1, now, :])
            here = (lane >= s) & (lane < s + 2 * MARGIN)
            packed[g] = jnp.where(here, pltpu.roll(edges, s + MARGIN, 1), packed[g])
        near, far = packed
        send_east[pl.ds(r, TILE), :] = jnp.where(easterly, pltpu.roll(far, MARGIN, 1), near)
        send_west[pl.ds(r, TILE), :] = jnp.where(easterly, near, pltpu.roll(far, LANES - MARGIN, 1))
        return carry

    def pack_halos():
        for load in load_other + [load_region]:
            load.wait()
        if other_rows:
            lax.fori_loop(other_row // TILE, other_row // TILE + other_rows // TILE, make_ocean, 0)
        for k in range(fields // 2):
            for c in range(slots):
                send_north[k, c, 0:half, :] = field[2 * k, c, rows + half : rows + TILE, :]
                send_north[k, c, half:TILE, :] = field[2 * k + 1, c, rows + half : rows + TILE, :]
                send_south[k, c, 0:half, :] = field[2 * k, c, TILE : TILE + half, :]
                send_south[k, c, half:TILE, :] = field[2 * k + 1, c, TILE : TILE + half, :]
        lax.fori_loop(0, tiles, pack_tile, 0)

    def send_halos():
        all_here()

        @pl.when(has_north)
        def _():
            for copy in north:
                copy.start()

        @pl.when(has_south)
        def _():
            for copy in south:
                copy.start()

        for copy in sideways:
            copy.start()

    def south_rows():
        @pl.when(has_south)
        def _():
            north[0].wait_recv()

        @pl.when(jnp.logical_not(has_south))
        def _():
            from_south[...] = jnp.zeros_like(from_south)

        for k in range(fields // 2):
            for c in range(slots):
                field[2 * k, c, half:TILE, :] = from_south[k, c, 0:half, :]
                field[2 * k + 1, c, half:TILE, :] = from_south[k, c, half:TILE, :]
                field[2 * k, c, 0:half, :] = from_south[k, c, 0:half, :]
                field[2 * k + 1, c, 0:half, :] = from_south[k, c, half:TILE, :]

    def north_rows():
        @pl.when(has_north)
        def _():
            south[0].wait_recv()

        @pl.when(jnp.logical_not(has_north))
        def _():
            from_north[...] = jnp.zeros_like(from_north)

        base = rows + TILE
        for k in range(fields // 2):
            for c in range(slots):
                field[2 * k, c, base : base + half, :] = from_north[k, c, 0:half, :]
                field[2 * k + 1, c, base : base + half, :] = from_north[k, c, half:TILE, :]
                field[2 * k, c, base + half : base + TILE, :] = from_north[k, c, 0:half, :]
                field[2 * k + 1, c, base + half : base + TILE, :] = from_north[k, c, half:TILE, :]

    def join_middle(order, back=False):
        now = pl.ds(pl.multiple_of(tall_of(order) * TILE, TILE), TILE)
        for f in range(fields):
            field[f, halo, now, :] = jnp.where(low_lanes, field[f, slots - 1, now, :], field[f, 0, now, :])

    def join_halo(order, back):
        now = pl.ds(pl.multiple_of(tall_of(order, back) * TILE, TILE), TILE)
        east, west = from_east[now, :], from_west[now, :]
        both = [
            jnp.where(easterly, east, west),
            jnp.where(easterly, pltpu.roll(east, MARGIN, 1), pltpu.roll(west, LANES - MARGIN, 1)),
        ]
        for f in range(fields):
            g, s = divmod(f * 2 * MARGIN, LANES)
            field[f, halo, now, :] = pltpu.roll(both[g], LANES - s - MARGIN, 1)

    class Ring:
        def __init__(self, ring, todo):
            self.todo = todo
            size = len(ring)
            place = {c: i for i, c in enumerate(ring)}
            self.east = {c: ring[(place[c] + 1) % size] for c in todo}
            self.west = {c: ring[(place[c] - 1) % size] for c in todo}
            self.used = sorted(set(todo) | set(self.east.values()) | set(self.west.values()))

        def sides(self, q):
            to_east = {c: pltpu.roll(q[c], LANES - 1, 1) for c in {*self.todo, *self.east.values()}}
            to_west = {c: pltpu.roll(q[c], 1, 1) for c in {*self.todo, *self.west.values()}}
            e = {c: jnp.where(lane == LANES - 1, to_east[self.east[c]], to_east[c]) for c in self.todo}
            w = {c: jnp.where(lane == 0, to_west[self.west[c]], to_west[c]) for c in self.todo}
            return e, w

    def surface_rows(src, dst, ring, r):
        now, above_r, below_r = pl.ds(r, TILE), pl.ds(r + 1, TILE), pl.ds(r - 1, TILE)

        def add_up(base, c, where):
            total = src[base, c, where, :]
            for k in range(1, LEV):
                total = total + src[base + k, c, where, :]
            return total

        e, w = ring.sides({c: add_up(1, c, now) for c in ring.used})
        for c in ring.todo:
            n, s = add_up(1 + LEV, c, above_r), add_up(1 + LEV, c, below_r)
            divergence = (e[c] - w[c]) + (n - s)
            dst[c, now, :] = field[OCEAN, c, now, :] * (
                src[0, c, now, :] - (divergence_gain / LEV) * field[DEPTH, c, now, :] * divergence
            )

    def update_rows(src, surface, ring, r, write):
        now, above_r, below_r = pl.ds(r, TILE), pl.ds(r + 1, TILE), pl.ds(r - 1, TILE)
        h = {c: surface[c, now, :] for c in ring.used}
        e, w = ring.sides(h)
        slope_east, slope_north = {}, {}
        for c in ring.todo:
            slope_east[c] = pressure_gain * (e[c] - w[c])
            slope_north[c] = pressure_gain * (surface[c, above_r, :] - surface[c, below_r, :])
            write(0, c, h[c])
        for k in range(LEV):
            iu, iv, ic = 1 + k, 1 + LEV + k, 1 + 2 * LEV + k
            u = {c: src[iu, c, now, :] for c in ring.used}
            v = {c: src[iv, c, now, :] for c in ring.used}
            t = {c: src[ic, c, now, :] for c in ring.used}
            ue, uw = ring.sides(u)
            ve, vw = ring.sides(v)
            te, tw = ring.sides(t)
            for c in ring.todo:
                ocean = field[OCEAN, c, now, :]
                rotation = field[ROT, c, now, :]
                mixing = field[DIFF + k, c, now, :]
                tn, ts = src[ic, c, above_r, :], src[ic, c, below_r, :]
                heat_east, heat_north = te[c] - tw[c], tn - ts
                around_u = (ue[c] + uw[c]) + (src[iu, c, above_r, :] + src[iu, c, below_r, :])
                around_v = (ve[c] + vw[c]) + (src[iv, c, above_r, :] + src[iv, c, below_r, :])
                around_t = (te[c] + tw[c]) + (tn + ts)
                new_u = ocean * (
                    u[c] + rotation * v[c] - slope_east[c] - buoyancy_gain * heat_east
                    + mixing * (around_u - 4.0 * u[c])
                )
                new_v = ocean * (
                    v[c] - rotation * u[c] - slope_north[c] - buoyancy_gain * heat_north
                    + mixing * (around_v - 4.0 * v[c])
                )
                new_t = ocean * (
                    t[c] + mixing * (around_t - 4.0 * t[c])
                    - advection_gain * (new_u * heat_east + new_v * heat_north)
                )
                write(iu, c, new_u)
                write(iv, c, new_v)
                write(ic, c, new_t)

    def run_pass(join, one, two, own, own_slots, at_order, leave, back=False):
        step = jnp.where(down ^ back, -1, 1)

        def body(i, carry):
            j = i - 1
            at_order(j)
            join(j + 2, back)
            r = jnp.where(down ^ back, rows - TILE * j, TILE + TILE * j)
            surface_rows(field, surface_one, one, r + 3 * step)
            r_one = r + 2 * step

            def middle_write(channel, c, new):
                middle[channel, c, pl.ds(r_one, TILE), :] = new

            update_rows(field, surface_one, one, r_one, middle_write)
            surface_rows(middle, surface_two, one, r + step)

            @pl.when(j >= 0)
            def _():
                order = jnp.where(back, tiles - 1 - j, j)
                t = tile_of(order)

                def last_write(channel, c, new):
                    own[t, channel, own_slots[c]] = new

                update_rows(
                    middle, surface_two, two, pl.multiple_of(r, TILE), last_write
                )
                leave(order, t)

            return carry

        lax.fori_loop(0, tiles + 1, body, 0)

    def pair_copy(ref, kind, t):
        return pltpu.make_async_remote_copy(
            src_ref=ref.at[t], dst_ref=ref.at[t],
            send_sem=pair_send.at[kind, t], recv_sem=pair_recv.at[kind, t],
            device_id=to_member(me + 1), device_id_type=MESH,
        )

    def next_copy(ref, kind, t):
        return pltpu.make_async_remote_copy(
            src_ref=ref.at[t], dst_ref=ref.at[t],
            send_sem=next_send.at[kind, t], recv_sem=next_recv.at[kind, t],
            device_id=to_member(me + 2), device_id_type=MESH,
        )

    def lend_copy(own, lent, kind, early, which, order):
        return pltpu.make_async_remote_copy(
            src_ref=own.at[tile_of(order)], dst_ref=lent.at[which, order - early],
            send_sem=lend_send.at[kind, which, order - early],
            recv_sem=lend_recv.at[kind, which, order - early],
            device_id=to_member(lender), device_id_type=MESH,
        )

    def leave_mid(order, t):
        @pl.when(me == 0)
        def _():
            for k in range(channels):
                for n in range(len(mids)):
                    control_mid[t, k, n] = own_mid[t, k, n]
            pair_copy(control_mid, 0, t).start()

            @pl.when(has_next & (order < mids_early))
            def _():
                next_copy(control_mid, 0, t).start()

        @pl.when((me > 1) & (order >= mids_early))
        def _():
            lend_copy(own_mid, lent_mid, 0, mids_early, client, order).start()

    def leave_rim(order, t):
        @pl.when(me == 0)
        def _():
            for k in range(channels):
                for n in range(len(rims)):
                    control_rim[t, k, n] = own_rim[t, k, n]
            pair_copy(control_rim, 1, t).start()

            @pl.when(has_next)
            def _():
                next_copy(control_rim, 1, t).start()

        @pl.when((me > 1) & (order >= rims_early))
        def _():
            lend_copy(own_rim, lent_rim, 1, rims_early, client, order).start()

    def start_rows():
        @pl.when(down)
        def _():
            north_rows()

        @pl.when(jnp.logical_not(down))
        def _():
            south_rows()

    def end_rows():
        @pl.when(down)
        def _():
            south_rows()

        @pl.when(jnp.logical_not(down))
        def _():
            north_rows()

    load_at = min(first_tiles - 1, tiles - 1)
    send_at = max(load_at, min(SEND_AT, tiles - 2))

    def events_mid(j):
        if lats <= 2:
            @pl.when(j == load_at)
            def _():
                pack_halos()

            @pl.when(j == send_at)
            def _():
                send_halos()

        @pl.when(j == tiles - 1)
        def _():
            end_rows()

    if lats > 2:
        pack_halos()
        send_halos()
    start_rows()
    join_middle(0)
    ring_mid = mids + [halo]
    run_pass(
        join_middle, Ring(ring_mid, ring_mid), Ring(ring_mid, mids),
        own_mid, {c: n for n, c in enumerate(mids)}, events_mid, leave_mid,
    )

    for copy in sideways:
        copy.wait_recv()

    @pl.when(has_north)
    def _():
        for copy in south[1:]:
            copy.wait_recv()

    @pl.when(has_south)
    def _():
        for copy in north[1:]:
            copy.wait_recv()

    @pl.when(jnp.logical_not(has_north))
    def _():
        from_east[above, :] = zero_tile
        from_west[above, :] = zero_tile

    @pl.when(jnp.logical_not(has_south))
    def _():
        from_east[first, :] = zero_tile
        from_west[first, :] = zero_tile

    back = me > 1
    join_halo(0, back)
    ring_all = list(range(slots)) + [halo]
    run_pass(
        join_halo, Ring(ring_all, [slots - 1, halo, 0]), Ring(ring_all, rims),
        own_rim, {c: n for n, c in enumerate(rims)}, lambda j: None, leave_rim, back,
    )

    @pl.when((me == 0) & has_next)
    def _():
        def body(order, carry):
            next_copy(control_mid, 0, tile_of(order)).start()
            return carry

        lax.fori_loop(mids_early, tiles, body, 0)

    def clear(ref):
        for k in range(regions):
            ref[k] = zero_tile

    def ids_at(t, c):
        return region[pl.ds(pl.multiple_of(t * TILE, TILE), TILE), c * LANES : (c + 1) * LANES]

    def ocean_at(t, c):
        return field[OCEAN, c, pl.ds(pl.multiple_of(t * TILE + TILE, TILE), TILE), :]

    def add_regions(ref, items):
        for k in range(regions):
            total = ref[k]
            for ids, amount in items:
                total = total + jnp.where(ids == k, amount, 0.0)
            ref[k] = total

    def compare(ref, mine, its, t, part):
        items = []
        for n, c in enumerate(part):
            total = None
            for k in range(channels):
                d = mine(k, n) - its(k, n)
                total = d * d if total is None else total + d * d
            items.append((ids_at(t, c), ocean_at(t, c) * total))
        add_regions(ref, items)

    def share(which):
        for p, (a, b) in enumerate(peers):
            pltpu.make_async_remote_copy(
                src_ref=gathered.at[which, 0], dst_ref=gathered.at[which, p + 1],
                send_sem=sum_send.at[which, p], recv_sem=sum_recv.at[which, p],
                device_id=at(a, b), device_id_type=MESH,
            ).start()

    def collect(which):
        for p, (a, b) in enumerate(peers):
            pltpu.make_async_remote_copy(
                src_ref=gathered.at[which, 0], dst_ref=gathered.at[which, p + 1],
                send_sem=sum_send.at[which, p], recv_sem=sum_recv.at[which, p],
                device_id=at(a, b), device_id_type=MESH,
            ).wait()
        total = gathered[which, 0]
        for p in range(len(peers)):
            total = total + gathered[which, p + 1]
        return jnp.sum(total, axis=1, keepdims=True)

    clear(squares)
    clear(counts)

    def count(t, carry):
        add_regions(counts, [(ids_at(t, c), ocean_at(t, c)) for c in range(slots)])
        return carry

    lax.fori_loop(0, tiles, count, 0)
    gathered[0, 0] = jnp.sum(counts[...], axis=1)
    share(0)

    kinds = [
        (0, own_mid, control_mid, lent_mid, mids, mids_early),
        (1, own_rim, control_rim, lent_rim, rims, rims_early),
    ]

    def take(kind, order):
        _, own, control, _, part, _ = kinds[kind]
        t = tile_of(order)

        @pl.when(even)
        def _():
            next_copy(control, kind, t).wait_recv()

            @pl.when(has_pair)
            def _():
                pair_copy(control, kind, t).start()

            @pl.when(has_next)
            def _():
                next_copy(control, kind, t).start()

        @pl.when(jnp.logical_not(even))
        def _():
            pair_copy(control, kind, t).wait_recv()

    def weigh(kind, order):
        _, own, control, _, part, _ = kinds[kind]
        t = tile_of(order)
        compare(squares, lambda k, n: own[t, k, n], lambda k, n: control[t, k, n], t, part)

    def loop(begin, end, *actions):
        def body(order, carry):
            for action in actions:
                action(order)
            return carry

        lax.fori_loop(begin, end, body, 0)

    @pl.when(me > 0)
    def _():
        late_mids = jnp.where(me == 1, tiles, mids_early)
        late_rims = jnp.where(me == 1, tiles, rims_early)
        loop(0, mids_early, lambda o: take(0, o), lambda o: weigh(0, o))
        loop(0, late_rims, lambda o: take(1, o), lambda o: weigh(1, o))
        loop(mids_early, late_mids, lambda o: take(0, o), lambda o: weigh(0, o))

    def loan_copy(other, which):
        return pltpu.make_async_remote_copy(
            src_ref=loan_out.at[which], dst_ref=loan,
            send_sem=loan_send.at[which], recv_sem=loan_recv,
            device_id=to_member(other), device_id_type=MESH,
        )

    def lend(which, other):
        clear(lent_squares)
        for kind, own, control, lent, part, early in kinds:
            def body(order, carry):
                lend_copy(own, lent, kind, early, which, order).wait_recv()
                t = tile_of(order)
                compare(
                    lent_squares,
                    lambda k, n: lent[which, order - early, k, n],
                    lambda k, n: control[t, k, n], t, part,
                )
                return carry

            lax.fori_loop(early, tiles, body, 0)
        loan_out[which] = jnp.sum(lent_squares[...], axis=1)
        loan_copy(other, which).start()

    gathered[1, 0] = jnp.sum(squares[...], axis=1)

    @pl.when(me == 1)
    def _():
        for which in range(clients):
            lend(which, which + 2)

    @pl.when(me > 1)
    def _():
        loan_copy(me, 0).wait_recv()
        gathered[1, 0] = gathered[1, 0] + loan[...]

    share(1)
    count_sum = collect(0)
    square_sum = collect(1)
    growth = jnp.sqrt(square_sum / (count_sum * channels) + epsilon)
    growth_wide = jnp.broadcast_to(growth, (regions, LANES))
    growth_out[...] = growth_wide
    for k in range(regions):
        value[k] = jnp.broadcast_to(target_in[k] / growth_wide[k : k + 1, :], (TILE, LANES))

    def make_factor(t, carry):
        for c in range(slots):
            ids = ids_at(t, c)
            total = zero_tile
            for k in range(regions):
                total = jnp.where(ids == k, value[k], total)
            factor[t, c] = total
        return carry

    lax.fori_loop(0, tiles, make_factor, 0)

    def breed(kind, order):
        _, own, control, _, part, _ = kinds[kind]
        t = tile_of(order)
        now = pl.ds(pl.multiple_of(t * TILE, TILE), TILE)
        for n, c in enumerate(part):
            scale = factor[t, c]
            for k in range(channels):
                base = control[t, k, n]
                bred[k, now, c * LANES : (c + 1) * LANES] = base + scale * (own[t, k, n] - base)

    def take_late(kind, order):
        @pl.when(me > 1)
        def _():
            take(kind, order)

    loop(0, mids_early, lambda o: breed(0, o))
    loop(0, rims_early, lambda o: breed(1, o))
    loop(rims_early, tiles, lambda o: take_late(1, o), lambda o: breed(1, o))
    loop(mids_early, tiles, lambda o: take_late(0, o), lambda o: breed(0, o))

    for copy in sideways:
        copy.wait_send()

    @pl.when(has_north)
    def _():
        for copy in north:
            copy.wait_send()

    @pl.when(has_south)
    def _():
        for copy in south:
            copy.wait_send()

    def finish(t, carry):
        for kind, own, control, lent, part, early in kinds:
            @pl.when(has_pair)
            def _():
                pair_copy(control, kind, t).wait_send()

            @pl.when(has_next)
            def _():
                next_copy(control, kind, t).wait_send()

        return carry

    lax.fori_loop(0, tiles, finish, 0)

    @pl.when(me == 1)
    def _():
        for which in range(clients):
            loan_copy(which + 2, which).wait_send()

    @pl.when(me > 1)
    def _():
        for kind, own, control, lent, part, early in kinds:
            loop(early, tiles, lambda o: lend_copy(own, lent, kind, early, client, o).wait_send())


def write_kernel(bred_in, growth_in, bred, growth, out_sem):
    channels = bred_in.shape[0]
    copies = [
        pltpu.make_async_copy(bred_in.at[k], bred.at[k], out_sem.at[k]) for k in range(channels)
    ]
    for copy in copies:
        copy.start()
    shape = growth_in.shape
    diagonal = lax.broadcasted_iota(jnp.int32, shape, 0) == lax.broadcasted_iota(jnp.int32, shape, 1)
    line = jnp.sum(jnp.where(diagonal, growth_in[...], 0.0), axis=0, keepdims=True)
    growth[...] = line[:, 0 : growth.shape[1]]
    for copy in copies:
        copy.wait()


def per_device(
    sizes, member_state, column_depth, rotation, diffusivity, ocean_mask, region_id, target_rms
):
    members, lons, lats = sizes
    _, channels, rows, columns = member_state.shape
    regions = target_rms.shape[0]
    fields = channels + 3 + LEV
    tall = rows + 2 * TILE
    tiles = rows // TILE
    slots = columns // LANES
    group = lons * lats
    clients = max(members - 2, 1)
    late_mids = max(tiles - MIDS_EARLY, 1)
    late_rims = max(tiles - RIMS_EARLY, 1)
    late = max(late_mids, late_rims)
    f32 = jnp.float32
    anywhere = pl.BlockSpec(memory_space=pl.ANY)
    resident = pl.BlockSpec(memory_space=pltpu.VMEM)
    piece_mid = (channels, slots - 2, TILE, LANES)
    piece_rim = (channels, 2, TILE, LANES)
    bred, growth_wide = pl.pallas_call(
        functools.partial(cycle_kernel, sizes),
        out_shape=(
            pltpu.VMEM((channels, rows, columns), f32),
            pltpu.VMEM((regions, LANES), f32),
        ),
        in_specs=[anywhere] * 6 + [pl.BlockSpec(memory_space=pltpu.SMEM)],
        out_specs=(resident,) * 2,
        scratch_shapes=[
            pltpu.VMEM((fields, slots + 1, tall, LANES), f32),
            pltpu.VMEM((channels, slots + 1, tall, LANES), f32),
            pltpu.VMEM((slots + 1, tall, LANES), f32),
            pltpu.VMEM((slots + 1, tall, LANES), f32),
            pltpu.VMEM((tiles,) + piece_mid, f32),
            pltpu.VMEM((tiles,) + piece_rim, f32),
            pltpu.VMEM((tiles,) + piece_mid, f32),
            pltpu.VMEM((tiles,) + piece_rim, f32),
            pltpu.VMEM((clients, late_mids) + piece_mid, f32),
            pltpu.VMEM((clients, late_rims) + piece_rim, f32),
            pltpu.VMEM((rows, LANES), f32),
            pltpu.VMEM((rows, LANES), f32),
            pltpu.VMEM((tall, LANES), f32),
            pltpu.VMEM((tall, LANES), f32),
            pltpu.VMEM((fields // 2, slots, TILE, LANES), f32),
            pltpu.VMEM((fields // 2, slots, TILE, LANES), f32),
            pltpu.VMEM((fields // 2, slots, TILE, LANES), f32),
            pltpu.VMEM((fields // 2, slots, TILE, LANES), f32),
            pltpu.VMEM((rows, columns), jnp.int32),
            pltpu.VMEM((rows, columns), jnp.int32),
            pltpu.VMEM((regions, TILE, LANES), f32),
            pltpu.VMEM((regions, TILE, LANES), f32),
            pltpu.VMEM((regions, TILE, LANES), f32),
            pltpu.VMEM((2, group, regions, LANES), f32),
            pltpu.VMEM((clients, regions, LANES), f32),
            pltpu.VMEM((regions, LANES), f32),
            pltpu.VMEM((regions, TILE, LANES), f32),
            pltpu.VMEM((tiles, slots, TILE, LANES), f32),
            pltpu.SemaphoreType.DMA((3, 4 * slots + 1)),
            pltpu.SemaphoreType.DMA((8,)),
            pltpu.SemaphoreType.DMA((8,)),
            pltpu.SemaphoreType.DMA((2, tiles)),
            pltpu.SemaphoreType.DMA((2, tiles)),
            pltpu.SemaphoreType.DMA((2, tiles)),
            pltpu.SemaphoreType.DMA((2, tiles)),
            pltpu.SemaphoreType.DMA((2, clients, late)),
            pltpu.SemaphoreType.DMA((2, clients, late)),
            pltpu.SemaphoreType.DMA((clients,)),
            pltpu.SemaphoreType.DMA,
            pltpu.SemaphoreType.DMA((2, group - 1)),
            pltpu.SemaphoreType.DMA((2, group - 1)),
            pltpu.SemaphoreType.REGULAR,
        ],
        compiler_params=pltpu.CompilerParams(
            collective_id=0, has_side_effects=True, vmem_limit_bytes=KERNEL_BYTES
        ),
    )(
        member_state.reshape(channels, rows, columns),
        column_depth, rotation, diffusivity, ocean_mask, region_id, target_rms,
    )
    bred, growth = pl.pallas_call(
        write_kernel,
        out_shape=(
            jax.ShapeDtypeStruct((channels, rows, columns), f32),
            jax.ShapeDtypeStruct((1, regions), f32),
        ),
        in_specs=[resident, resident],
        out_specs=(anywhere, resident),
        scratch_shapes=[pltpu.SemaphoreType.DMA((channels,))],
        compiler_params=pltpu.CompilerParams(vmem_limit_bytes=WRITE_BYTES),
    )(bred, growth_wide)
    return (bred[None], growth)


def solution(mesh):
    sizes = (mesh.shape["member"], mesh.shape["lon"], mesh.shape["lat"])
    return jax.shard_map(
        functools.partial(per_device, sizes),
        mesh=mesh,
        in_specs=(
            P("member", None, "lat", "lon"),
            P("lat", "lon"),
            P("lat", "lon"),
            P(None, "lat", "lon"),
            P("lat", "lon"),
            P("lat", "lon"),
            P(),
        ),
        out_specs=(P("member", None, "lat", "lon"), P("member", None)),
        check_vma=False,
    )
```

```python
import functools

import jax
import jax.numpy as jnp
from jax import lax
from jax.experimental import pallas as pl
from jax.experimental.pallas import tpu as pltpu
from jax.sharding import PartitionSpec as P

LEV = 5
STEPS = 2
MARGIN = 2 * STEPS
TILE = 8
LANES = 128
FIRST_ROWS = 4
PACK_STEPS = 2
MIDS_EARLY = 15
RIMS_EARLY = 11
KERNEL_BYTES = 56 * 2**20
WRITE_BYTES = 16 * 2**20

divergence_gain = 0.25
pressure_gain = 0.25
buoyancy_gain = 0.1
advection_gain = 0.05
epsilon = 1e-06

MESH = pl.DeviceIdType.MESH


def cycle_kernel(
    sizes,
    state_in, depth_in, rotation_in, diffusivity_in, mask_in, region_in, target_in,
    bred, growth_out,
    field, middle, surface_one, surface_two,
    own_mid, own_rim, control_mid, control_rim, lent_mid, lent_rim,
    send_east, send_west, from_east, from_west, send_north, send_south, from_north, from_south,
    mask, region, squares, lent_squares, counts, gathered, loan_out, loan, value, factor, target,
    in_sem, halo_send, halo_recv, pair_send, next_send, take_recv,
    lend_send, lend_recv, loan_send, loan_recv, sum_send, sum_recv, go,
):
    members, lons, lats = sizes
    channels, rows, columns = state_in.shape
    regions = squares.shape[0]
    fields = field.shape[0]
    slots = columns // LANES
    halo = slots
    tiles = rows // TILE
    tall = rows + 2 * TILE
    clients = members - 2
    DEPTH, ROT, OCEAN, DIFF = channels, channels + 1, channels + 2, channels + 3
    mids = list(range(1, slots - 1))
    rims = [0, slots - 1]
    half = TILE // 2
    first_tiles = min(FIRST_ROWS, tiles)
    mids_early = min(MIDS_EARLY, tiles)
    rims_early = min(RIMS_EARLY, tiles)

    me = lax.axis_index("member")
    lon = lax.axis_index("lon")
    lat = lax.axis_index("lat")
    core = lax.rem(me, 2)
    client = me - 2

    down = 2 * lat >= lats
    has_north = lat < lats - 1
    has_south = lat > 0

    def tile_of(order):
        return jnp.where(down, tiles - 1 - order, order)

    def tall_of(order, back=False):
        return jnp.where(down ^ back, tiles + 1 - order, order)

    def at(dlat, dlon, member=None):
        return {
            "member": me if member is None else member,
            "lon": lax.rem(lon + dlon + lons, lons),
            "lat": lax.rem(lat + dlat + lats, lats),
        }

    def to_member(other):
        return {"member": other, "lon": lon, "lat": lat}

    even = core == 0
    has_pair = even & (me + 1 < members)
    has_next = even & (me + 2 < members)
    parent = jnp.where(even, me - 2, me - 1)
    lender = 1
    peers = [(a, b) for a in range(lats) for b in range(lons) if (a, b) != (0, 0)]
    peers.sort(key=lambda p: -(p[0] + min(p[1], lons - p[1]) + p[1]))

    first_rows = first_tiles * TILE
    other_rows = rows - first_rows
    first_row = pl.multiple_of(jnp.where(down, rows - first_rows, 0), TILE)
    other_row = pl.multiple_of(jnp.where(down, 0, first_rows), TILE)

    def loads(index, row, count):
        src = pl.ds(row, count)
        dst = pl.ds(pl.multiple_of(row + TILE, TILE), count)
        copies = []
        for c in range(slots):
            part = slice(c * LANES, (c + 1) * LANES)
            copies += [
                (state_in.at[:, src, part], field.at[0:channels, c, dst, :]),
                (depth_in.at[src, part], field.at[DEPTH, c, dst, :]),
                (rotation_in.at[src, part], field.at[ROT, c, dst, :]),
                (diffusivity_in.at[:, src, part], field.at[DIFF:fields, c, dst, :]),
            ]
        copies.append((mask_in.at[src, :], mask.at[src, :]))
        return [pltpu.make_async_copy(a, b, in_sem.at[index]) for a, b in copies]

    def loaded(index, row, count):
        part = field.at[:, 0:slots, pl.ds(pl.multiple_of(row + TILE, TILE), count), :]
        pltpu.make_async_copy(part, part, in_sem.at[index]).wait()

    load_first = loads(0, first_row, first_rows)
    load_region = pltpu.make_async_copy(region_in, region, in_sem.at[2])
    load_target = pltpu.make_async_copy(target_in, target, in_sem.at[3])
    for load in load_first:
        load.start()

    barrier = pltpu.get_barrier_semaphore()

    def greet(device):
        pl.semaphore_signal(barrier, inc=1, device_id=device, device_id_type=MESH)

    @pl.when(me == 0)
    def _():
        greet(to_member(1))
        for a, b in peers:
            greet(at(a, b, 1))

    @pl.when(me > 0)
    def _():
        for a, b in peers:
            greet(at(a, b))
        greet(to_member(parent))

    @pl.when(me == 1)
    def _():
        for other in range(2, members):
            greet(to_member(other))

    @pl.when(me > 1)
    def _():
        greet(to_member(lender))

    @pl.when(me == 0)
    def _():
        pl.semaphore_wait(barrier, 2 if members > 2 else 1)

    def all_here():
        @pl.when(me == 0)
        def _():
            pl.semaphore_wait(go, 1)

        @pl.when(me > 1)
        def _():
            pl.semaphore_wait(
                barrier,
                len(peers) + 1 + has_pair.astype(jnp.int32) + has_next.astype(jnp.int32),
            )

    @pl.when(me == 1)
    def _():
        pl.semaphore_wait(barrier, 2 * len(peers) + 1 + clients)
        pl.semaphore_signal(go, inc=1, device_id=to_member(0), device_id_type=MESH)

    lane = lax.broadcasted_iota(jnp.int32, (TILE, LANES), 1)
    zero_tile = jnp.zeros((TILE, LANES), jnp.float32)
    low_lanes = lane < LANES // 2
    easterly = lax.rem(lane, 2 * MARGIN) >= MARGIN

    loaded(0, first_row, first_rows)
    load_other = loads(1, other_row, other_rows) if other_rows else []
    for load in load_other + [load_region, load_target]:
        load.start()

    def make_ocean(t, carry):
        r = pl.multiple_of(t * TILE, TILE)
        for c in range(slots):
            field[OCEAN, c, pl.ds(pl.multiple_of(r + TILE, TILE), TILE), :] = mask[
                pl.ds(r, TILE), c * LANES : (c + 1) * LANES
            ].astype(jnp.float32)
        return carry

    lax.fori_loop(first_row // TILE, first_row // TILE + first_tiles, make_ocean, 0)

    def remote(src, dst, index, device):
        return pltpu.make_async_remote_copy(
            src_ref=src, dst_ref=dst, send_sem=halo_send.at[index], recv_sem=halo_recv.at[index],
            device_id=device, device_id_type=MESH,
        )

    whole = slice(TILE, TILE + rows)
    last = slice(rows - TILE, rows)
    first = slice(0, TILE)
    above = slice(rows + TILE, rows + 2 * TILE)
    north = [
        remote(send_north, from_south, 0, at(1, 0)),
        remote(send_east.at[last], from_west.at[first], 4, at(1, 1)),
        remote(send_west.at[last], from_east.at[first], 5, at(1, -1)),
    ]
    south = [
        remote(send_south, from_north, 1, at(-1, 0)),
        remote(send_east.at[first], from_west.at[above], 6, at(-1, 1)),
        remote(send_west.at[first], from_east.at[above], 7, at(-1, -1)),
    ]
    sideways = [
        remote(send_east, from_west.at[whole], 2, at(0, 1)),
        remote(send_west, from_east.at[whole], 3, at(0, -1)),
    ]

    def pack_tile(t, carry):
        r = pl.multiple_of(t * TILE, TILE)
        now = pl.ds(pl.multiple_of(r + TILE, TILE), TILE)
        packed = [zero_tile] * 2
        for f in range(fields):
            g, s = divmod(f * 2 * MARGIN, LANES)
            edges = jnp.where(low_lanes, field[f, 0, now, :], field[f, slots - 1, now, :])
            here = (lane >= s) & (lane < s + 2 * MARGIN)
            packed[g] = jnp.where(here, pltpu.roll(edges, s + MARGIN, 1), packed[g])
        near, far = packed
        send_east[pl.ds(r, TILE), :] = jnp.where(easterly, pltpu.roll(far, MARGIN, 1), near)
        send_west[pl.ds(r, TILE), :] = jnp.where(easterly, near, pltpu.roll(far, LANES - MARGIN, 1))
        return carry

    def finish_loads():
        if other_rows:
            loaded(1, other_row, other_rows)
            lax.fori_loop(other_row // TILE, other_row // TILE + other_rows // TILE, make_ocean, 0)

    def pack_rows():
        for k in range(fields // 2):
            for c in range(slots):
                send_north[k, c, 0:half, :] = field[2 * k, c, rows + half : rows + TILE, :]
                send_north[k, c, half:TILE, :] = field[2 * k + 1, c, rows + half : rows + TILE, :]
                send_south[k, c, 0:half, :] = field[2 * k, c, TILE : TILE + half, :]
                send_south[k, c, half:TILE, :] = field[2 * k + 1, c, TILE : TILE + half, :]

    def send_halos():
        pack_rows()
        all_here()

        @pl.when(has_north)
        def _():
            for copy in north:
                copy.start()

        @pl.when(has_south)
        def _():
            for copy in south:
                copy.start()

        for copy in sideways:
            copy.start()

    def south_rows():
        @pl.when(has_south)
        def _():
            north[0].wait_recv()

        @pl.when(jnp.logical_not(has_south))
        def _():
            from_south[...] = jnp.zeros_like(from_south)

        for k in range(fields // 2):
            for c in range(slots):
                field[2 * k, c, half:TILE, :] = from_south[k, c, 0:half, :]
                field[2 * k + 1, c, half:TILE, :] = from_south[k, c, half:TILE, :]
                field[2 * k, c, 0:half, :] = from_south[k, c, 0:half, :]
                field[2 * k + 1, c, 0:half, :] = from_south[k, c, half:TILE, :]

    def north_rows():
        @pl.when(has_north)
        def _():
            south[0].wait_recv()

        @pl.when(jnp.logical_not(has_north))
        def _():
            from_north[...] = jnp.zeros_like(from_north)

        base = rows + TILE
        for k in range(fields // 2):
            for c in range(slots):
                field[2 * k, c, base : base + half, :] = from_north[k, c, 0:half, :]
                field[2 * k + 1, c, base : base + half, :] = from_north[k, c, half:TILE, :]
                field[2 * k, c, base + half : base + TILE, :] = from_north[k, c, 0:half, :]
                field[2 * k + 1, c, base + half : base + TILE, :] = from_north[k, c, half:TILE, :]

    def join_middle(order, back=False):
        now = pl.ds(pl.multiple_of(tall_of(order) * TILE, TILE), TILE)
        for f in range(fields):
            field[f, halo, now, :] = jnp.where(low_lanes, field[f, slots - 1, now, :], field[f, 0, now, :])

    def join_halo(order, back):
        now = pl.ds(pl.multiple_of(tall_of(order, back) * TILE, TILE), TILE)
        east, west = from_east[now, :], from_west[now, :]
        both = [
            jnp.where(easterly, east, west),
            jnp.where(easterly, pltpu.roll(east, MARGIN, 1), pltpu.roll(west, LANES - MARGIN, 1)),
        ]
        for f in range(fields):
            g, s = divmod(f * 2 * MARGIN, LANES)
            field[f, halo, now, :] = pltpu.roll(both[g], LANES - s - MARGIN, 1)

    class Ring:
        def __init__(self, ring, todo):
            self.todo = todo
            size = len(ring)
            place = {c: i for i, c in enumerate(ring)}
            self.east = {c: ring[(place[c] + 1) % size] for c in todo}
            self.west = {c: ring[(place[c] - 1) % size] for c in todo}
            self.used = sorted(set(todo) | set(self.east.values()) | set(self.west.values()))

        def sides(self, q):
            to_east = {c: pltpu.roll(q[c], LANES - 1, 1) for c in {*self.todo, *self.east.values()}}
            to_west = {c: pltpu.roll(q[c], 1, 1) for c in {*self.todo, *self.west.values()}}
            e = {c: jnp.where(lane == LANES - 1, to_east[self.east[c]], to_east[c]) for c in self.todo}
            w = {c: jnp.where(lane == 0, to_west[self.west[c]], to_west[c]) for c in self.todo}
            return e, w

    def surface_rows(src, dst, ring, r):
        now, above_r, below_r = pl.ds(r, TILE), pl.ds(r + 1, TILE), pl.ds(r - 1, TILE)

        def add_up(base, c, where):
            total = src[base, c, where, :]
            for k in range(1, LEV):
                total = total + src[base + k, c, where, :]
            return total

        e, w = ring.sides({c: add_up(1, c, now) for c in ring.used})
        for c in ring.todo:
            n, s = add_up(1 + LEV, c, above_r), add_up(1 + LEV, c, below_r)
            divergence = (e[c] - w[c]) + (n - s)
            dst[c, now, :] = field[OCEAN, c, now, :] * (
                src[0, c, now, :] - (divergence_gain / LEV) * field[DEPTH, c, now, :] * divergence
            )

    def update_rows(src, surface, ring, r, write):
        now, above_r, below_r = pl.ds(r, TILE), pl.ds(r + 1, TILE), pl.ds(r - 1, TILE)
        h = {c: surface[c, now, :] for c in ring.used}
        e, w = ring.sides(h)
        slope_east, slope_north = {}, {}
        for c in ring.todo:
            slope_east[c] = pressure_gain * (e[c] - w[c])
            slope_north[c] = pressure_gain * (surface[c, above_r, :] - surface[c, below_r, :])
            write(0, c, h[c])
        for k in range(LEV):
            iu, iv, ic = 1 + k, 1 + LEV + k, 1 + 2 * LEV + k
            u = {c: src[iu, c, now, :] for c in ring.used}
            v = {c: src[iv, c, now, :] for c in ring.used}
            t = {c: src[ic, c, now, :] for c in ring.used}
            ue, uw = ring.sides(u)
            ve, vw = ring.sides(v)
            te, tw = ring.sides(t)
            for c in ring.todo:
                ocean = field[OCEAN, c, now, :]
                rotation = field[ROT, c, now, :]
                mixing = field[DIFF + k, c, now, :]
                tn, ts = src[ic, c, above_r, :], src[ic, c, below_r, :]
                heat_east, heat_north = te[c] - tw[c], tn - ts
                around_u = (ue[c] + uw[c]) + (src[iu, c, above_r, :] + src[iu, c, below_r, :])
                around_v = (ve[c] + vw[c]) + (src[iv, c, above_r, :] + src[iv, c, below_r, :])
                around_t = (te[c] + tw[c]) + (tn + ts)
                new_u = ocean * (
                    u[c] + rotation * v[c] - slope_east[c] - buoyancy_gain * heat_east
                    + mixing * (around_u - 4.0 * u[c])
                )
                new_v = ocean * (
                    v[c] - rotation * u[c] - slope_north[c] - buoyancy_gain * heat_north
                    + mixing * (around_v - 4.0 * v[c])
                )
                new_t = ocean * (
                    t[c] + mixing * (around_t - 4.0 * t[c])
                    - advection_gain * (new_u * heat_east + new_v * heat_north)
                )
                write(iu, c, new_u)
                write(iv, c, new_v)
                write(ic, c, new_t)

    def run_pass(join, one, two, own, own_slots, at_order, leave, back=False):
        step = jnp.where(down ^ back, -1, 1)

        def body(i, carry):
            j = i - 1
            at_order(j)
            join(j + 2, back)
            r = jnp.where(down ^ back, rows - TILE * j, TILE + TILE * j)
            surface_rows(field, surface_one, one, r + 3 * step)
            r_one = r + 2 * step

            def middle_write(channel, c, new):
                middle[channel, c, pl.ds(r_one, TILE), :] = new

            update_rows(field, surface_one, one, r_one, middle_write)
            surface_rows(middle, surface_two, one, r + step)

            @pl.when(j >= 0)
            def _():
                order = jnp.where(back, tiles - 1 - j, j)
                t = tile_of(order)

                def last_write(channel, c, new):
                    own[t, channel, own_slots[c]] = new

                update_rows(
                    middle, surface_two, two, pl.multiple_of(r, TILE), last_write
                )
                leave(order, t)

            return carry

        lax.fori_loop(0, tiles + 1, body, 0)

    def pair_copy(ref, kind, t):
        return pltpu.make_async_remote_copy(
            src_ref=ref.at[t], dst_ref=ref.at[t],
            send_sem=pair_send.at[kind], recv_sem=take_recv.at[kind, t],
            device_id=to_member(me + 1), device_id_type=MESH,
        )

    def next_copy(ref, kind, t):
        return pltpu.make_async_remote_copy(
            src_ref=ref.at[t], dst_ref=ref.at[t],
            send_sem=next_send.at[kind], recv_sem=take_recv.at[kind, t],
            device_id=to_member(me + 2), device_id_type=MESH,
        )

    def lend_copy(own, lent, kind, early, which, order):
        return pltpu.make_async_remote_copy(
            src_ref=own.at[tile_of(order)], dst_ref=lent.at[which, order - early],
            send_sem=lend_send.at[kind], recv_sem=lend_recv.at[kind, which],
            device_id=to_member(lender), device_id_type=MESH,
        )

    def lend_whole(own, lent, kind, early, which):
        return pltpu.make_async_remote_copy(
            src_ref=own.at[0 : tiles - early], dst_ref=lent.at[which, 0 : tiles - early],
            send_sem=lend_send.at[kind], recv_sem=lend_recv.at[kind, which],
            device_id=to_member(lender), device_id_type=MESH,
        )

    def leave_mid(order, t):
        @pl.when(me == 0)
        def _():
            for k in range(channels):
                for n in range(len(mids)):
                    control_mid[t, k, n] = own_mid[t, k, n]
            pair_copy(control_mid, 0, t).start()

            @pl.when(has_next & (order < mids_early))
            def _():
                next_copy(control_mid, 0, t).start()

        @pl.when((me > 1) & (order >= mids_early))
        def _():
            lend_copy(own_mid, lent_mid, 0, mids_early, client, order).start()

    def leave_rim(order, t):
        @pl.when(me == 0)
        def _():
            for k in range(channels):
                for n in range(len(rims)):
                    control_rim[t, k, n] = own_rim[t, k, n]
            pair_copy(control_rim, 1, t).start()

            @pl.when(has_next)
            def _():
                next_copy(control_rim, 1, t).start()

        @pl.when((me > 1) & (order >= rims_early))
        def _():
            lend_copy(own_rim, lent_rim, 1, rims_early, client, order).start()

    def start_rows():
        @pl.when(down)
        def _():
            north_rows()

        @pl.when(jnp.logical_not(down))
        def _():
            south_rows()

    def end_rows():
        @pl.when(down)
        def _():
            south_rows()

        @pl.when(jnp.logical_not(down))
        def _():
            north_rows()

    load_at = min(first_tiles - 1, tiles - 1)
    per = -(-tiles // PACK_STEPS)
    send_at = load_at + PACK_STEPS
    ahead = lats > 2 or send_at > tiles - 2

    def events_mid(j):
        if not ahead:
            @pl.when(j == load_at)
            def _():
                finish_loads()

            @pl.when((j >= load_at) & (j < send_at))
            def _():
                begin = (j - load_at) * per
                lax.fori_loop(begin, jnp.minimum(begin + per, tiles), pack_tile, 0)

            @pl.when(j == send_at)
            def _():
                send_halos()

        @pl.when(j == tiles - 1)
        def _():
            end_rows()

    if ahead:
        finish_loads()
        lax.fori_loop(0, tiles, pack_tile, 0)
        send_halos()
    start_rows()
    join_middle(0)
    ring_mid = mids + [halo]
    run_pass(
        join_middle, Ring(ring_mid, ring_mid), Ring(ring_mid, mids),
        own_mid, {c: n for n, c in enumerate(mids)}, events_mid, leave_mid,
    )

    for copy in sideways:
        copy.wait_recv()

    @pl.when(has_north)
    def _():
        for copy in south[1:]:
            copy.wait_recv()

    @pl.when(has_south)
    def _():
        for copy in north[1:]:
            copy.wait_recv()

    @pl.when(jnp.logical_not(has_north))
    def _():
        from_east[above, :] = zero_tile
        from_west[above, :] = zero_tile

    @pl.when(jnp.logical_not(has_south))
    def _():
        from_east[first, :] = zero_tile
        from_west[first, :] = zero_tile

    back = me > 1
    join_halo(0, back)
    ring_all = list(range(slots)) + [halo]
    run_pass(
        join_halo, Ring(ring_all, [slots - 1, halo, 0]), Ring(ring_all, rims),
        own_rim, {c: n for n, c in enumerate(rims)}, lambda j: None, leave_rim, back,
    )

    @pl.when((me == 0) & has_next)
    def _():
        def body(order, carry):
            next_copy(control_mid, 0, tile_of(order)).start()
            return carry

        lax.fori_loop(mids_early, tiles, body, 0)

    def clear(ref):
        for k in range(regions):
            ref[k] = zero_tile

    def ids_at(t, c):
        return region[pl.ds(pl.multiple_of(t * TILE, TILE), TILE), c * LANES : (c + 1) * LANES]

    def ocean_at(t, c):
        return field[OCEAN, c, pl.ds(pl.multiple_of(t * TILE + TILE, TILE), TILE), :]

    def add_regions(ref, items):
        for k in range(regions):
            total = ref[k]
            for ids, amount in items:
                total = total + jnp.where(ids == k, amount, 0.0)
            ref[k] = total

    def compare(ref, mine, its, t, part):
        items = []
        for n, c in enumerate(part):
            total = None
            for k in range(channels):
                d = mine(k, n) - its(k, n)
                total = d * d if total is None else total + d * d
            items.append((ids_at(t, c), ocean_at(t, c) * total))
        add_regions(ref, items)

    def share(which):
        for p, (a, b) in enumerate(peers):
            pltpu.make_async_remote_copy(
                src_ref=gathered.at[which, 0], dst_ref=gathered.at[which, p + 1],
                send_sem=sum_send.at[which], recv_sem=sum_recv.at[which],
                device_id=at(a, b), device_id_type=MESH,
            ).start()

    def collect(which):
        others = gathered.at[which, 1 : len(peers) + 1]
        pltpu.make_async_remote_copy(
            src_ref=others, dst_ref=others, send_sem=sum_send.at[which], recv_sem=sum_recv.at[which],
            device_id=at(*peers[0]), device_id_type=MESH,
        ).wait()
        total = gathered[which, 0]
        for p in range(len(peers)):
            total = total + gathered[which, p + 1]
        return jnp.sum(total, axis=1, keepdims=True)

    load_region.wait()
    clear(squares)
    clear(counts)

    def count(t, carry):
        add_regions(counts, [(ids_at(t, c), ocean_at(t, c)) for c in range(slots)])
        return carry

    lax.fori_loop(0, tiles, count, 0)
    gathered[0, 0] = jnp.sum(counts[...], axis=1)
    share(0)

    kinds = [
        (0, own_mid, control_mid, lent_mid, mids, mids_early),
        (1, own_rim, control_rim, lent_rim, rims, rims_early),
    ]

    def take(kind, order):
        _, own, control, _, part, _ = kinds[kind]
        t = tile_of(order)

        @pl.when(even)
        def _():
            next_copy(control, kind, t).wait_recv()

            @pl.when(has_pair)
            def _():
                pair_copy(control, kind, t).start()

            @pl.when(has_next)
            def _():
                next_copy(control, kind, t).start()

        @pl.when(jnp.logical_not(even))
        def _():
            pair_copy(control, kind, t).wait_recv()

    def weigh(kind, order):
        _, own, control, _, part, _ = kinds[kind]
        t = tile_of(order)
        compare(squares, lambda k, n: own[t, k, n], lambda k, n: control[t, k, n], t, part)

    def loop(begin, end, *actions):
        def body(order, carry):
            for action in actions:
                action(order)
            return carry

        lax.fori_loop(begin, end, body, 0)

    @pl.when(me > 0)
    def _():
        late_mids = jnp.where(me == 1, tiles, mids_early)
        late_rims = jnp.where(me == 1, tiles, rims_early)
        loop(0, mids_early, lambda o: take(0, o), lambda o: weigh(0, o))
        loop(0, late_rims, lambda o: take(1, o), lambda o: weigh(1, o))
        loop(mids_early, late_mids, lambda o: take(0, o), lambda o: weigh(0, o))

    def loan_copy(other, which):
        return pltpu.make_async_remote_copy(
            src_ref=loan_out.at[which], dst_ref=loan,
            send_sem=loan_send.at[which], recv_sem=loan_recv,
            device_id=to_member(other), device_id_type=MESH,
        )

    def lend(which, other):
        clear(lent_squares)
        for kind, own, control, lent, part, early in kinds:
            if early == tiles:
                continue

            def body(order, carry):
                t = tile_of(order)
                compare(
                    lent_squares,
                    lambda k, n: lent[which, order - early, k, n],
                    lambda k, n: control[t, k, n], t, part,
                )
                return carry

            lend_whole(own, lent, kind, early, which).wait_recv()
            lax.fori_loop(early, tiles, body, 0)
        loan_out[which] = jnp.sum(lent_squares[...], axis=1)
        loan_copy(other, which).start()

    gathered[1, 0] = jnp.sum(squares[...], axis=1)

    @pl.when(me == 1)
    def _():
        for which in range(clients):
            lend(which, which + 2)

    @pl.when(me > 1)
    def _():
        loan_copy(me, 0).wait_recv()
        gathered[1, 0] = gathered[1, 0] + loan[...]

    share(1)
    count_sum = collect(0)
    square_sum = collect(1)
    growth = jnp.sqrt(square_sum / (count_sum * channels) + epsilon)
    growth_wide = jnp.broadcast_to(growth, (regions, LANES))
    growth_out[...] = growth_wide
    load_target.wait()
    for k in range(regions):
        value[k] = jnp.broadcast_to(target[k] / growth_wide[k : k + 1, :], (TILE, LANES))

    def make_factor(t, carry):
        for c in range(slots):
            ids = ids_at(t, c)
            total = zero_tile
            for k in range(regions):
                total = jnp.where(ids == k, value[k], total)
            factor[t, c] = total
        return carry

    lax.fori_loop(0, tiles, make_factor, 0)

    def breed(kind, order):
        _, own, control, _, part, _ = kinds[kind]
        t = tile_of(order)
        now = pl.ds(pl.multiple_of(t * TILE, TILE), TILE)
        for n, c in enumerate(part):
            scale = factor[t, c]
            for k in range(channels):
                base = control[t, k, n]
                bred[k, now, c * LANES : (c + 1) * LANES] = base + scale * (own[t, k, n] - base)

    def take_late(kind, order):
        @pl.when(me > 1)
        def _():
            take(kind, order)

    loop(0, mids_early, lambda o: breed(0, o))
    loop(0, rims_early, lambda o: breed(1, o))
    loop(rims_early, tiles, lambda o: take_late(1, o), lambda o: breed(1, o))
    loop(mids_early, tiles, lambda o: take_late(0, o), lambda o: breed(0, o))

    for copy in sideways:
        copy.wait_send()

    @pl.when(has_north)
    def _():
        for copy in north:
            copy.wait_send()

    @pl.when(has_south)
    def _():
        for copy in south:
            copy.wait_send()

    for kind, own, control, lent, part, early in kinds:
        def whole_control(send, other):
            return pltpu.make_async_remote_copy(
                src_ref=control, dst_ref=control, send_sem=send.at[kind], recv_sem=take_recv.at[kind, 0],
                device_id=to_member(other), device_id_type=MESH,
            )

        @pl.when(has_pair)
        def _():
            whole_control(pair_send, me + 1).wait_send()

        @pl.when(has_next)
        def _():
            whole_control(next_send, me + 2).wait_send()

    @pl.when(me == 1)
    def _():
        for which in range(clients):
            loan_copy(which + 2, which).wait_send()

    @pl.when(me > 1)
    def _():
        for kind, own, control, lent, part, early in kinds:
            if early < tiles:
                lend_whole(own, lent, kind, early, client).wait_send()


def write_kernel(bred_in, growth_in, bred, growth, out_sem):
    copy = pltpu.make_async_copy(bred_in, bred, out_sem)
    copy.start()
    shape = growth_in.shape
    diagonal = lax.broadcasted_iota(jnp.int32, shape, 0) == lax.broadcasted_iota(jnp.int32, shape, 1)
    line = jnp.sum(jnp.where(diagonal, growth_in[...], 0.0), axis=0, keepdims=True)
    growth[...] = line[:, 0 : growth.shape[1]]
    copy.wait()


def per_device(
    sizes, member_state, column_depth, rotation, diffusivity, ocean_mask, region_id, target_rms
):
    members, lons, lats = sizes
    _, channels, rows, columns = member_state.shape
    regions = target_rms.shape[0]
    fields = channels + 3 + LEV
    tall = rows + 2 * TILE
    tiles = rows // TILE
    slots = columns // LANES
    group = lons * lats
    clients = max(members - 2, 1)
    late_mids = max(tiles - MIDS_EARLY, 1)
    late_rims = max(tiles - RIMS_EARLY, 1)
    f32 = jnp.float32
    anywhere = pl.BlockSpec(memory_space=pl.ANY)
    resident = pl.BlockSpec(memory_space=pltpu.VMEM)
    piece_mid = (channels, slots - 2, TILE, LANES)
    piece_rim = (channels, 2, TILE, LANES)
    bred, growth_wide = pl.pallas_call(
        functools.partial(cycle_kernel, sizes),
        out_shape=(
            pltpu.VMEM((channels, rows, columns), f32),
            pltpu.VMEM((regions, LANES), f32),
        ),
        in_specs=[anywhere] * 7,
        out_specs=(resident,) * 2,
        scratch_shapes=[
            pltpu.VMEM((fields, slots + 1, tall, LANES), f32),
            pltpu.VMEM((channels, slots + 1, tall, LANES), f32),
            pltpu.VMEM((slots + 1, tall, LANES), f32),
            pltpu.VMEM((slots + 1, tall, LANES), f32),
            pltpu.VMEM((tiles,) + piece_mid, f32),
            pltpu.VMEM((tiles,) + piece_rim, f32),
            pltpu.VMEM((tiles,) + piece_mid, f32),
            pltpu.VMEM((tiles,) + piece_rim, f32),
            pltpu.VMEM((clients, late_mids) + piece_mid, f32),
            pltpu.VMEM((clients, late_rims) + piece_rim, f32),
            pltpu.VMEM((rows, LANES), f32),
            pltpu.VMEM((rows, LANES), f32),
            pltpu.VMEM((tall, LANES), f32),
            pltpu.VMEM((tall, LANES), f32),
            pltpu.VMEM((fields // 2, slots, TILE, LANES), f32),
            pltpu.VMEM((fields // 2, slots, TILE, LANES), f32),
            pltpu.VMEM((fields // 2, slots, TILE, LANES), f32),
            pltpu.VMEM((fields // 2, slots, TILE, LANES), f32),
            pltpu.VMEM((rows, columns), jnp.int32),
            pltpu.VMEM((rows, columns), jnp.int32),
            pltpu.VMEM((regions, TILE, LANES), f32),
            pltpu.VMEM((regions, TILE, LANES), f32),
            pltpu.VMEM((regions, TILE, LANES), f32),
            pltpu.VMEM((2, group, regions, LANES), f32),
            pltpu.VMEM((clients, regions, LANES), f32),
            pltpu.VMEM((regions, LANES), f32),
            pltpu.VMEM((regions, TILE, LANES), f32),
            pltpu.VMEM((tiles, slots, TILE, LANES), f32),
            pltpu.SMEM((regions,), f32),
            pltpu.SemaphoreType.DMA((4,)),
            pltpu.SemaphoreType.DMA((8,)),
            pltpu.SemaphoreType.DMA((8,)),
            pltpu.SemaphoreType.DMA((2,)),
            pltpu.SemaphoreType.DMA((2,)),
            pltpu.SemaphoreType.DMA((2, tiles)),
            pltpu.SemaphoreType.DMA((2,)),
            pltpu.SemaphoreType.DMA((2, clients)),
            pltpu.SemaphoreType.DMA((clients,)),
            pltpu.SemaphoreType.DMA,
            pltpu.SemaphoreType.DMA((2,)),
            pltpu.SemaphoreType.DMA((2,)),
            pltpu.SemaphoreType.REGULAR,
        ],
        compiler_params=pltpu.CompilerParams(
            collective_id=0, has_side_effects=True, vmem_limit_bytes=KERNEL_BYTES
        ),
    )(
        member_state.reshape(channels, rows, columns),
        column_depth, rotation, diffusivity, ocean_mask, region_id, target_rms,
    )
    bred, growth = pl.pallas_call(
        write_kernel,
        out_shape=(
            jax.ShapeDtypeStruct((channels, rows, columns), f32),
            jax.ShapeDtypeStruct((1, regions), f32),
        ),
        in_specs=[resident, resident],
        out_specs=(anywhere, resident),
        scratch_shapes=[pltpu.SemaphoreType.DMA],
        compiler_params=pltpu.CompilerParams(vmem_limit_bytes=WRITE_BYTES),
    )(bred, growth_wide)
    return (bred[None], growth)


def solution(mesh):
    sizes = (mesh.shape["member"], mesh.shape["lon"], mesh.shape["lat"])
    return jax.shard_map(
        functools.partial(per_device, sizes),
        mesh=mesh,
        in_specs=(
            P("member", None, "lat", "lon"),
            P("lat", "lon"),
            P("lat", "lon"),
            P(None, "lat", "lon"),
            P("lat", "lon"),
            P("lat", "lon"),
            P(),
        ),
        out_specs=(P("member", None, "lat", "lon"), P("member", None)),
        check_vma=False,
    )
```

```python
import functools

import jax
import jax.numpy as jnp
from jax import lax
from jax.experimental import pallas as pl
from jax.experimental.pallas import tpu as pltpu
from jax.sharding import PartitionSpec as P

LEV = 5
STEPS = 2
MARGIN = 2 * STEPS
TILE = 8
LANES = 128
FIRST_ROWS = 4
PACK_AT = 4
PACK_STEPS = 2
PACK_TILES = 4
TAKE_FIRST = 3
MIDS_EARLY = 16
RIMS_EARLY = 11
KERNEL_BYTES = 56 * 2**20
WRITE_BYTES = 16 * 2**20

divergence_gain = 0.25
pressure_gain = 0.25
buoyancy_gain = 0.1
advection_gain = 0.05
epsilon = 1e-06

MESH = pl.DeviceIdType.MESH


def cycle_kernel(
    sizes,
    state_in, depth_in, rotation_in, diffusivity_in, mask_in, region_in, target_in,
    bred, growth_out,
    field, middle, surface_one, surface_two,
    own_mid, own_rim, control_mid, control_rim, lent_mid, lent_rim,
    send_east, send_west, from_east, from_west, send_north, send_south, from_north, from_south,
    mask, region, squares, lent_squares, counts, gathered, loan_out, loan, value, factor, target,
    in_sem, halo_send, halo_recv, pair_send, next_send, take_recv,
    lend_send, lend_recv, loan_send, loan_recv, sum_send, sum_recv, go,
):
    members, lons, lats = sizes
    channels, rows, columns = state_in.shape
    regions = squares.shape[0]
    fields = field.shape[0]
    slots = columns // LANES
    halo = slots
    tiles = rows // TILE
    tall = rows + 2 * TILE
    clients = members - 2
    DEPTH, ROT, OCEAN, DIFF = channels, channels + 1, channels + 2, channels + 3
    mids = list(range(1, slots - 1))
    rims = [0, slots - 1]
    half = TILE // 2
    first_tiles = min(FIRST_ROWS, tiles)
    mids_early = min(MIDS_EARLY, tiles)
    rims_early = min(RIMS_EARLY, tiles)

    me = lax.axis_index("member")
    lon = lax.axis_index("lon")
    lat = lax.axis_index("lat")
    core = lax.rem(me, 2)
    client = me - 2

    down = 2 * lat >= lats
    has_north = lat < lats - 1
    has_south = lat > 0

    def tile_of(order):
        return jnp.where(down, tiles - 1 - order, order)

    def tall_of(order, back=False):
        return jnp.where(down ^ back, tiles + 1 - order, order)

    def at(dlat, dlon, member=None):
        return {
            "member": me if member is None else member,
            "lon": lax.rem(lon + dlon + lons, lons),
            "lat": lax.rem(lat + dlat + lats, lats),
        }

    def to_member(other):
        return {"member": other, "lon": lon, "lat": lat}

    even = core == 0
    has_pair = even & (me + 1 < members)
    has_next = even & (me + 2 < members)
    parent = jnp.where(even, me - 2, me - 1)
    lender = 1
    peers = [(a, b) for a in range(lats) for b in range(lons) if (a, b) != (0, 0)]
    peers.sort(key=lambda p: -(p[0] + min(p[1], lons - p[1]) + p[1]))

    first_rows = first_tiles * TILE
    other_rows = rows - first_rows
    first_row = pl.multiple_of(jnp.where(down, rows - first_rows, 0), TILE)
    other_row = pl.multiple_of(jnp.where(down, 0, first_rows), TILE)

    def loads(index, row, count):
        src = pl.ds(row, count)
        dst = pl.ds(pl.multiple_of(row + TILE, TILE), count)
        copies = []
        for c in range(slots):
            part = slice(c * LANES, (c + 1) * LANES)
            copies += [
                (state_in.at[:, src, part], field.at[0:channels, c, dst, :]),
                (depth_in.at[src, part], field.at[DEPTH, c, dst, :]),
                (rotation_in.at[src, part], field.at[ROT, c, dst, :]),
                (diffusivity_in.at[:, src, part], field.at[DIFF:fields, c, dst, :]),
            ]
        copies.append((mask_in.at[src, :], mask.at[src, :]))
        return [pltpu.make_async_copy(a, b, in_sem.at[index]) for a, b in copies]

    def loaded(index, row, count):
        part = field.at[:, 0:slots, pl.ds(pl.multiple_of(row + TILE, TILE), count), :]
        pltpu.make_async_copy(part, part, in_sem.at[index]).wait()

    load_first = loads(0, first_row, first_rows)
    load_other = loads(1, other_row, other_rows) if other_rows else []
    load_region = pltpu.make_async_copy(region_in, region, in_sem.at[2])
    load_target = pltpu.make_async_copy(target_in, target, in_sem.at[3])
    for load in load_first + load_other + [load_region, load_target]:
        load.start()

    barrier = pltpu.get_barrier_semaphore()

    def greet(device):
        pl.semaphore_signal(barrier, inc=1, device_id=device, device_id_type=MESH)

    @pl.when(me == 0)
    def _():
        greet(to_member(1))
        for a, b in peers:
            greet(at(a, b, 1))

    @pl.when(me > 0)
    def _():
        for a, b in peers:
            greet(at(a, b))
        greet(to_member(parent))

    @pl.when(me == 1)
    def _():
        for other in range(2, members):
            greet(to_member(other))

    @pl.when(me > 1)
    def _():
        greet(to_member(lender))

    @pl.when(me == 0)
    def _():
        pl.semaphore_wait(barrier, 2 if members > 2 else 1)

    def all_here():
        @pl.when(me == 0)
        def _():
            pl.semaphore_wait(go, 1)

        @pl.when(me > 1)
        def _():
            pl.semaphore_wait(
                barrier,
                len(peers) + 1 + has_pair.astype(jnp.int32) + has_next.astype(jnp.int32),
            )

    @pl.when(me == 1)
    def _():
        pl.semaphore_wait(barrier, 2 * len(peers) + 1 + clients)
        pl.semaphore_signal(go, inc=1, device_id=to_member(0), device_id_type=MESH)

    lane = lax.broadcasted_iota(jnp.int32, (TILE, LANES), 1)
    zero_tile = jnp.zeros((TILE, LANES), jnp.float32)
    low_lanes = lane < LANES // 2
    easterly = lax.rem(lane, 2 * MARGIN) >= MARGIN

    loaded(0, first_row, first_rows)

    def make_ocean(t, carry):
        r = pl.multiple_of(t * TILE, TILE)
        for c in range(slots):
            field[OCEAN, c, pl.ds(pl.multiple_of(r + TILE, TILE), TILE), :] = mask[
                pl.ds(r, TILE), c * LANES : (c + 1) * LANES
            ].astype(jnp.float32)
        return carry

    lax.fori_loop(first_row // TILE, first_row // TILE + first_tiles, make_ocean, 0)

    def remote(src, dst, index, device):
        return pltpu.make_async_remote_copy(
            src_ref=src, dst_ref=dst, send_sem=halo_send.at[index], recv_sem=halo_recv.at[index],
            device_id=device, device_id_type=MESH,
        )

    whole = slice(TILE, TILE + rows)
    last = slice(rows - TILE, rows)
    first = slice(0, TILE)
    above = slice(rows + TILE, rows + 2 * TILE)
    north = [
        remote(send_north, from_south, 0, at(1, 0)),
        remote(send_east.at[last], from_west.at[first], 4, at(1, 1)),
        remote(send_west.at[last], from_east.at[first], 5, at(1, -1)),
    ]
    south = [
        remote(send_south, from_north, 1, at(-1, 0)),
        remote(send_east.at[first], from_west.at[above], 6, at(-1, 1)),
        remote(send_west.at[first], from_east.at[above], 7, at(-1, -1)),
    ]
    sideways = [
        remote(send_east, from_west.at[whole], 2, at(0, 1)),
        remote(send_west, from_east.at[whole], 3, at(0, -1)),
    ]

    block = PACK_TILES if tiles % PACK_TILES == 0 else 1
    blocks = tiles // block

    def pack_block(b, carry):
        for i in range(block):
            r = pl.multiple_of((b * block + i) * TILE, TILE)
            now = pl.ds(pl.multiple_of(r + TILE, TILE), TILE)
            packed = [zero_tile] * 2
            for f in range(fields):
                g, s = divmod(f * 2 * MARGIN, LANES)
                edges = jnp.where(low_lanes, field[f, 0, now, :], field[f, slots - 1, now, :])
                here = (lane >= s) & (lane < s + 2 * MARGIN)
                packed[g] = jnp.where(here, pltpu.roll(edges, s + MARGIN, 1), packed[g])
            near, far = packed
            send_east[pl.ds(r, TILE), :] = jnp.where(easterly, pltpu.roll(far, MARGIN, 1), near)
            send_west[pl.ds(r, TILE), :] = jnp.where(easterly, near, pltpu.roll(far, LANES - MARGIN, 1))
        return carry

    def finish_loads():
        if other_rows:
            loaded(1, other_row, other_rows)
            lax.fori_loop(other_row // TILE, other_row // TILE + other_rows // TILE, make_ocean, 0)

    def pack_rows():
        for k in range(fields // 2):
            for c in range(slots):
                send_north[k, c, 0:half, :] = field[2 * k, c, rows + half : rows + TILE, :]
                send_north[k, c, half:TILE, :] = field[2 * k + 1, c, rows + half : rows + TILE, :]
                send_south[k, c, 0:half, :] = field[2 * k, c, TILE : TILE + half, :]
                send_south[k, c, half:TILE, :] = field[2 * k + 1, c, TILE : TILE + half, :]

    def send_halos():
        pack_rows()
        all_here()

        @pl.when(has_north)
        def _():
            for copy in north:
                copy.start()

        @pl.when(has_south)
        def _():
            for copy in south:
                copy.start()

        for copy in sideways:
            copy.start()

    def south_rows():
        @pl.when(has_south)
        def _():
            north[0].wait_recv()

        @pl.when(jnp.logical_not(has_south))
        def _():
            from_south[...] = jnp.zeros_like(from_south)

        for k in range(fields // 2):
            for c in range(slots):
                field[2 * k, c, half:TILE, :] = from_south[k, c, 0:half, :]
                field[2 * k + 1, c, half:TILE, :] = from_south[k, c, half:TILE, :]
                field[2 * k, c, 0:half, :] = from_south[k, c, 0:half, :]
                field[2 * k + 1, c, 0:half, :] = from_south[k, c, half:TILE, :]

    def north_rows():
        @pl.when(has_north)
        def _():
            south[0].wait_recv()

        @pl.when(jnp.logical_not(has_north))
        def _():
            from_north[...] = jnp.zeros_like(from_north)

        base = rows + TILE
        for k in range(fields // 2):
            for c in range(slots):
                field[2 * k, c, base : base + half, :] = from_north[k, c, 0:half, :]
                field[2 * k + 1, c, base : base + half, :] = from_north[k, c, half:TILE, :]
                field[2 * k, c, base + half : base + TILE, :] = from_north[k, c, 0:half, :]
                field[2 * k + 1, c, base + half : base + TILE, :] = from_north[k, c, half:TILE, :]

    def join_middle(order, back=False):
        now = pl.ds(pl.multiple_of(tall_of(order) * TILE, TILE), TILE)
        for f in range(fields):
            field[f, halo, now, :] = jnp.where(low_lanes, field[f, slots - 1, now, :], field[f, 0, now, :])

    def join_halo(order, back):
        now = pl.ds(pl.multiple_of(tall_of(order, back) * TILE, TILE), TILE)
        east, west = from_east[now, :], from_west[now, :]
        both = [
            jnp.where(easterly, east, west),
            jnp.where(easterly, pltpu.roll(east, MARGIN, 1), pltpu.roll(west, LANES - MARGIN, 1)),
        ]
        for f in range(fields):
            g, s = divmod(f * 2 * MARGIN, LANES)
            field[f, halo, now, :] = pltpu.roll(both[g], LANES - s - MARGIN, 1)

    class Ring:
        def __init__(self, ring, todo):
            self.todo = todo
            size = len(ring)
            place = {c: i for i, c in enumerate(ring)}
            self.east = {c: ring[(place[c] + 1) % size] for c in todo}
            self.west = {c: ring[(place[c] - 1) % size] for c in todo}
            self.used = sorted(set(todo) | set(self.east.values()) | set(self.west.values()))

        def sides(self, q):
            to_east = {c: pltpu.roll(q[c], LANES - 1, 1) for c in {*self.todo, *self.east.values()}}
            to_west = {c: pltpu.roll(q[c], 1, 1) for c in {*self.todo, *self.west.values()}}
            e = {c: jnp.where(lane == LANES - 1, to_east[self.east[c]], to_east[c]) for c in self.todo}
            w = {c: jnp.where(lane == 0, to_west[self.west[c]], to_west[c]) for c in self.todo}
            return e, w

    def surface_rows(src, dst, ring, r):
        now, above_r, below_r = pl.ds(r, TILE), pl.ds(r + 1, TILE), pl.ds(r - 1, TILE)

        def add_up(base, c, where):
            total = src[base, c, where, :]
            for k in range(1, LEV):
                total = total + src[base + k, c, where, :]
            return total

        e, w = ring.sides({c: add_up(1, c, now) for c in ring.used})
        for c in ring.todo:
            n, s = add_up(1 + LEV, c, above_r), add_up(1 + LEV, c, below_r)
            divergence = (e[c] - w[c]) + (n - s)
            dst[c, now, :] = field[OCEAN, c, now, :] * (
                src[0, c, now, :] - (divergence_gain / LEV) * field[DEPTH, c, now, :] * divergence
            )

    def update_rows(src, surface, ring, r, write):
        now, above_r, below_r = pl.ds(r, TILE), pl.ds(r + 1, TILE), pl.ds(r - 1, TILE)
        h = {c: surface[c, now, :] for c in ring.used}
        e, w = ring.sides(h)
        slope_east, slope_north = {}, {}
        for c in ring.todo:
            slope_east[c] = pressure_gain * (e[c] - w[c])
            slope_north[c] = pressure_gain * (surface[c, above_r, :] - surface[c, below_r, :])
            write(0, c, h[c])
        for k in range(LEV):
            iu, iv, ic = 1 + k, 1 + LEV + k, 1 + 2 * LEV + k
            u = {c: src[iu, c, now, :] for c in ring.used}
            v = {c: src[iv, c, now, :] for c in ring.used}
            t = {c: src[ic, c, now, :] for c in ring.used}
            ue, uw = ring.sides(u)
            ve, vw = ring.sides(v)
            te, tw = ring.sides(t)
            for c in ring.todo:
                ocean = field[OCEAN, c, now, :]
                rotation = field[ROT, c, now, :]
                mixing = field[DIFF + k, c, now, :]
                tn, ts = src[ic, c, above_r, :], src[ic, c, below_r, :]
                heat_east, heat_north = te[c] - tw[c], tn - ts
                around_u = (ue[c] + uw[c]) + (src[iu, c, above_r, :] + src[iu, c, below_r, :])
                around_v = (ve[c] + vw[c]) + (src[iv, c, above_r, :] + src[iv, c, below_r, :])
                around_t = (te[c] + tw[c]) + (tn + ts)
                new_u = ocean * (
                    u[c] + rotation * v[c] - slope_east[c] - buoyancy_gain * heat_east
                    + mixing * (around_u - 4.0 * u[c])
                )
                new_v = ocean * (
                    v[c] - rotation * u[c] - slope_north[c] - buoyancy_gain * heat_north
                    + mixing * (around_v - 4.0 * v[c])
                )
                new_t = ocean * (
                    t[c] + mixing * (around_t - 4.0 * t[c])
                    - advection_gain * (new_u * heat_east + new_v * heat_north)
                )
                write(iu, c, new_u)
                write(iv, c, new_v)
                write(ic, c, new_t)

    def run_pass(join, one, two, own, own_slots, at_order, leave, back=False):
        step = jnp.where(down ^ back, -1, 1)

        def body(i, carry):
            j = i - 1
            at_order(j)
            join(j + 2, back)
            r = jnp.where(down ^ back, rows - TILE * j, TILE + TILE * j)
            surface_rows(field, surface_one, one, r + 3 * step)
            r_one = r + 2 * step

            def middle_write(channel, c, new):
                middle[channel, c, pl.ds(r_one, TILE), :] = new

            update_rows(field, surface_one, one, r_one, middle_write)
            surface_rows(middle, surface_two, one, r + step)

            @pl.when(j >= 0)
            def _():
                order = jnp.where(back, tiles - 1 - j, j)
                t = tile_of(order)

                def last_write(channel, c, new):
                    own[t, channel, own_slots[c]] = new

                update_rows(
                    middle, surface_two, two, pl.multiple_of(r, TILE), last_write
                )
                leave(order, t)

            return carry

        lax.fori_loop(0, tiles + 1, body, 0)

    def pair_copy(ref, kind, t):
        return pltpu.make_async_remote_copy(
            src_ref=ref.at[t], dst_ref=ref.at[t],
            send_sem=pair_send.at[kind], recv_sem=take_recv.at[kind, t],
            device_id=to_member(me + 1), device_id_type=MESH,
        )

    def next_copy(ref, kind, t):
        return pltpu.make_async_remote_copy(
            src_ref=ref.at[t], dst_ref=ref.at[t],
            send_sem=next_send.at[kind], recv_sem=take_recv.at[kind, t],
            device_id=to_member(me + 2), device_id_type=MESH,
        )

    def lend_copy(own, lent, kind, early, which, order):
        return pltpu.make_async_remote_copy(
            src_ref=own.at[tile_of(order)], dst_ref=lent.at[which, order - early],
            send_sem=lend_send.at[kind], recv_sem=lend_recv.at[kind, which],
            device_id=to_member(lender), device_id_type=MESH,
        )

    def lend_whole(own, lent, kind, early, which):
        return pltpu.make_async_remote_copy(
            src_ref=own.at[0 : tiles - early], dst_ref=lent.at[which, 0 : tiles - early],
            send_sem=lend_send.at[kind], recv_sem=lend_recv.at[kind, which],
            device_id=to_member(lender), device_id_type=MESH,
        )

    def leave_mid(order, t):
        @pl.when(me == 0)
        def _():
            for k in range(channels):
                for n in range(len(mids)):
                    control_mid[t, k, n] = own_mid[t, k, n]
            pair_copy(control_mid, 0, t).start()

            @pl.when(has_next & (order < mids_early))
            def _():
                next_copy(control_mid, 0, t).start()

        @pl.when((me > 1) & (order >= mids_early))
        def _():
            lend_copy(own_mid, lent_mid, 0, mids_early, client, order).start()

    def leave_rim(order, t):
        @pl.when(me == 0)
        def _():
            for k in range(channels):
                for n in range(len(rims)):
                    control_rim[t, k, n] = own_rim[t, k, n]
            pair_copy(control_rim, 1, t).start()

            @pl.when(has_next)
            def _():
                next_copy(control_rim, 1, t).start()

        @pl.when((me > 1) & (order >= rims_early))
        def _():
            lend_copy(own_rim, lent_rim, 1, rims_early, client, order).start()

    def start_rows():
        @pl.when(down)
        def _():
            north_rows()

        @pl.when(jnp.logical_not(down))
        def _():
            south_rows()

    def end_rows():
        @pl.when(down)
        def _():
            south_rows()

        @pl.when(jnp.logical_not(down))
        def _():
            north_rows()

    load_at = min(first_tiles - 1, tiles - 1)
    per = -(-blocks // PACK_STEPS)
    pack_at = max(load_at, PACK_AT)
    send_at = pack_at + PACK_STEPS
    ahead = lats > 2 or send_at > tiles - 2

    def events_mid(j):
        if not ahead:
            @pl.when(j == load_at)
            def _():
                finish_loads()

            @pl.when((j >= pack_at) & (j < send_at))
            def _():
                begin = (j - pack_at) * per
                lax.fori_loop(begin, jnp.minimum(begin + per, blocks), pack_block, 0)

            @pl.when(j == send_at)
            def _():
                send_halos()

        @pl.when(j == tiles - 1)
        def _():
            end_rows()

    if ahead:
        finish_loads()
        lax.fori_loop(0, blocks, pack_block, 0)
        send_halos()
    start_rows()
    join_middle(0)
    ring_mid = mids + [halo]
    run_pass(
        join_middle, Ring(ring_mid, ring_mid), Ring(ring_mid, mids),
        own_mid, {c: n for n, c in enumerate(mids)}, events_mid, leave_mid,
    )

    for copy in sideways:
        copy.wait_recv()

    @pl.when(has_north)
    def _():
        for copy in south[1:]:
            copy.wait_recv()

    @pl.when(has_south)
    def _():
        for copy in north[1:]:
            copy.wait_recv()

    @pl.when(jnp.logical_not(has_north))
    def _():
        from_east[above, :] = zero_tile
        from_west[above, :] = zero_tile

    @pl.when(jnp.logical_not(has_south))
    def _():
        from_east[first, :] = zero_tile
        from_west[first, :] = zero_tile

    back = me > 1
    join_halo(0, back)
    ring_all = list(range(slots)) + [halo]
    run_pass(
        join_halo, Ring(ring_all, [slots - 1, halo, 0]), Ring(ring_all, rims),
        own_rim, {c: n for n, c in enumerate(rims)}, lambda j: None, leave_rim, back,
    )

    @pl.when((me == 0) & has_next)
    def _():
        def body(order, carry):
            next_copy(control_mid, 0, tile_of(order)).start()
            return carry

        lax.fori_loop(mids_early, tiles, body, 0)

    def clear(ref):
        for k in range(regions):
            ref[k] = zero_tile

    def ids_at(t, c):
        return region[pl.ds(pl.multiple_of(t * TILE, TILE), TILE), c * LANES : (c + 1) * LANES]

    def ocean_at(t, c):
        return field[OCEAN, c, pl.ds(pl.multiple_of(t * TILE + TILE, TILE), TILE), :]

    def add_regions(ref, items):
        for k in range(regions):
            total = ref[k]
            for ids, amount in items:
                total = total + jnp.where(ids == k, amount, 0.0)
            ref[k] = total

    def compare(ref, mine, its, t, part):
        items = []
        for n, c in enumerate(part):
            total = None
            for k in range(channels):
                d = mine(k, n) - its(k, n)
                total = d * d if total is None else total + d * d
            items.append((ids_at(t, c), ocean_at(t, c) * total))
        add_regions(ref, items)

    def share(which):
        for p, (a, b) in enumerate(peers):
            pltpu.make_async_remote_copy(
                src_ref=gathered.at[which, 0], dst_ref=gathered.at[which, p + 1],
                send_sem=sum_send.at[which], recv_sem=sum_recv.at[which],
                device_id=at(a, b), device_id_type=MESH,
            ).start()

    def collect(which):
        others = gathered.at[which, 1 : len(peers) + 1]
        pltpu.make_async_remote_copy(
            src_ref=others, dst_ref=others, send_sem=sum_send.at[which], recv_sem=sum_recv.at[which],
            device_id=at(*peers[0]), device_id_type=MESH,
        ).wait()
        total = gathered[which, 0]
        for p in range(len(peers)):
            total = total + gathered[which, p + 1]
        return jnp.sum(total, axis=1, keepdims=True)

    load_region.wait()
    clear(squares)
    clear(counts)

    def count(t, carry):
        add_regions(counts, [(ids_at(t, c), ocean_at(t, c)) for c in range(slots)])
        return carry

    lax.fori_loop(0, tiles, count, 0)
    gathered[0, 0] = jnp.sum(counts[...], axis=1)
    share(0)

    kinds = [
        (0, own_mid, control_mid, lent_mid, mids, mids_early),
        (1, own_rim, control_rim, lent_rim, rims, rims_early),
    ]

    def take(kind, order):
        _, own, control, _, part, _ = kinds[kind]
        t = tile_of(order)

        @pl.when(even)
        def _():
            next_copy(control, kind, t).wait_recv()

            @pl.when(has_pair)
            def _():
                pair_copy(control, kind, t).start()

            @pl.when(has_next)
            def _():
                next_copy(control, kind, t).start()

        @pl.when(jnp.logical_not(even))
        def _():
            pair_copy(control, kind, t).wait_recv()

    def weigh(kind, order):
        _, own, control, _, part, _ = kinds[kind]
        t = tile_of(order)
        compare(squares, lambda k, n: own[t, k, n], lambda k, n: control[t, k, n], t, part)

    def loop(begin, end, *actions):
        def body(order, carry):
            for action in actions:
                action(order)
            return carry

        lax.fori_loop(begin, end, body, 0)

    @pl.when(me > 0)
    def _():
        late_mids = jnp.where(me == 1, tiles, mids_early)
        late_rims = jnp.where(me == 1, tiles, rims_early)
        loop(0, mids_early, lambda o: take(0, o), lambda o: weigh(0, o))
        loop(0, late_rims, lambda o: take(1, o), lambda o: weigh(1, o))
        loop(mids_early, late_mids, lambda o: take(0, o), lambda o: weigh(0, o))

    def loan_copy(other, which):
        return pltpu.make_async_remote_copy(
            src_ref=loan_out.at[which], dst_ref=loan,
            send_sem=loan_send.at[which], recv_sem=loan_recv,
            device_id=to_member(other), device_id_type=MESH,
        )

    def lend(which, other):
        clear(lent_squares)
        for kind, own, control, lent, part, early in kinds:
            if early == tiles:
                continue

            def body(order, carry):
                t = tile_of(order)
                compare(
                    lent_squares,
                    lambda k, n: lent[which, order - early, k, n],
                    lambda k, n: control[t, k, n], t, part,
                )
                return carry

            lend_whole(own, lent, kind, early, which).wait_recv()
            lax.fori_loop(early, tiles, body, 0)
        loan_out[which] = jnp.sum(lent_squares[...], axis=1)
        loan_copy(other, which).start()

    gathered[1, 0] = jnp.sum(squares[...], axis=1)

    @pl.when(me == 1)
    def _():
        for which in range(clients):
            lend(which, which + 2)

    @pl.when(me > 1)
    def _():
        loan_copy(me, 0).wait_recv()
        gathered[1, 0] = gathered[1, 0] + loan[...]

    share(1)
    taken = min(rims_early + TAKE_FIRST, tiles)

    @pl.when(me > 1)
    def _():
        loop(rims_early, taken, lambda o: take(1, o))

    count_sum = collect(0)
    square_sum = collect(1)
    growth = jnp.sqrt(square_sum / (count_sum * channels) + epsilon)
    growth_wide = jnp.broadcast_to(growth, (regions, LANES))
    growth_out[...] = growth_wide
    load_target.wait()
    for k in range(regions):
        value[k] = jnp.broadcast_to(target[k] / growth_wide[k : k + 1, :], (TILE, LANES))

    def make_factor(b, carry):
        for i in range(block):
            t = b * block + i
            for c in range(slots):
                ids = ids_at(t, c)
                total = zero_tile
                for k in range(regions):
                    total = jnp.where(ids == k, value[k], total)
                factor[t, c] = total
        return carry

    lax.fori_loop(0, blocks, make_factor, 0)

    def breed(kind, order):
        _, own, control, _, part, _ = kinds[kind]
        t = tile_of(order)
        now = pl.ds(pl.multiple_of(t * TILE, TILE), TILE)
        for n, c in enumerate(part):
            scale = factor[t, c]
            for k in range(channels):
                base = control[t, k, n]
                bred[k, now, c * LANES : (c + 1) * LANES] = base + scale * (own[t, k, n] - base)

    def take_late(kind, order):
        @pl.when(me > 1)
        def _():
            take(kind, order)

    loop(0, mids_early, lambda o: breed(0, o))
    loop(0, rims_early, lambda o: breed(1, o))
    loop(rims_early, taken, lambda o: breed(1, o))
    loop(taken, tiles, lambda o: take_late(1, o), lambda o: breed(1, o))
    loop(mids_early, tiles, lambda o: take_late(0, o), lambda o: breed(0, o))

    for copy in sideways:
        copy.wait_send()

    @pl.when(has_north)
    def _():
        for copy in north:
            copy.wait_send()

    @pl.when(has_south)
    def _():
        for copy in south:
            copy.wait_send()

    for kind, own, control, lent, part, early in kinds:
        def whole_control(send, other):
            return pltpu.make_async_remote_copy(
                src_ref=control, dst_ref=control, send_sem=send.at[kind], recv_sem=take_recv.at[kind, 0],
                device_id=to_member(other), device_id_type=MESH,
            )

        @pl.when(has_pair)
        def _():
            whole_control(pair_send, me + 1).wait_send()

        @pl.when(has_next)
        def _():
            whole_control(next_send, me + 2).wait_send()

    @pl.when(me == 1)
    def _():
        for which in range(clients):
            loan_copy(which + 2, which).wait_send()

    @pl.when(me > 1)
    def _():
        for kind, own, control, lent, part, early in kinds:
            if early < tiles:
                lend_whole(own, lent, kind, early, client).wait_send()


def write_kernel(bred_in, growth_in, bred, growth, out_sem):
    copy = pltpu.make_async_copy(bred_in, bred, out_sem)
    copy.start()
    shape = growth_in.shape
    diagonal = lax.broadcasted_iota(jnp.int32, shape, 0) == lax.broadcasted_iota(jnp.int32, shape, 1)
    line = jnp.sum(jnp.where(diagonal, growth_in[...], 0.0), axis=0, keepdims=True)
    growth[...] = line[:, 0 : growth.shape[1]]
    copy.wait()


def per_device(
    sizes, member_state, column_depth, rotation, diffusivity, ocean_mask, region_id, target_rms
):
    members, lons, lats = sizes
    _, channels, rows, columns = member_state.shape
    regions = target_rms.shape[0]
    fields = channels + 3 + LEV
    tall = rows + 2 * TILE
    tiles = rows // TILE
    slots = columns // LANES
    group = lons * lats
    clients = max(members - 2, 1)
    late_mids = max(tiles - MIDS_EARLY, 1)
    late_rims = max(tiles - RIMS_EARLY, 1)
    f32 = jnp.float32
    anywhere = pl.BlockSpec(memory_space=pl.ANY)
    resident = pl.BlockSpec(memory_space=pltpu.VMEM)
    piece_mid = (channels, slots - 2, TILE, LANES)
    piece_rim = (channels, 2, TILE, LANES)
    bred, growth_wide = pl.pallas_call(
        functools.partial(cycle_kernel, sizes),
        out_shape=(
            pltpu.VMEM((channels, rows, columns), f32),
            pltpu.VMEM((regions, LANES), f32),
        ),
        in_specs=[anywhere] * 7,
        out_specs=(resident,) * 2,
        scratch_shapes=[
            pltpu.VMEM((fields, slots + 1, tall, LANES), f32),
            pltpu.VMEM((channels, slots + 1, tall, LANES), f32),
            pltpu.VMEM((slots + 1, tall, LANES), f32),
            pltpu.VMEM((slots + 1, tall, LANES), f32),
            pltpu.VMEM((tiles,) + piece_mid, f32),
            pltpu.VMEM((tiles,) + piece_rim, f32),
            pltpu.VMEM((tiles,) + piece_mid, f32),
            pltpu.VMEM((tiles,) + piece_rim, f32),
            pltpu.VMEM((clients, late_mids) + piece_mid, f32),
            pltpu.VMEM((clients, late_rims) + piece_rim, f32),
            pltpu.VMEM((rows, LANES), f32),
            pltpu.VMEM((rows, LANES), f32),
            pltpu.VMEM((tall, LANES), f32),
            pltpu.VMEM((tall, LANES), f32),
            pltpu.VMEM((fields // 2, slots, TILE, LANES), f32),
            pltpu.VMEM((fields // 2, slots, TILE, LANES), f32),
            pltpu.VMEM((fields // 2, slots, TILE, LANES), f32),
            pltpu.VMEM((fields // 2, slots, TILE, LANES), f32),
            pltpu.VMEM((rows, columns), jnp.int32),
            pltpu.VMEM((rows, columns), jnp.int32),
            pltpu.VMEM((regions, TILE, LANES), f32),
            pltpu.VMEM((regions, TILE, LANES), f32),
            pltpu.VMEM((regions, TILE, LANES), f32),
            pltpu.VMEM((2, group, regions, LANES), f32),
            pltpu.VMEM((clients, regions, LANES), f32),
            pltpu.VMEM((regions, LANES), f32),
            pltpu.VMEM((regions, TILE, LANES), f32),
            pltpu.VMEM((tiles, slots, TILE, LANES), f32),
            pltpu.SMEM((regions,), f32),
            pltpu.SemaphoreType.DMA((4,)),
            pltpu.SemaphoreType.DMA((8,)),
            pltpu.SemaphoreType.DMA((8,)),
            pltpu.SemaphoreType.DMA((2,)),
            pltpu.SemaphoreType.DMA((2,)),
            pltpu.SemaphoreType.DMA((2, tiles)),
            pltpu.SemaphoreType.DMA((2,)),
            pltpu.SemaphoreType.DMA((2, clients)),
            pltpu.SemaphoreType.DMA((clients,)),
            pltpu.SemaphoreType.DMA,
            pltpu.SemaphoreType.DMA((2,)),
            pltpu.SemaphoreType.DMA((2,)),
            pltpu.SemaphoreType.REGULAR,
        ],
        compiler_params=pltpu.CompilerParams(
            collective_id=0, has_side_effects=True, vmem_limit_bytes=KERNEL_BYTES
        ),
    )(
        member_state.reshape(channels, rows, columns),
        column_depth, rotation, diffusivity, ocean_mask, region_id, target_rms,
    )
    bred, growth = pl.pallas_call(
        write_kernel,
        out_shape=(
            jax.ShapeDtypeStruct((channels, rows, columns), f32),
            jax.ShapeDtypeStruct((1, regions), f32),
        ),
        in_specs=[resident, resident],
        out_specs=(anywhere, resident),
        scratch_shapes=[pltpu.SemaphoreType.DMA],
        compiler_params=pltpu.CompilerParams(vmem_limit_bytes=WRITE_BYTES),
    )(bred, growth_wide)
    return (bred[None], growth)


def solution(mesh):
    sizes = (mesh.shape["member"], mesh.shape["lon"], mesh.shape["lat"])
    return jax.shard_map(
        functools.partial(per_device, sizes),
        mesh=mesh,
        in_specs=(
            P("member", None, "lat", "lon"),
            P("lat", "lon"),
            P("lat", "lon"),
            P(None, "lat", "lon"),
            P("lat", "lon"),
            P("lat", "lon"),
            P(),
        ),
        out_specs=(P("member", None, "lat", "lon"), P("member", None)),
        check_vma=False,
    )
```

```python
import functools

import jax
import jax.numpy as jnp
from jax import lax
from jax.experimental import pallas as pl
from jax.experimental.pallas import tpu as pltpu
from jax.sharding import PartitionSpec as P

LEV = 5
STEPS = 2
MARGIN = 2 * STEPS
TILE = 8
LANES = 128
FIRST_ROWS = 4
PACK_AT = 4
PACK_STEPS = 2
PACK_TILES = 4
TAKE_FIRST = 3
MIDS_EARLY = 16
RIMS_EARLY = 11
KERNEL_BYTES = 56 * 2**20
WRITE_BYTES = 16 * 2**20

divergence_gain = 0.25
pressure_gain = 0.25
buoyancy_gain = 0.1
advection_gain = 0.05
epsilon = 1e-06

MESH = pl.DeviceIdType.MESH


def cycle_kernel(
    sizes,
    state_in, depth_in, rotation_in, diffusivity_in, mask_in, region_in, target_in,
    bred, growth_out,
    field, middle, surface_one, surface_two,
    own_mid, own_rim, control_mid, control_rim, lent_mid, lent_rim,
    send_east, send_west, from_east, from_west, send_north, send_south, from_north, from_south,
    mask, region, squares, lent_squares, counts, gathered, loan_out, loan, value, factor, target,
    in_sem, halo_send, halo_recv, pair_send, next_send, take_recv,
    lend_send, lend_recv, loan_send, loan_recv, sum_send, sum_recv, go,
    half_send, far_send, last_recv,
):
    members, lons, lats = sizes
    channels, rows, columns = state_in.shape
    regions = squares.shape[0]
    fields = field.shape[0]
    slots = columns // LANES
    halo = slots
    tiles = rows // TILE
    tall = rows + 2 * TILE
    clients = members - 2
    DEPTH, ROT, OCEAN, DIFF = channels, channels + 1, channels + 2, channels + 3
    mids = list(range(1, slots - 1))
    rims = [0, slots - 1]
    half = TILE // 2
    first_tiles = min(FIRST_ROWS, tiles)
    mids_early = min(MIDS_EARLY, tiles)
    rims_early = min(RIMS_EARLY, tiles - 1)
    split = channels // 2

    me = lax.axis_index("member")
    lon = lax.axis_index("lon")
    lat = lax.axis_index("lat")
    core = lax.rem(me, 2)
    client = me - 2

    down = 2 * lat >= lats
    has_north = lat < lats - 1
    has_south = lat > 0

    def tile_of(order):
        return jnp.where(down, tiles - 1 - order, order)

    def tall_of(order, back=False):
        return jnp.where(down ^ back, tiles + 1 - order, order)

    def at(dlat, dlon, member=None):
        return {
            "member": me if member is None else member,
            "lon": lax.rem(lon + dlon + lons, lons),
            "lat": lax.rem(lat + dlat + lats, lats),
        }

    def to_member(other):
        return {"member": other, "lon": lon, "lat": lat}

    even = core == 0
    has_pair = even & (me + 1 < members)
    has_next = even & (me + 2 < members)
    has_far = even & (me + 3 < members)
    parent = jnp.where(even, me - 2, me - 1)
    lender = 1
    peers = [(a, b) for a in range(lats) for b in range(lons) if (a, b) != (0, 0)]
    peers.sort(key=lambda p: -(p[0] + min(p[1], lons - p[1]) + p[1]))

    first_rows = first_tiles * TILE
    other_rows = rows - first_rows
    first_row = pl.multiple_of(jnp.where(down, rows - first_rows, 0), TILE)
    other_row = pl.multiple_of(jnp.where(down, 0, first_rows), TILE)

    def loads(index, row, count):
        src = pl.ds(row, count)
        dst = pl.ds(pl.multiple_of(row + TILE, TILE), count)
        copies = []
        for c in range(slots):
            part = slice(c * LANES, (c + 1) * LANES)
            copies += [
                (state_in.at[:, src, part], field.at[0:channels, c, dst, :]),
                (depth_in.at[src, part], field.at[DEPTH, c, dst, :]),
                (rotation_in.at[src, part], field.at[ROT, c, dst, :]),
                (diffusivity_in.at[:, src, part], field.at[DIFF:fields, c, dst, :]),
            ]
        copies.append((mask_in.at[src, :], mask.at[src, :]))
        return [pltpu.make_async_copy(a, b, in_sem.at[index]) for a, b in copies]

    def loaded(index, row, count):
        part = field.at[:, 0:slots, pl.ds(pl.multiple_of(row + TILE, TILE), count), :]
        pltpu.make_async_copy(part, part, in_sem.at[index]).wait()

    load_first = loads(0, first_row, first_rows)
    load_other = loads(1, other_row, other_rows) if other_rows else []
    load_region = pltpu.make_async_copy(region_in, region, in_sem.at[2])
    load_target = pltpu.make_async_copy(target_in, target, in_sem.at[3])
    for load in load_first + load_other + [load_region, load_target]:
        load.start()

    barrier = pltpu.get_barrier_semaphore()

    def greet(device):
        pl.semaphore_signal(barrier, inc=1, device_id=device, device_id_type=MESH)

    @pl.when(me == 0)
    def _():
        greet(to_member(1))
        for a, b in peers:
            greet(at(a, b, 1))

    @pl.when(me > 0)
    def _():
        for a, b in peers:
            greet(at(a, b))
        greet(to_member(parent))

    @pl.when(me == 1)
    def _():
        for other in range(2, members):
            greet(to_member(other))

    @pl.when(me > 1)
    def _():
        greet(to_member(lender))

    @pl.when((me > 1) & (core == 1))
    def _():
        greet(to_member(me - 3))

    @pl.when(me == 0)
    def _():
        pl.semaphore_wait(barrier, min(members - 1, 3))

    def all_here():
        @pl.when(me == 0)
        def _():
            pl.semaphore_wait(go, 1)

        @pl.when(me > 1)
        def _():
            pl.semaphore_wait(
                barrier,
                len(peers) + 1 + has_pair.astype(jnp.int32) + has_next.astype(jnp.int32)
                + has_far.astype(jnp.int32),
            )

    @pl.when(me == 1)
    def _():
        pl.semaphore_wait(barrier, 2 * len(peers) + 1 + clients)
        pl.semaphore_signal(go, inc=1, device_id=to_member(0), device_id_type=MESH)

    lane = lax.broadcasted_iota(jnp.int32, (TILE, LANES), 1)
    zero_tile = jnp.zeros((TILE, LANES), jnp.float32)
    low_lanes = lane < LANES // 2
    easterly = lax.rem(lane, 2 * MARGIN) >= MARGIN

    loaded(0, first_row, first_rows)

    def make_ocean(t, carry):
        r = pl.multiple_of(t * TILE, TILE)
        for c in range(slots):
            field[OCEAN, c, pl.ds(pl.multiple_of(r + TILE, TILE), TILE), :] = mask[
                pl.ds(r, TILE), c * LANES : (c + 1) * LANES
            ].astype(jnp.float32)
        return carry

    lax.fori_loop(first_row // TILE, first_row // TILE + first_tiles, make_ocean, 0)

    def remote(src, dst, index, device):
        return pltpu.make_async_remote_copy(
            src_ref=src, dst_ref=dst, send_sem=halo_send.at[index], recv_sem=halo_recv.at[index],
            device_id=device, device_id_type=MESH,
        )

    whole = slice(TILE, TILE + rows)
    last = slice(rows - TILE, rows)
    first = slice(0, TILE)
    above = slice(rows + TILE, rows + 2 * TILE)
    north = [
        remote(send_north, from_south, 0, at(1, 0)),
        remote(send_east.at[last], from_west.at[first], 4, at(1, 1)),
        remote(send_west.at[last], from_east.at[first], 5, at(1, -1)),
    ]
    south = [
        remote(send_south, from_north, 1, at(-1, 0)),
        remote(send_east.at[first], from_west.at[above], 6, at(-1, 1)),
        remote(send_west.at[first], from_east.at[above], 7, at(-1, -1)),
    ]
    sideways = [
        remote(send_east, from_west.at[whole], 2, at(0, 1)),
        remote(send_west, from_east.at[whole], 3, at(0, -1)),
    ]

    block = PACK_TILES if tiles % PACK_TILES == 0 else 1
    blocks = tiles // block

    def pack_block(b, carry):
        for i in range(block):
            r = pl.multiple_of((b * block + i) * TILE, TILE)
            now = pl.ds(pl.multiple_of(r + TILE, TILE), TILE)
            packed = [zero_tile] * 2
            for f in range(fields):
                g, s = divmod(f * 2 * MARGIN, LANES)
                edges = jnp.where(low_lanes, field[f, 0, now, :], field[f, slots - 1, now, :])
                here = (lane >= s) & (lane < s + 2 * MARGIN)
                packed[g] = jnp.where(here, pltpu.roll(edges, s + MARGIN, 1), packed[g])
            near, far = packed
            send_east[pl.ds(r, TILE), :] = jnp.where(easterly, pltpu.roll(far, MARGIN, 1), near)
            send_west[pl.ds(r, TILE), :] = jnp.where(easterly, near, pltpu.roll(far, LANES - MARGIN, 1))
        return carry

    def finish_loads():
        if other_rows:
            loaded(1, other_row, other_rows)
            lax.fori_loop(other_row // TILE, other_row // TILE + other_rows // TILE, make_ocean, 0)

    def pack_rows():
        for k in range(fields // 2):
            for c in range(slots):
                send_north[k, c, 0:half, :] = field[2 * k, c, rows + half : rows + TILE, :]
                send_north[k, c, half:TILE, :] = field[2 * k + 1, c, rows + half : rows + TILE, :]
                send_south[k, c, 0:half, :] = field[2 * k, c, TILE : TILE + half, :]
                send_south[k, c, half:TILE, :] = field[2 * k + 1, c, TILE : TILE + half, :]

    def send_halos():
        pack_rows()
        all_here()

        @pl.when(has_north)
        def _():
            for copy in north:
                copy.start()

        @pl.when(has_south)
        def _():
            for copy in south:
                copy.start()

        for copy in sideways:
            copy.start()

    def south_rows():
        @pl.when(has_south)
        def _():
            north[0].wait_recv()

        @pl.when(jnp.logical_not(has_south))
        def _():
            from_south[...] = jnp.zeros_like(from_south)

        for k in range(fields // 2):
            for c in range(slots):
                field[2 * k, c, half:TILE, :] = from_south[k, c, 0:half, :]
                field[2 * k + 1, c, half:TILE, :] = from_south[k, c, half:TILE, :]
                field[2 * k, c, 0:half, :] = from_south[k, c, 0:half, :]
                field[2 * k + 1, c, 0:half, :] = from_south[k, c, half:TILE, :]

    def north_rows():
        @pl.when(has_north)
        def _():
            south[0].wait_recv()

        @pl.when(jnp.logical_not(has_north))
        def _():
            from_north[...] = jnp.zeros_like(from_north)

        base = rows + TILE
        for k in range(fields // 2):
            for c in range(slots):
                field[2 * k, c, base : base + half, :] = from_north[k, c, 0:half, :]
                field[2 * k + 1, c, base : base + half, :] = from_north[k, c, half:TILE, :]
                field[2 * k, c, base + half : base + TILE, :] = from_north[k, c, 0:half, :]
                field[2 * k + 1, c, base + half : base + TILE, :] = from_north[k, c, half:TILE, :]

    def join_middle(order, back=False):
        now = pl.ds(pl.multiple_of(tall_of(order) * TILE, TILE), TILE)
        for f in range(fields):
            field[f, halo, now, :] = jnp.where(low_lanes, field[f, slots - 1, now, :], field[f, 0, now, :])

    def join_halo(order, back):
        now = pl.ds(pl.multiple_of(tall_of(order, back) * TILE, TILE), TILE)
        east, west = from_east[now, :], from_west[now, :]
        both = [
            jnp.where(easterly, east, west),
            jnp.where(easterly, pltpu.roll(east, MARGIN, 1), pltpu.roll(west, LANES - MARGIN, 1)),
        ]
        for f in range(fields):
            g, s = divmod(f * 2 * MARGIN, LANES)
            field[f, halo, now, :] = pltpu.roll(both[g], LANES - s - MARGIN, 1)

    class Ring:
        def __init__(self, ring, todo):
            self.todo = todo
            size = len(ring)
            place = {c: i for i, c in enumerate(ring)}
            self.east = {c: ring[(place[c] + 1) % size] for c in todo}
            self.west = {c: ring[(place[c] - 1) % size] for c in todo}
            self.used = sorted(set(todo) | set(self.east.values()) | set(self.west.values()))

        def sides(self, q):
            to_east = {c: pltpu.roll(q[c], LANES - 1, 1) for c in {*self.todo, *self.east.values()}}
            to_west = {c: pltpu.roll(q[c], 1, 1) for c in {*self.todo, *self.west.values()}}
            e = {c: jnp.where(lane == LANES - 1, to_east[self.east[c]], to_east[c]) for c in self.todo}
            w = {c: jnp.where(lane == 0, to_west[self.west[c]], to_west[c]) for c in self.todo}
            return e, w

    def surface_rows(src, dst, ring, r):
        now, above_r, below_r = pl.ds(r, TILE), pl.ds(r + 1, TILE), pl.ds(r - 1, TILE)

        def add_up(base, c, where):
            total = src[base, c, where, :]
            for k in range(1, LEV):
                total = total + src[base + k, c, where, :]
            return total

        e, w = ring.sides({c: add_up(1, c, now) for c in ring.used})
        for c in ring.todo:
            n, s = add_up(1 + LEV, c, above_r), add_up(1 + LEV, c, below_r)
            divergence = (e[c] - w[c]) + (n - s)
            dst[c, now, :] = field[OCEAN, c, now, :] * (
                src[0, c, now, :] - (divergence_gain / LEV) * field[DEPTH, c, now, :] * divergence
            )

    def update_rows(src, surface, ring, r, write):
        now, above_r, below_r = pl.ds(r, TILE), pl.ds(r + 1, TILE), pl.ds(r - 1, TILE)
        h = {c: surface[c, now, :] for c in ring.used}
        e, w = ring.sides(h)
        slope_east, slope_north = {}, {}
        for c in ring.todo:
            slope_east[c] = pressure_gain * (e[c] - w[c])
            slope_north[c] = pressure_gain * (surface[c, above_r, :] - surface[c, below_r, :])
            write(0, c, h[c])
        for k in range(LEV):
            iu, iv, ic = 1 + k, 1 + LEV + k, 1 + 2 * LEV + k
            u = {c: src[iu, c, now, :] for c in ring.used}
            v = {c: src[iv, c, now, :] for c in ring.used}
            t = {c: src[ic, c, now, :] for c in ring.used}
            ue, uw = ring.sides(u)
            ve, vw = ring.sides(v)
            te, tw = ring.sides(t)
            for c in ring.todo:
                ocean = field[OCEAN, c, now, :]
                rotation = field[ROT, c, now, :]
                mixing = field[DIFF + k, c, now, :]
                tn, ts = src[ic, c, above_r, :], src[ic, c, below_r, :]
                heat_east, heat_north = te[c] - tw[c], tn - ts
                around_u = (ue[c] + uw[c]) + (src[iu, c, above_r, :] + src[iu, c, below_r, :])
                around_v = (ve[c] + vw[c]) + (src[iv, c, above_r, :] + src[iv, c, below_r, :])
                around_t = (te[c] + tw[c]) + (tn + ts)
                new_u = ocean * (
                    u[c] + rotation * v[c] - slope_east[c] - buoyancy_gain * heat_east
                    + mixing * (around_u - 4.0 * u[c])
                )
                new_v = ocean * (
                    v[c] - rotation * u[c] - slope_north[c] - buoyancy_gain * heat_north
                    + mixing * (around_v - 4.0 * v[c])
                )
                new_t = ocean * (
                    t[c] + mixing * (around_t - 4.0 * t[c])
                    - advection_gain * (new_u * heat_east + new_v * heat_north)
                )
                write(iu, c, new_u)
                write(iv, c, new_v)
                write(ic, c, new_t)

    def run_pass(join, one, two, own, own_slots, at_order, leave, back=False):
        step = jnp.where(down ^ back, -1, 1)

        def body(i, carry):
            j = i - 1
            at_order(j)
            join(j + 2, back)
            r = jnp.where(down ^ back, rows - TILE * j, TILE + TILE * j)
            surface_rows(field, surface_one, one, r + 3 * step)
            r_one = r + 2 * step

            def middle_write(channel, c, new):
                middle[channel, c, pl.ds(r_one, TILE), :] = new

            update_rows(field, surface_one, one, r_one, middle_write)
            surface_rows(middle, surface_two, one, r + step)

            @pl.when(j >= 0)
            def _():
                order = jnp.where(back, tiles - 1 - j, j)
                t = tile_of(order)

                def last_write(channel, c, new):
                    own[t, channel, own_slots[c]] = new

                update_rows(
                    middle, surface_two, two, pl.multiple_of(r, TILE), last_write
                )
                leave(order, t)

            return carry

        lax.fori_loop(0, tiles + 1, body, 0)

    def pair_copy(ref, kind, t):
        return pltpu.make_async_remote_copy(
            src_ref=ref.at[t], dst_ref=ref.at[t],
            send_sem=pair_send.at[kind], recv_sem=take_recv.at[kind, t],
            device_id=to_member(me + 1), device_id_type=MESH,
        )

    def next_copy(ref, kind, t):
        return pltpu.make_async_remote_copy(
            src_ref=ref.at[t], dst_ref=ref.at[t],
            send_sem=next_send.at[kind], recv_sem=take_recv.at[kind, t],
            device_id=to_member(me + 2), device_id_type=MESH,
        )

    last_tile = tile_of(tiles - 1)

    def last_copy(begin, end, send, recv, other):
        part = control_rim.at[last_tile, begin:end]
        return pltpu.make_async_remote_copy(
            src_ref=part, dst_ref=part, send_sem=send, recv_sem=recv,
            device_id=to_member(other), device_id_type=MESH,
        )

    first_half = [0, split]
    second_half = [split, channels]

    def last_first(send, other):
        return last_copy(*first_half, send, take_recv.at[1, last_tile], other)

    def last_second(send, other):
        return last_copy(*second_half, send, last_recv, other)

    def send_second():
        @pl.when(has_next)
        def _():
            last_second(next_send.at[1], me + 2).start()

        @pl.when(has_far)
        def _():
            last_second(far_send, me + 3).start()

    def lend_copy(own, lent, kind, early, which, order):
        return pltpu.make_async_remote_copy(
            src_ref=own.at[tile_of(order)], dst_ref=lent.at[which, order - early],
            send_sem=lend_send.at[kind], recv_sem=lend_recv.at[kind, which],
            device_id=to_member(lender), device_id_type=MESH,
        )

    def lend_whole(own, lent, kind, early, which):
        return pltpu.make_async_remote_copy(
            src_ref=own.at[0 : tiles - early], dst_ref=lent.at[which, 0 : tiles - early],
            send_sem=lend_send.at[kind], recv_sem=lend_recv.at[kind, which],
            device_id=to_member(lender), device_id_type=MESH,
        )

    def leave_mid(order, t):
        @pl.when(me == 0)
        def _():
            for k in range(channels):
                for n in range(len(mids)):
                    control_mid[t, k, n] = own_mid[t, k, n]
            pair_copy(control_mid, 0, t).start()

            @pl.when(has_next & (order < mids_early))
            def _():
                next_copy(control_mid, 0, t).start()

        @pl.when((me > 1) & (order >= mids_early))
        def _():
            lend_copy(own_mid, lent_mid, 0, mids_early, client, order).start()

    def leave_rim(order, t):
        @pl.when(me == 0)
        def _():
            for k in range(channels):
                for n in range(len(rims)):
                    control_rim[t, k, n] = own_rim[t, k, n]
            pair_copy(control_rim, 1, t).start()

            @pl.when(has_next & (order < tiles - 1))
            def _():
                next_copy(control_rim, 1, t).start()

            @pl.when(order == tiles - 1)
            def _():
                @pl.when(has_next)
                def _():
                    last_first(next_send.at[1], me + 2).start()

                send_second()

        @pl.when((me > 1) & (order >= rims_early))
        def _():
            lend_copy(own_rim, lent_rim, 1, rims_early, client, order).start()

    def start_rows():
        @pl.when(down)
        def _():
            north_rows()

        @pl.when(jnp.logical_not(down))
        def _():
            south_rows()

    def end_rows():
        @pl.when(down)
        def _():
            south_rows()

        @pl.when(jnp.logical_not(down))
        def _():
            north_rows()

    load_at = min(first_tiles - 1, tiles - 1)
    per = -(-blocks // PACK_STEPS)
    pack_at = max(load_at, PACK_AT)
    send_at = pack_at + PACK_STEPS
    ahead = lats > 2 or send_at > tiles - 2

    def events_mid(j):
        if not ahead:
            @pl.when(j == load_at)
            def _():
                finish_loads()

            @pl.when((j >= pack_at) & (j < send_at))
            def _():
                begin = (j - pack_at) * per
                lax.fori_loop(begin, jnp.minimum(begin + per, blocks), pack_block, 0)

            @pl.when(j == send_at)
            def _():
                send_halos()

        @pl.when(j == tiles - 1)
        def _():
            end_rows()

    if ahead:
        finish_loads()
        lax.fori_loop(0, blocks, pack_block, 0)
        send_halos()
    start_rows()
    join_middle(0)
    ring_mid = mids + [halo]
    run_pass(
        join_middle, Ring(ring_mid, ring_mid), Ring(ring_mid, mids),
        own_mid, {c: n for n, c in enumerate(mids)}, events_mid, leave_mid,
    )

    for copy in sideways:
        copy.wait_recv()

    @pl.when(has_north)
    def _():
        for copy in south[1:]:
            copy.wait_recv()

    @pl.when(has_south)
    def _():
        for copy in north[1:]:
            copy.wait_recv()

    @pl.when(jnp.logical_not(has_north))
    def _():
        from_east[above, :] = zero_tile
        from_west[above, :] = zero_tile

    @pl.when(jnp.logical_not(has_south))
    def _():
        from_east[first, :] = zero_tile
        from_west[first, :] = zero_tile

    back = me > 1
    join_halo(0, back)
    ring_all = list(range(slots)) + [halo]
    run_pass(
        join_halo, Ring(ring_all, [slots - 1, halo, 0]), Ring(ring_all, rims),
        own_rim, {c: n for n, c in enumerate(rims)}, lambda j: None, leave_rim, back,
    )

    @pl.when((me == 0) & has_next)
    def _():
        def body(order, carry):
            next_copy(control_mid, 0, tile_of(order)).start()
            return carry

        lax.fori_loop(mids_early, tiles, body, 0)

    def clear(ref):
        for k in range(regions):
            ref[k] = zero_tile

    def ids_at(t, c):
        return region[pl.ds(pl.multiple_of(t * TILE, TILE), TILE), c * LANES : (c + 1) * LANES]

    def ocean_at(t, c):
        return field[OCEAN, c, pl.ds(pl.multiple_of(t * TILE + TILE, TILE), TILE), :]

    def add_regions(ref, items):
        for k in range(regions):
            total = ref[k]
            for ids, amount in items:
                total = total + jnp.where(ids == k, amount, 0.0)
            ref[k] = total

    def compare(ref, mine, its, t, part):
        items = []
        for n, c in enumerate(part):
            total = None
            for k in range(channels):
                d = mine(k, n) - its(k, n)
                total = d * d if total is None else total + d * d
            items.append((ids_at(t, c), ocean_at(t, c) * total))
        add_regions(ref, items)

    def share(which):
        for p, (a, b) in enumerate(peers):
            pltpu.make_async_remote_copy(
                src_ref=gathered.at[which, 0], dst_ref=gathered.at[which, p + 1],
                send_sem=sum_send.at[which], recv_sem=sum_recv.at[which],
                device_id=at(a, b), device_id_type=MESH,
            ).start()

    def collect(which):
        others = gathered.at[which, 1 : len(peers) + 1]
        pltpu.make_async_remote_copy(
            src_ref=others, dst_ref=others, send_sem=sum_send.at[which], recv_sem=sum_recv.at[which],
            device_id=at(*peers[0]), device_id_type=MESH,
        ).wait()
        total = gathered[which, 0]
        for p in range(len(peers)):
            total = total + gathered[which, p + 1]
        return jnp.sum(total, axis=1, keepdims=True)

    load_region.wait()
    clear(squares)
    clear(counts)

    def count(t, carry):
        add_regions(counts, [(ids_at(t, c), ocean_at(t, c)) for c in range(slots)])
        return carry

    lax.fori_loop(0, tiles, count, 0)
    gathered[0, 0] = jnp.sum(counts[...], axis=1)
    share(0)

    kinds = [
        (0, own_mid, control_mid, lent_mid, mids, mids_early),
        (1, own_rim, control_rim, lent_rim, rims, rims_early),
    ]

    def take(kind, order):
        _, own, control, _, part, _ = kinds[kind]
        t = tile_of(order)

        @pl.when(even)
        def _():
            next_copy(control, kind, t).wait_recv()

            @pl.when(has_pair)
            def _():
                pair_copy(control, kind, t).start()

            @pl.when(has_next)
            def _():
                next_copy(control, kind, t).start()

        @pl.when(jnp.logical_not(even))
        def _():
            pair_copy(control, kind, t).wait_recv()

    def weigh(kind, order):
        _, own, control, _, part, _ = kinds[kind]
        t = tile_of(order)
        compare(squares, lambda k, n: own[t, k, n], lambda k, n: control[t, k, n], t, part)

    def loop(begin, end, *actions):
        def body(order, carry):
            for action in actions:
                action(order)
            return carry

        lax.fori_loop(begin, end, body, 0)

    @pl.when(me > 0)
    def _():
        late_mids = jnp.where(me == 1, tiles, mids_early)
        late_rims = jnp.where(me == 1, tiles, rims_early)
        loop(0, mids_early, lambda o: take(0, o), lambda o: weigh(0, o))
        loop(0, late_rims, lambda o: take(1, o), lambda o: weigh(1, o))
        loop(mids_early, late_mids, lambda o: take(0, o), lambda o: weigh(0, o))

    def loan_copy(other, which):
        return pltpu.make_async_remote_copy(
            src_ref=loan_out.at[which], dst_ref=loan,
            send_sem=loan_send.at[which], recv_sem=loan_recv,
            device_id=to_member(other), device_id_type=MESH,
        )

    def lend(which, other):
        clear(lent_squares)
        for kind, own, control, lent, part, early in kinds:
            if early == tiles:
                continue

            def body(order, carry):
                t = tile_of(order)
                compare(
                    lent_squares,
                    lambda k, n: lent[which, order - early, k, n],
                    lambda k, n: control[t, k, n], t, part,
                )
                return carry

            lend_whole(own, lent, kind, early, which).wait_recv()
            lax.fori_loop(early, tiles, body, 0)
        loan_out[which] = jnp.sum(lent_squares[...], axis=1)
        loan_copy(other, which).start()

    gathered[1, 0] = jnp.sum(squares[...], axis=1)

    @pl.when(me == 1)
    def _():
        for which in range(clients):
            lend(which, which + 2)

    @pl.when(me > 1)
    def _():
        loan_copy(me, 0).wait_recv()
        gathered[1, 0] = gathered[1, 0] + loan[...]

    share(1)
    taken = min(rims_early + TAKE_FIRST, tiles - 1)

    @pl.when(me > 1)
    def _():
        loop(rims_early, taken, lambda o: take(1, o))

    count_sum = collect(0)
    square_sum = collect(1)
    growth = jnp.sqrt(square_sum / (count_sum * channels) + epsilon)
    growth_wide = jnp.broadcast_to(growth, (regions, LANES))
    growth_out[...] = growth_wide
    load_target.wait()
    for k in range(regions):
        value[k] = jnp.broadcast_to(target[k] / growth_wide[k : k + 1, :], (TILE, LANES))

    def make_factor(b, carry):
        for i in range(block):
            t = b * block + i
            for c in range(slots):
                ids = ids_at(t, c)
                total = zero_tile
                for k in range(regions):
                    total = jnp.where(ids == k, value[k], total)
                factor[t, c] = total
        return carry

    lax.fori_loop(0, blocks, make_factor, 0)

    def breed(kind, order):
        _, own, control, _, part, _ = kinds[kind]
        t = tile_of(order)
        now = pl.ds(pl.multiple_of(t * TILE, TILE), TILE)
        for n, c in enumerate(part):
            scale = factor[t, c]
            for k in range(channels):
                base = control[t, k, n]
                bred[k, now, c * LANES : (c + 1) * LANES] = base + scale * (own[t, k, n] - base)

    def take_late(kind, order):
        @pl.when(me > 1)
        def _():
            take(kind, order)

    loop(0, mids_early, lambda o: breed(0, o))
    loop(0, rims_early, lambda o: breed(1, o))
    loop(rims_early, taken, lambda o: breed(1, o))
    loop(taken, tiles - 1, lambda o: take_late(1, o), lambda o: breed(1, o))

    @pl.when(me > 1)
    def _():
        last_first(half_send, me).wait_recv()

        @pl.when(has_pair)
        def _():
            last_first(half_send, me + 1).start()

        @pl.when(has_next)
        def _():
            last_first(next_send.at[1], me + 2).start()

        last_second(far_send, me).wait_recv()
        send_second()

    breed(1, tiles - 1)
    loop(mids_early, tiles, lambda o: take_late(0, o), lambda o: breed(0, o))

    for copy in sideways:
        copy.wait_send()

    @pl.when(has_north)
    def _():
        for copy in north:
            copy.wait_send()

    @pl.when(has_south)
    def _():
        for copy in south:
            copy.wait_send()

    for kind, own, control, lent, part, early in kinds:
        def whole_control(send, other, part=control):
            return pltpu.make_async_remote_copy(
                src_ref=part, dst_ref=part, send_sem=send.at[kind], recv_sem=take_recv.at[kind, 0],
                device_id=to_member(other), device_id_type=MESH,
            )

        @pl.when(me == 0)
        def _():
            whole_control(pair_send, 1).wait_send()

        @pl.when(has_pair & (me > 1))
        def _():
            if kind == 0:
                whole_control(pair_send, me + 1).wait_send()
            else:
                whole_control(pair_send, me + 1, control.at[0 : tiles - 1]).wait_send()
                last_first(half_send, me + 1).wait_send()

        @pl.when(has_next)
        def _():
            whole_control(next_send, me + 2).wait_send()

    @pl.when(has_far)
    def _():
        last_second(far_send, me + 3).wait_send()

    @pl.when(me == 1)
    def _():
        for which in range(clients):
            loan_copy(which + 2, which).wait_send()

    @pl.when(me > 1)
    def _():
        for kind, own, control, lent, part, early in kinds:
            if early < tiles:
                lend_whole(own, lent, kind, early, client).wait_send()


def write_kernel(bred_in, growth_in, bred, growth, out_sem):
    copy = pltpu.make_async_copy(bred_in, bred, out_sem)
    copy.start()
    shape = growth_in.shape
    diagonal = lax.broadcasted_iota(jnp.int32, shape, 0) == lax.broadcasted_iota(jnp.int32, shape, 1)
    line = jnp.sum(jnp.where(diagonal, growth_in[...], 0.0), axis=0, keepdims=True)
    growth[...] = line[:, 0 : growth.shape[1]]
    copy.wait()


def per_device(
    sizes, member_state, column_depth, rotation, diffusivity, ocean_mask, region_id, target_rms
):
    members, lons, lats = sizes
    _, channels, rows, columns = member_state.shape
    regions = target_rms.shape[0]
    fields = channels + 3 + LEV
    tall = rows + 2 * TILE
    tiles = rows // TILE
    slots = columns // LANES
    group = lons * lats
    clients = max(members - 2, 1)
    late_mids = max(tiles - MIDS_EARLY, 1)
    late_rims = max(tiles - RIMS_EARLY, 1)
    f32 = jnp.float32
    anywhere = pl.BlockSpec(memory_space=pl.ANY)
    resident = pl.BlockSpec(memory_space=pltpu.VMEM)
    piece_mid = (channels, slots - 2, TILE, LANES)
    piece_rim = (channels, 2, TILE, LANES)
    bred, growth_wide = pl.pallas_call(
        functools.partial(cycle_kernel, sizes),
        out_shape=(
            pltpu.VMEM((channels, rows, columns), f32),
            pltpu.VMEM((regions, LANES), f32),
        ),
        in_specs=[anywhere] * 7,
        out_specs=(resident,) * 2,
        scratch_shapes=[
            pltpu.VMEM((fields, slots + 1, tall, LANES), f32),
            pltpu.VMEM((channels, slots + 1, tall, LANES), f32),
            pltpu.VMEM((slots + 1, tall, LANES), f32),
            pltpu.VMEM((slots + 1, tall, LANES), f32),
            pltpu.VMEM((tiles,) + piece_mid, f32),
            pltpu.VMEM((tiles,) + piece_rim, f32),
            pltpu.VMEM((tiles,) + piece_mid, f32),
            pltpu.VMEM((tiles,) + piece_rim, f32),
            pltpu.VMEM((clients, late_mids) + piece_mid, f32),
            pltpu.VMEM((clients, late_rims) + piece_rim, f32),
            pltpu.VMEM((rows, LANES), f32),
            pltpu.VMEM((rows, LANES), f32),
            pltpu.VMEM((tall, LANES), f32),
            pltpu.VMEM((tall, LANES), f32),
            pltpu.VMEM((fields // 2, slots, TILE, LANES), f32),
            pltpu.VMEM((fields // 2, slots, TILE, LANES), f32),
            pltpu.VMEM((fields // 2, slots, TILE, LANES), f32),
            pltpu.VMEM((fields // 2, slots, TILE, LANES), f32),
            pltpu.VMEM((rows, columns), jnp.int32),
            pltpu.VMEM((rows, columns), jnp.int32),
            pltpu.VMEM((regions, TILE, LANES), f32),
            pltpu.VMEM((regions, TILE, LANES), f32),
            pltpu.VMEM((regions, TILE, LANES), f32),
            pltpu.VMEM((2, group, regions, LANES), f32),
            pltpu.VMEM((clients, regions, LANES), f32),
            pltpu.VMEM((regions, LANES), f32),
            pltpu.VMEM((regions, TILE, LANES), f32),
            pltpu.VMEM((tiles, slots, TILE, LANES), f32),
            pltpu.SMEM((regions,), f32),
            pltpu.SemaphoreType.DMA((4,)),
            pltpu.SemaphoreType.DMA((8,)),
            pltpu.SemaphoreType.DMA((8,)),
            pltpu.SemaphoreType.DMA((2,)),
            pltpu.SemaphoreType.DMA((2,)),
            pltpu.SemaphoreType.DMA((2, tiles)),
            pltpu.SemaphoreType.DMA((2,)),
            pltpu.SemaphoreType.DMA((2, clients)),
            pltpu.SemaphoreType.DMA((clients,)),
            pltpu.SemaphoreType.DMA,
            pltpu.SemaphoreType.DMA((2,)),
            pltpu.SemaphoreType.DMA((2,)),
            pltpu.SemaphoreType.REGULAR,
            pltpu.SemaphoreType.DMA,
            pltpu.SemaphoreType.DMA,
            pltpu.SemaphoreType.DMA,
        ],
        compiler_params=pltpu.CompilerParams(
            collective_id=0, has_side_effects=True, vmem_limit_bytes=KERNEL_BYTES
        ),
    )(
        member_state.reshape(channels, rows, columns),
        column_depth, rotation, diffusivity, ocean_mask, region_id, target_rms,
    )
    bred, growth = pl.pallas_call(
        write_kernel,
        out_shape=(
            jax.ShapeDtypeStruct((channels, rows, columns), f32),
            jax.ShapeDtypeStruct((1, regions), f32),
        ),
        in_specs=[resident, resident],
        out_specs=(anywhere, resident),
        scratch_shapes=[pltpu.SemaphoreType.DMA],
        compiler_params=pltpu.CompilerParams(vmem_limit_bytes=WRITE_BYTES),
    )(bred, growth_wide)
    return (bred[None], growth)


def solution(mesh):
    sizes = (mesh.shape["member"], mesh.shape["lon"], mesh.shape["lat"])
    return jax.shard_map(
        functools.partial(per_device, sizes),
        mesh=mesh,
        in_specs=(
            P("member", None, "lat", "lon"),
            P("lat", "lon"),
            P("lat", "lon"),
            P(None, "lat", "lon"),
            P("lat", "lon"),
            P("lat", "lon"),
            P(),
        ),
        out_specs=(P("member", None, "lat", "lon"), P("member", None)),
        check_vma=False,
    )
```

```python
import functools

import jax
import jax.numpy as jnp
from jax import lax
from jax.experimental import pallas as pl
from jax.experimental.pallas import tpu as pltpu
from jax.sharding import PartitionSpec as P

LEV = 5
STEPS = 2
MARGIN = 2 * STEPS
TILE = 8
LANES = 128
FIRST_ROWS = 4
PACK_AT = 4
PACK_STEPS = 2
PACK_TILES = 4
TAKE_FIRST = 2
MIDS_EARLY = 15
RIMS_EARLY = 11
KERNEL_BYTES = 56 * 2**20
WRITE_BYTES = 16 * 2**20

divergence_gain = 0.25
pressure_gain = 0.25
buoyancy_gain = 0.1
advection_gain = 0.05
epsilon = 1e-06

MESH = pl.DeviceIdType.MESH


def cycle_kernel(
    sizes,
    state_in, depth_in, rotation_in, diffusivity_in, mask_in, region_in, target_in,
    bred, growth_out,
    field, middle, surface_one, surface_two,
    own_mid, own_rim, control_mid, control_rim, lent_mid, lent_rim,
    send_east, send_west, from_east, from_west, send_north, send_south, from_north, from_south,
    mask, region, squares, lent_squares, counts, gathered, loan_out, loan, value, factor, target,
    in_sem, halo_send, halo_recv, pair_send, next_send, take_recv,
    lend_send, lend_recv, loan_send, loan_recv, sum_send, sum_recv, go,
    half_send, far_send, last_recv,
):
    members, lons, lats = sizes
    channels, rows, columns = state_in.shape
    regions = squares.shape[0]
    fields = field.shape[0]
    slots = columns // LANES
    halo = slots
    tiles = rows // TILE
    tall = rows + 2 * TILE
    clients = members - 2
    DEPTH, ROT, OCEAN, DIFF = channels, channels + 1, channels + 2, channels + 3
    mids = list(range(1, slots - 1))
    rims = [0, slots - 1]
    half = TILE // 2
    first_tiles = min(FIRST_ROWS, tiles)
    mids_early = min(MIDS_EARLY, tiles)
    rims_early = min(RIMS_EARLY, tiles - 1)
    split = channels // 2

    me = lax.axis_index("member")
    lon = lax.axis_index("lon")
    lat = lax.axis_index("lat")
    core = lax.rem(me, 2)
    client = me - 2

    down = 2 * lat >= lats
    has_north = lat < lats - 1
    has_south = lat > 0

    def tile_of(order):
        return jnp.where(down, tiles - 1 - order, order)

    def tall_of(order, back=False):
        return jnp.where(down ^ back, tiles + 1 - order, order)

    def at(dlat, dlon, member=None):
        return {
            "member": me if member is None else member,
            "lon": lax.rem(lon + dlon + lons, lons),
            "lat": lax.rem(lat + dlat + lats, lats),
        }

    def to_member(other):
        return {"member": other, "lon": lon, "lat": lat}

    even = core == 0
    has_pair = even & (me + 1 < members)
    has_next = even & (me + 2 < members)
    has_far = even & (me + 3 < members)
    late_here = 2 * lon >= lons
    mids_cut = jnp.where(late_here, mids_early, tiles)
    parent = jnp.where(even, me - 2, me - 1)
    lender = 1
    peers = [(a, b) for a in range(lats) for b in range(lons) if (a, b) != (0, 0)]
    peers.sort(key=lambda p: -(p[0] + min(p[1], lons - p[1]) + p[1]))

    first_rows = first_tiles * TILE
    other_rows = rows - first_rows
    first_row = pl.multiple_of(jnp.where(down, rows - first_rows, 0), TILE)
    other_row = pl.multiple_of(jnp.where(down, 0, first_rows), TILE)

    def loads(index, row, count):
        src = pl.ds(row, count)
        dst = pl.ds(pl.multiple_of(row + TILE, TILE), count)
        copies = []
        for c in range(slots):
            part = slice(c * LANES, (c + 1) * LANES)
            copies += [
                (state_in.at[:, src, part], field.at[0:channels, c, dst, :]),
                (depth_in.at[src, part], field.at[DEPTH, c, dst, :]),
                (rotation_in.at[src, part], field.at[ROT, c, dst, :]),
                (diffusivity_in.at[:, src, part], field.at[DIFF:fields, c, dst, :]),
            ]
        copies.append((mask_in.at[src, :], mask.at[src, :]))
        return [pltpu.make_async_copy(a, b, in_sem.at[index]) for a, b in copies]

    def loaded(index, row, count):
        part = field.at[:, 0:slots, pl.ds(pl.multiple_of(row + TILE, TILE), count), :]
        pltpu.make_async_copy(part, part, in_sem.at[index]).wait()

    load_first = loads(0, first_row, first_rows)
    load_other = loads(1, other_row, other_rows) if other_rows else []
    load_region = pltpu.make_async_copy(region_in, region, in_sem.at[2])
    load_target = pltpu.make_async_copy(target_in, target, in_sem.at[3])
    for load in load_first + load_other + [load_region, load_target]:
        load.start()

    barrier = pltpu.get_barrier_semaphore()

    def greet(device):
        pl.semaphore_signal(barrier, inc=1, device_id=device, device_id_type=MESH)

    @pl.when(me == 0)
    def _():
        greet(to_member(1))
        for a, b in peers:
            greet(at(a, b, 1))

    @pl.when(me > 0)
    def _():
        for a, b in peers:
            greet(at(a, b))
        greet(to_member(parent))

    @pl.when(me == 1)
    def _():
        for other in range(2, members):
            greet(to_member(other))

    @pl.when(me > 1)
    def _():
        greet(to_member(lender))

    @pl.when((me > 1) & (core == 1))
    def _():
        greet(to_member(me - 3))

    @pl.when(me == 0)
    def _():
        pl.semaphore_wait(barrier, min(members - 1, 3))

    def all_here():
        @pl.when(me == 0)
        def _():
            pl.semaphore_wait(go, 1)

        @pl.when(me > 1)
        def _():
            pl.semaphore_wait(
                barrier,
                len(peers) + 1 + has_pair.astype(jnp.int32) + has_next.astype(jnp.int32)
                + has_far.astype(jnp.int32),
            )

    @pl.when(me == 1)
    def _():
        pl.semaphore_wait(barrier, 2 * len(peers) + 1 + clients)
        pl.semaphore_signal(go, inc=1, device_id=to_member(0), device_id_type=MESH)

    lane = lax.broadcasted_iota(jnp.int32, (TILE, LANES), 1)
    zero_tile = jnp.zeros((TILE, LANES), jnp.float32)
    low_lanes = lane < LANES // 2
    easterly = lax.rem(lane, 2 * MARGIN) >= MARGIN

    loaded(0, first_row, first_rows)

    def make_ocean(t, carry):
        r = pl.multiple_of(t * TILE, TILE)
        for c in range(slots):
            field[OCEAN, c, pl.ds(pl.multiple_of(r + TILE, TILE), TILE), :] = mask[
                pl.ds(r, TILE), c * LANES : (c + 1) * LANES
            ].astype(jnp.float32)
        return carry

    lax.fori_loop(first_row // TILE, first_row // TILE + first_tiles, make_ocean, 0)

    def remote(src, dst, index, device):
        return pltpu.make_async_remote_copy(
            src_ref=src, dst_ref=dst, send_sem=halo_send.at[index], recv_sem=halo_recv.at[index],
            device_id=device, device_id_type=MESH,
        )

    whole = slice(TILE, TILE + rows)
    last = slice(rows - TILE, rows)
    first = slice(0, TILE)
    above = slice(rows + TILE, rows + 2 * TILE)
    north = [
        remote(send_north, from_south, 0, at(1, 0)),
        remote(send_east.at[last], from_west.at[first], 4, at(1, 1)),
        remote(send_west.at[last], from_east.at[first], 5, at(1, -1)),
    ]
    south = [
        remote(send_south, from_north, 1, at(-1, 0)),
        remote(send_east.at[first], from_west.at[above], 6, at(-1, 1)),
        remote(send_west.at[first], from_east.at[above], 7, at(-1, -1)),
    ]
    sideways = [
        remote(send_east, from_west.at[whole], 2, at(0, 1)),
        remote(send_west, from_east.at[whole], 3, at(0, -1)),
    ]

    block = PACK_TILES if tiles % PACK_TILES == 0 else 1
    blocks = tiles // block

    def pack_block(b, carry):
        for i in range(block):
            r = pl.multiple_of((b * block + i) * TILE, TILE)
            now = pl.ds(pl.multiple_of(r + TILE, TILE), TILE)
            packed = [zero_tile] * 2
            for f in range(fields):
                g, s = divmod(f * 2 * MARGIN, LANES)
                edges = jnp.where(low_lanes, field[f, 0, now, :], field[f, slots - 1, now, :])
                here = (lane >= s) & (lane < s + 2 * MARGIN)
                packed[g] = jnp.where(here, pltpu.roll(edges, s + MARGIN, 1), packed[g])
            near, far = packed
            send_east[pl.ds(r, TILE), :] = jnp.where(easterly, pltpu.roll(far, MARGIN, 1), near)
            send_west[pl.ds(r, TILE), :] = jnp.where(easterly, near, pltpu.roll(far, LANES - MARGIN, 1))
        return carry

    def finish_loads():
        if other_rows:
            loaded(1, other_row, other_rows)
            lax.fori_loop(other_row // TILE, other_row // TILE + other_rows // TILE, make_ocean, 0)

    def pack_rows():
        for k in range(fields // 2):
            for c in range(slots):
                send_north[k, c, 0:half, :] = field[2 * k, c, rows + half : rows + TILE, :]
                send_north[k, c, half:TILE, :] = field[2 * k + 1, c, rows + half : rows + TILE, :]
                send_south[k, c, 0:half, :] = field[2 * k, c, TILE : TILE + half, :]
                send_south[k, c, half:TILE, :] = field[2 * k + 1, c, TILE : TILE + half, :]

    def send_halos():
        pack_rows()
        all_here()

        @pl.when(has_north)
        def _():
            for copy in north:
                copy.start()

        @pl.when(has_south)
        def _():
            for copy in south:
                copy.start()

        for copy in sideways:
            copy.start()

    def south_rows():
        @pl.when(has_south)
        def _():
            north[0].wait_recv()

        @pl.when(jnp.logical_not(has_south))
        def _():
            from_south[...] = jnp.zeros_like(from_south)

        for k in range(fields // 2):
            for c in range(slots):
                field[2 * k, c, half:TILE, :] = from_south[k, c, 0:half, :]
                field[2 * k + 1, c, half:TILE, :] = from_south[k, c, half:TILE, :]
                field[2 * k, c, 0:half, :] = from_south[k, c, 0:half, :]
                field[2 * k + 1, c, 0:half, :] = from_south[k, c, half:TILE, :]

    def north_rows():
        @pl.when(has_north)
        def _():
            south[0].wait_recv()

        @pl.when(jnp.logical_not(has_north))
        def _():
            from_north[...] = jnp.zeros_like(from_north)

        base = rows + TILE
        for k in range(fields // 2):
            for c in range(slots):
                field[2 * k, c, base : base + half, :] = from_north[k, c, 0:half, :]
                field[2 * k + 1, c, base : base + half, :] = from_north[k, c, half:TILE, :]
                field[2 * k, c, base + half : base + TILE, :] = from_north[k, c, 0:half, :]
                field[2 * k + 1, c, base + half : base + TILE, :] = from_north[k, c, half:TILE, :]

    def join_middle(order, back=False):
        now = pl.ds(pl.multiple_of(tall_of(order) * TILE, TILE), TILE)
        for f in range(fields):
            field[f, halo, now, :] = jnp.where(low_lanes, field[f, slots - 1, now, :], field[f, 0, now, :])

    def join_halo(order, back):
        now = pl.ds(pl.multiple_of(tall_of(order, back) * TILE, TILE), TILE)
        east, west = from_east[now, :], from_west[now, :]
        both = [
            jnp.where(easterly, east, west),
            jnp.where(easterly, pltpu.roll(east, MARGIN, 1), pltpu.roll(west, LANES - MARGIN, 1)),
        ]
        for f in range(fields):
            g, s = divmod(f * 2 * MARGIN, LANES)
            field[f, halo, now, :] = pltpu.roll(both[g], LANES - s - MARGIN, 1)

    class Ring:
        def __init__(self, ring, todo):
            self.todo = todo
            size = len(ring)
            place = {c: i for i, c in enumerate(ring)}
            self.east = {c: ring[(place[c] + 1) % size] for c in todo}
            self.west = {c: ring[(place[c] - 1) % size] for c in todo}
            self.used = sorted(set(todo) | set(self.east.values()) | set(self.west.values()))

        def sides(self, q):
            to_east = {c: pltpu.roll(q[c], LANES - 1, 1) for c in {*self.todo, *self.east.values()}}
            to_west = {c: pltpu.roll(q[c], 1, 1) for c in {*self.todo, *self.west.values()}}
            e = {c: jnp.where(lane == LANES - 1, to_east[self.east[c]], to_east[c]) for c in self.todo}
            w = {c: jnp.where(lane == 0, to_west[self.west[c]], to_west[c]) for c in self.todo}
            return e, w

    def surface_rows(src, dst, ring, r):
        now, above_r, below_r = pl.ds(r, TILE), pl.ds(r + 1, TILE), pl.ds(r - 1, TILE)

        def add_up(base, c, where):
            total = src[base, c, where, :]
            for k in range(1, LEV):
                total = total + src[base + k, c, where, :]
            return total

        e, w = ring.sides({c: add_up(1, c, now) for c in ring.used})
        for c in ring.todo:
            n, s = add_up(1 + LEV, c, above_r), add_up(1 + LEV, c, below_r)
            divergence = (e[c] - w[c]) + (n - s)
            dst[c, now, :] = field[OCEAN, c, now, :] * (
                src[0, c, now, :] - (divergence_gain / LEV) * field[DEPTH, c, now, :] * divergence
            )

    def update_rows(src, surface, ring, r, write):
        now, above_r, below_r = pl.ds(r, TILE), pl.ds(r + 1, TILE), pl.ds(r - 1, TILE)
        h = {c: surface[c, now, :] for c in ring.used}
        e, w = ring.sides(h)
        slope_east, slope_north = {}, {}
        for c in ring.todo:
            slope_east[c] = pressure_gain * (e[c] - w[c])
            slope_north[c] = pressure_gain * (surface[c, above_r, :] - surface[c, below_r, :])
            write(0, c, h[c])
        for k in range(LEV):
            iu, iv, ic = 1 + k, 1 + LEV + k, 1 + 2 * LEV + k
            u = {c: src[iu, c, now, :] for c in ring.used}
            v = {c: src[iv, c, now, :] for c in ring.used}
            t = {c: src[ic, c, now, :] for c in ring.used}
            ue, uw = ring.sides(u)
            ve, vw = ring.sides(v)
            te, tw = ring.sides(t)
            for c in ring.todo:
                ocean = field[OCEAN, c, now, :]
                rotation = field[ROT, c, now, :]
                mixing = field[DIFF + k, c, now, :]
                tn, ts = src[ic, c, above_r, :], src[ic, c, below_r, :]
                heat_east, heat_north = te[c] - tw[c], tn - ts
                around_u = (ue[c] + uw[c]) + (src[iu, c, above_r, :] + src[iu, c, below_r, :])
                around_v = (ve[c] + vw[c]) + (src[iv, c, above_r, :] + src[iv, c, below_r, :])
                around_t = (te[c] + tw[c]) + (tn + ts)
                new_u = ocean * (
                    u[c] + rotation * v[c] - slope_east[c] - buoyancy_gain * heat_east
                    + mixing * (around_u - 4.0 * u[c])
                )
                new_v = ocean * (
                    v[c] - rotation * u[c] - slope_north[c] - buoyancy_gain * heat_north
                    + mixing * (around_v - 4.0 * v[c])
                )
                new_t = ocean * (
                    t[c] + mixing * (around_t - 4.0 * t[c])
                    - advection_gain * (new_u * heat_east + new_v * heat_north)
                )
                write(iu, c, new_u)
                write(iv, c, new_v)
                write(ic, c, new_t)

    def run_pass(join, one, two, own, own_slots, at_order, leave, back=False):
        step = jnp.where(down ^ back, -1, 1)

        def body(i, carry):
            j = i - 1
            at_order(j)
            join(j + 2, back)
            r = jnp.where(down ^ back, rows - TILE * j, TILE + TILE * j)
            surface_rows(field, surface_one, one, r + 3 * step)
            r_one = r + 2 * step

            def middle_write(channel, c, new):
                middle[channel, c, pl.ds(r_one, TILE), :] = new

            update_rows(field, surface_one, one, r_one, middle_write)
            surface_rows(middle, surface_two, one, r + step)

            @pl.when(j >= 0)
            def _():
                order = jnp.where(back, tiles - 1 - j, j)
                t = tile_of(order)

                def last_write(channel, c, new):
                    own[t, channel, own_slots[c]] = new

                update_rows(
                    middle, surface_two, two, pl.multiple_of(r, TILE), last_write
                )
                leave(order, t)

            return carry

        lax.fori_loop(0, tiles + 1, body, 0)

    def pair_copy(ref, kind, t):
        return pltpu.make_async_remote_copy(
            src_ref=ref.at[t], dst_ref=ref.at[t],
            send_sem=pair_send.at[kind], recv_sem=take_recv.at[kind, t],
            device_id=to_member(me + 1), device_id_type=MESH,
        )

    def next_copy(ref, kind, t):
        return pltpu.make_async_remote_copy(
            src_ref=ref.at[t], dst_ref=ref.at[t],
            send_sem=next_send.at[kind], recv_sem=take_recv.at[kind, t],
            device_id=to_member(me + 2), device_id_type=MESH,
        )

    last_tile = tile_of(tiles - 1)

    def last_copy(begin, end, send, recv, other):
        part = control_rim.at[last_tile, begin:end]
        return pltpu.make_async_remote_copy(
            src_ref=part, dst_ref=part, send_sem=send, recv_sem=recv,
            device_id=to_member(other), device_id_type=MESH,
        )

    first_half = [0, split]
    second_half = [split, channels]

    def last_first(send, other):
        return last_copy(*first_half, send, take_recv.at[1, last_tile], other)

    def last_second(send, other):
        return last_copy(*second_half, send, last_recv, other)

    def send_second():
        @pl.when(has_next)
        def _():
            last_second(next_send.at[1], me + 2).start()

        @pl.when(has_far)
        def _():
            last_second(far_send, me + 3).start()

    def lend_copy(own, lent, kind, early, which, order):
        return pltpu.make_async_remote_copy(
            src_ref=own.at[tile_of(order)], dst_ref=lent.at[which, order - early],
            send_sem=lend_send.at[kind], recv_sem=lend_recv.at[kind, which],
            device_id=to_member(lender), device_id_type=MESH,
        )

    def lend_whole(own, lent, kind, early, which):
        return pltpu.make_async_remote_copy(
            src_ref=own.at[0 : tiles - early], dst_ref=lent.at[which, 0 : tiles - early],
            send_sem=lend_send.at[kind], recv_sem=lend_recv.at[kind, which],
            device_id=to_member(lender), device_id_type=MESH,
        )

    def leave_mid(order, t):
        @pl.when(me == 0)
        def _():
            for k in range(channels):
                for n in range(len(mids)):
                    control_mid[t, k, n] = own_mid[t, k, n]
            pair_copy(control_mid, 0, t).start()

            @pl.when(has_next & (order < mids_cut))
            def _():
                next_copy(control_mid, 0, t).start()

        @pl.when((me > 1) & (order >= mids_cut))
        def _():
            lend_copy(own_mid, lent_mid, 0, mids_early, client, order).start()

    def leave_rim(order, t):
        @pl.when(me == 0)
        def _():
            for k in range(channels):
                for n in range(len(rims)):
                    control_rim[t, k, n] = own_rim[t, k, n]
            pair_copy(control_rim, 1, t).start()

            @pl.when(has_next & (order == rims_early))
            def _():
                def body(late, carry):
                    next_copy(control_mid, 0, tile_of(late)).start()
                    return carry

                lax.fori_loop(mids_cut, tiles, body, 0)

            @pl.when(has_next & (order < tiles - 1))
            def _():
                next_copy(control_rim, 1, t).start()

            @pl.when(order == tiles - 1)
            def _():
                @pl.when(has_next)
                def _():
                    last_first(next_send.at[1], me + 2).start()

                send_second()

        @pl.when((me > 1) & (order >= rims_early))
        def _():
            lend_copy(own_rim, lent_rim, 1, rims_early, client, order).start()

    def start_rows():
        @pl.when(down)
        def _():
            north_rows()

        @pl.when(jnp.logical_not(down))
        def _():
            south_rows()

    def end_rows():
        @pl.when(down)
        def _():
            south_rows()

        @pl.when(jnp.logical_not(down))
        def _():
            north_rows()

    load_at = min(first_tiles - 1, tiles - 1)
    per = -(-blocks // PACK_STEPS)
    pack_at = max(load_at, PACK_AT)
    send_at = pack_at + PACK_STEPS
    ahead = lats > 2 or send_at > tiles - 2

    def events_mid(j):
        if not ahead:
            @pl.when(j == load_at)
            def _():
                finish_loads()

            @pl.when((j >= pack_at) & (j < send_at))
            def _():
                begin = (j - pack_at) * per
                lax.fori_loop(begin, jnp.minimum(begin + per, blocks), pack_block, 0)

            @pl.when(j == send_at)
            def _():
                send_halos()

        @pl.when(j == tiles - 1)
        def _():
            end_rows()

    if ahead:
        finish_loads()
        lax.fori_loop(0, blocks, pack_block, 0)
        send_halos()
    start_rows()
    join_middle(0)
    ring_mid = mids + [halo]
    run_pass(
        join_middle, Ring(ring_mid, ring_mid), Ring(ring_mid, mids),
        own_mid, {c: n for n, c in enumerate(mids)}, events_mid, leave_mid,
    )

    for copy in sideways:
        copy.wait_recv()

    @pl.when(has_north)
    def _():
        for copy in south[1:]:
            copy.wait_recv()

    @pl.when(has_south)
    def _():
        for copy in north[1:]:
            copy.wait_recv()

    @pl.when(jnp.logical_not(has_north))
    def _():
        from_east[above, :] = zero_tile
        from_west[above, :] = zero_tile

    @pl.when(jnp.logical_not(has_south))
    def _():
        from_east[first, :] = zero_tile
        from_west[first, :] = zero_tile

    back = me > 1
    join_halo(0, back)
    ring_all = list(range(slots)) + [halo]
    run_pass(
        join_halo, Ring(ring_all, [slots - 1, halo, 0]), Ring(ring_all, rims),
        own_rim, {c: n for n, c in enumerate(rims)}, lambda j: None, leave_rim, back,
    )

    def clear(ref):
        for k in range(regions):
            ref[k] = zero_tile

    def ids_at(t, c):
        return region[pl.ds(pl.multiple_of(t * TILE, TILE), TILE), c * LANES : (c + 1) * LANES]

    def ocean_at(t, c):
        return field[OCEAN, c, pl.ds(pl.multiple_of(t * TILE + TILE, TILE), TILE), :]

    def add_regions(ref, items):
        for k in range(regions):
            total = ref[k]
            for ids, amount in items:
                total = total + jnp.where(ids == k, amount, 0.0)
            ref[k] = total

    def compare(ref, mine, its, t, part):
        items = []
        for n, c in enumerate(part):
            total = None
            for k in range(channels):
                d = mine(k, n) - its(k, n)
                total = d * d if total is None else total + d * d
            items.append((ids_at(t, c), ocean_at(t, c) * total))
        add_regions(ref, items)

    def share(which):
        for p, (a, b) in enumerate(peers):
            pltpu.make_async_remote_copy(
                src_ref=gathered.at[which, 0], dst_ref=gathered.at[which, p + 1],
                send_sem=sum_send.at[which], recv_sem=sum_recv.at[which],
                device_id=at(a, b), device_id_type=MESH,
            ).start()

    def collect(which):
        others = gathered.at[which, 1 : len(peers) + 1]
        pltpu.make_async_remote_copy(
            src_ref=others, dst_ref=others, send_sem=sum_send.at[which], recv_sem=sum_recv.at[which],
            device_id=at(*peers[0]), device_id_type=MESH,
        ).wait()
        total = gathered[which, 0]
        for p in range(len(peers)):
            total = total + gathered[which, p + 1]
        return jnp.sum(total, axis=1, keepdims=True)

    load_region.wait()
    clear(squares)
    clear(counts)

    def count(t, carry):
        add_regions(counts, [(ids_at(t, c), ocean_at(t, c)) for c in range(slots)])
        return carry

    lax.fori_loop(0, tiles, count, 0)
    gathered[0, 0] = jnp.sum(counts[...], axis=1)
    share(0)

    kinds = [
        (0, own_mid, control_mid, lent_mid, mids, mids_early),
        (1, own_rim, control_rim, lent_rim, rims, rims_early),
    ]

    def take(kind, order):
        _, own, control, _, part, _ = kinds[kind]
        t = tile_of(order)

        @pl.when(even)
        def _():
            next_copy(control, kind, t).wait_recv()

            @pl.when(has_pair)
            def _():
                pair_copy(control, kind, t).start()

            @pl.when(has_next)
            def _():
                next_copy(control, kind, t).start()

        @pl.when(jnp.logical_not(even))
        def _():
            pair_copy(control, kind, t).wait_recv()

    def weigh(kind, order):
        _, own, control, _, part, _ = kinds[kind]
        t = tile_of(order)
        compare(squares, lambda k, n: own[t, k, n], lambda k, n: control[t, k, n], t, part)

    def loop(begin, end, *actions):
        def body(order, carry):
            for action in actions:
                action(order)
            return carry

        lax.fori_loop(begin, end, body, 0)

    @pl.when(me > 0)
    def _():
        late_mids = jnp.where(me == 1, tiles, mids_cut)
        late_rims = jnp.where(me == 1, tiles, rims_early)
        loop(0, mids_cut, lambda o: take(0, o), lambda o: weigh(0, o))
        loop(0, late_rims, lambda o: take(1, o), lambda o: weigh(1, o))
        loop(mids_cut, late_mids, lambda o: take(0, o), lambda o: weigh(0, o))

    def loan_copy(other, which):
        return pltpu.make_async_remote_copy(
            src_ref=loan_out.at[which], dst_ref=loan,
            send_sem=loan_send.at[which], recv_sem=loan_recv,
            device_id=to_member(other), device_id_type=MESH,
        )

    def lend(which, other):
        clear(lent_squares)
        for kind, own, control, lent, part, early in kinds:
            if early == tiles:
                continue

            def body(order, carry):
                t = tile_of(order)
                compare(
                    lent_squares,
                    lambda k, n: lent[which, order - early, k, n],
                    lambda k, n: control[t, k, n], t, part,
                )
                return carry

            @pl.when(late_here | (kind == 1))
            def _():
                lend_whole(own, lent, kind, early, which).wait_recv()
                lax.fori_loop(early, tiles, body, 0)

        loan_out[which] = jnp.sum(lent_squares[...], axis=1)
        loan_copy(other, which).start()

    gathered[1, 0] = jnp.sum(squares[...], axis=1)

    @pl.when(me == 1)
    def _():
        for which in range(clients):
            lend(which, which + 2)

    @pl.when(me > 1)
    def _():
        loan_copy(me, 0).wait_recv()
        gathered[1, 0] = gathered[1, 0] + loan[...]

    share(1)
    taken = min(rims_early + TAKE_FIRST, tiles - 1)

    @pl.when(me > 1)
    def _():
        loop(mids_cut, tiles, lambda o: take(0, o))
        loop(rims_early, taken, lambda o: take(1, o))

    count_sum = collect(0)
    square_sum = collect(1)
    growth = jnp.sqrt(square_sum / (count_sum * channels) + epsilon)
    growth_wide = jnp.broadcast_to(growth, (regions, LANES))
    growth_out[...] = growth_wide
    load_target.wait()
    for k in range(regions):
        value[k] = jnp.broadcast_to(target[k] / growth_wide[k : k + 1, :], (TILE, LANES))

    def make_factor(b, carry):
        for i in range(block):
            t = b * block + i
            for c in range(slots):
                ids = ids_at(t, c)
                total = zero_tile
                for k in range(regions):
                    total = jnp.where(ids == k, value[k], total)
                factor[t, c] = total
        return carry

    lax.fori_loop(0, blocks, make_factor, 0)

    def breed(kind, order):
        _, own, control, _, part, _ = kinds[kind]
        t = tile_of(order)
        now = pl.ds(pl.multiple_of(t * TILE, TILE), TILE)
        for n, c in enumerate(part):
            scale = factor[t, c]
            for k in range(channels):
                base = control[t, k, n]
                bred[k, now, c * LANES : (c + 1) * LANES] = base + scale * (own[t, k, n] - base)

    def take_late(kind, order):
        @pl.when(me > 1)
        def _():
            take(kind, order)

    loop(0, tiles, lambda o: breed(0, o))
    loop(0, rims_early, lambda o: breed(1, o))
    loop(rims_early, taken, lambda o: breed(1, o))
    loop(taken, tiles - 1, lambda o: take_late(1, o), lambda o: breed(1, o))

    @pl.when(me > 1)
    def _():
        last_first(half_send, me).wait_recv()

        @pl.when(has_pair)
        def _():
            last_first(half_send, me + 1).start()

        @pl.when(has_next)
        def _():
            last_first(next_send.at[1], me + 2).start()

        last_second(far_send, me).wait_recv()
        send_second()

    breed(1, tiles - 1)

    for copy in sideways:
        copy.wait_send()

    @pl.when(has_north)
    def _():
        for copy in north:
            copy.wait_send()

    @pl.when(has_south)
    def _():
        for copy in south:
            copy.wait_send()

    for kind, own, control, lent, part, early in kinds:
        def whole_control(send, other, part=control):
            return pltpu.make_async_remote_copy(
                src_ref=part, dst_ref=part, send_sem=send.at[kind], recv_sem=take_recv.at[kind, 0],
                device_id=to_member(other), device_id_type=MESH,
            )

        @pl.when(me == 0)
        def _():
            whole_control(pair_send, 1).wait_send()

        @pl.when(has_pair & (me > 1))
        def _():
            if kind == 0:
                whole_control(pair_send, me + 1).wait_send()
            else:
                whole_control(pair_send, me + 1, control.at[0 : tiles - 1]).wait_send()
                last_first(half_send, me + 1).wait_send()

        @pl.when(has_next)
        def _():
            whole_control(next_send, me + 2).wait_send()

    @pl.when(has_far)
    def _():
        last_second(far_send, me + 3).wait_send()

    @pl.when(me == 1)
    def _():
        for which in range(clients):
            loan_copy(which + 2, which).wait_send()

    @pl.when(me > 1)
    def _():
        for kind, own, control, lent, part, early in kinds:
            if early < tiles:
                @pl.when(late_here | (kind == 1))
                def _():
                    lend_whole(own, lent, kind, early, client).wait_send()


def write_kernel(bred_in, growth_in, bred, growth, out_sem):
    copy = pltpu.make_async_copy(bred_in, bred, out_sem)
    copy.start()
    shape = growth_in.shape
    diagonal = lax.broadcasted_iota(jnp.int32, shape, 0) == lax.broadcasted_iota(jnp.int32, shape, 1)
    line = jnp.sum(jnp.where(diagonal, growth_in[...], 0.0), axis=0, keepdims=True)
    growth[...] = line[:, 0 : growth.shape[1]]
    copy.wait()


def per_device(
    sizes, member_state, column_depth, rotation, diffusivity, ocean_mask, region_id, target_rms
):
    members, lons, lats = sizes
    _, channels, rows, columns = member_state.shape
    regions = target_rms.shape[0]
    fields = channels + 3 + LEV
    tall = rows + 2 * TILE
    tiles = rows // TILE
    slots = columns // LANES
    group = lons * lats
    clients = max(members - 2, 1)
    late_mids = max(tiles - MIDS_EARLY, 1)
    late_rims = max(tiles - RIMS_EARLY, 1)
    f32 = jnp.float32
    anywhere = pl.BlockSpec(memory_space=pl.ANY)
    resident = pl.BlockSpec(memory_space=pltpu.VMEM)
    piece_mid = (channels, slots - 2, TILE, LANES)
    piece_rim = (channels, 2, TILE, LANES)
    bred, growth_wide = pl.pallas_call(
        functools.partial(cycle_kernel, sizes),
        out_shape=(
            pltpu.VMEM((channels, rows, columns), f32),
            pltpu.VMEM((regions, LANES), f32),
        ),
        in_specs=[anywhere] * 7,
        out_specs=(resident,) * 2,
        scratch_shapes=[
            pltpu.VMEM((fields, slots + 1, tall, LANES), f32),
            pltpu.VMEM((channels, slots + 1, tall, LANES), f32),
            pltpu.VMEM((slots + 1, tall, LANES), f32),
            pltpu.VMEM((slots + 1, tall, LANES), f32),
            pltpu.VMEM((tiles,) + piece_mid, f32),
            pltpu.VMEM((tiles,) + piece_rim, f32),
            pltpu.VMEM((tiles,) + piece_mid, f32),
            pltpu.VMEM((tiles,) + piece_rim, f32),
            pltpu.VMEM((clients, late_mids) + piece_mid, f32),
            pltpu.VMEM((clients, late_rims) + piece_rim, f32),
            pltpu.VMEM((rows, LANES), f32),
            pltpu.VMEM((rows, LANES), f32),
            pltpu.VMEM((tall, LANES), f32),
            pltpu.VMEM((tall, LANES), f32),
            pltpu.VMEM((fields // 2, slots, TILE, LANES), f32),
            pltpu.VMEM((fields // 2, slots, TILE, LANES), f32),
            pltpu.VMEM((fields // 2, slots, TILE, LANES), f32),
            pltpu.VMEM((fields // 2, slots, TILE, LANES), f32),
            pltpu.VMEM((rows, columns), jnp.int32),
            pltpu.VMEM((rows, columns), jnp.int32),
            pltpu.VMEM((regions, TILE, LANES), f32),
            pltpu.VMEM((regions, TILE, LANES), f32),
            pltpu.VMEM((regions, TILE, LANES), f32),
            pltpu.VMEM((2, group, regions, LANES), f32),
            pltpu.VMEM((clients, regions, LANES), f32),
            pltpu.VMEM((regions, LANES), f32),
            pltpu.VMEM((regions, TILE, LANES), f32),
            pltpu.VMEM((tiles, slots, TILE, LANES), f32),
            pltpu.SMEM((regions,), f32),
            pltpu.SemaphoreType.DMA((4,)),
            pltpu.SemaphoreType.DMA((8,)),
            pltpu.SemaphoreType.DMA((8,)),
            pltpu.SemaphoreType.DMA((2,)),
            pltpu.SemaphoreType.DMA((2,)),
            pltpu.SemaphoreType.DMA((2, tiles)),
            pltpu.SemaphoreType.DMA((2,)),
            pltpu.SemaphoreType.DMA((2, clients)),
            pltpu.SemaphoreType.DMA((clients,)),
            pltpu.SemaphoreType.DMA,
            pltpu.SemaphoreType.DMA((2,)),
            pltpu.SemaphoreType.DMA((2,)),
            pltpu.SemaphoreType.REGULAR,
            pltpu.SemaphoreType.DMA,
            pltpu.SemaphoreType.DMA,
            pltpu.SemaphoreType.DMA,
        ],
        compiler_params=pltpu.CompilerParams(
            collective_id=0, has_side_effects=True, vmem_limit_bytes=KERNEL_BYTES
        ),
    )(
        member_state.reshape(channels, rows, columns),
        column_depth, rotation, diffusivity, ocean_mask, region_id, target_rms,
    )
    bred, growth = pl.pallas_call(
        write_kernel,
        out_shape=(
            jax.ShapeDtypeStruct((channels, rows, columns), f32),
            jax.ShapeDtypeStruct((1, regions), f32),
        ),
        in_specs=[resident, resident],
        out_specs=(anywhere, resident),
        scratch_shapes=[pltpu.SemaphoreType.DMA],
        compiler_params=pltpu.CompilerParams(vmem_limit_bytes=WRITE_BYTES),
    )(bred, growth_wide)
    return (bred[None], growth)


def solution(mesh):
    sizes = (mesh.shape["member"], mesh.shape["lon"], mesh.shape["lat"])
    return jax.shard_map(
        functools.partial(per_device, sizes),
        mesh=mesh,
        in_specs=(
            P("member", None, "lat", "lon"),
            P("lat", "lon"),
            P("lat", "lon"),
            P(None, "lat", "lon"),
            P("lat", "lon"),
            P("lat", "lon"),
            P(),
        ),
        out_specs=(P("member", None, "lat", "lon"), P("member", None)),
        check_vma=False,
    )
```

```python
import functools

import jax
import jax.numpy as jnp
from jax import lax
from jax.experimental import pallas as pl
from jax.experimental.pallas import tpu as pltpu
from jax.sharding import PartitionSpec as P

LEV = 5
STEPS = 2
MARGIN = 2 * STEPS
TILE = 8
LANES = 128
FIRST_ROWS = 4
PACK_AT = 4
PACK_STEPS = 2
PACK_TILES = 4
TAKE_FIRST = 1
MIDS_EARLY = 15
RIMS_EARLY = 11
KERNEL_BYTES = 56 * 2**20
WRITE_BYTES = 16 * 2**20

divergence_gain = 0.25
pressure_gain = 0.25
buoyancy_gain = 0.1
advection_gain = 0.05
epsilon = 1e-06

MESH = pl.DeviceIdType.MESH


def cycle_kernel(
    sizes,
    state_in, depth_in, rotation_in, diffusivity_in, mask_in, region_in, target_in,
    bred, growth_out,
    field, middle, surface_one, surface_two,
    own_mid, own_rim, control_mid, control_rim, lent_mid, lent_rim,
    send_east, send_west, from_east, from_west, send_north, send_south, from_north, from_south,
    mask, region, squares, lent_squares, counts, gathered, loan_out, loan, value, factor, target,
    in_sem, halo_send, halo_recv, pair_send, next_send, take_recv,
    lend_send, lend_recv, loan_send, loan_recv, sum_send, sum_recv, go,
    half_send, far_send, last_recv,
):
    members, lons, lats = sizes
    channels, rows, columns = state_in.shape
    regions = squares.shape[0]
    fields = field.shape[0]
    slots = columns // LANES
    halo = slots
    tiles = rows // TILE
    tall = rows + 2 * TILE
    clients = members - 2
    DEPTH, ROT, OCEAN, DIFF = channels, channels + 1, channels + 2, channels + 3
    mids = list(range(1, slots - 1))
    rims = [0, slots - 1]
    half = TILE // 2
    first_tiles = min(FIRST_ROWS, tiles)
    mids_early = min(MIDS_EARLY, tiles)
    rims_early = min(RIMS_EARLY, tiles - 1)
    split = channels // 2 + 1

    me = lax.axis_index("member")
    lon = lax.axis_index("lon")
    lat = lax.axis_index("lat")
    core = lax.rem(me, 2)
    client = me - 2

    down = 2 * lat >= lats
    has_north = lat < lats - 1
    has_south = lat > 0

    def tile_of(order):
        return jnp.where(down, tiles - 1 - order, order)

    def tall_of(order, back=False):
        return jnp.where(down ^ back, tiles + 1 - order, order)

    def at(dlat, dlon, member=None):
        return {
            "member": me if member is None else member,
            "lon": lax.rem(lon + dlon + lons, lons),
            "lat": lax.rem(lat + dlat + lats, lats),
        }

    def to_member(other):
        return {"member": other, "lon": lon, "lat": lat}

    even = core == 0
    has_pair = even & (me + 1 < members)
    has_next = even & (me + 2 < members)
    has_far = even & (me + 3 < members)
    late_here = 2 * lon >= lons
    mids_cut = jnp.where(late_here, mids_early, tiles)
    parent = jnp.where(even, me - 2, me - 1)
    lender = 1
    peers = [(a, b) for a in range(lats) for b in range(lons) if (a, b) != (0, 0)]
    peers.sort(key=lambda p: -(p[0] + min(p[1], lons - p[1]) + p[1]))

    first_rows = first_tiles * TILE
    other_rows = rows - first_rows
    first_row = pl.multiple_of(jnp.where(down, rows - first_rows, 0), TILE)
    other_row = pl.multiple_of(jnp.where(down, 0, first_rows), TILE)

    def loads(index, row, count):
        src = pl.ds(row, count)
        dst = pl.ds(pl.multiple_of(row + TILE, TILE), count)
        copies = []
        for c in range(slots):
            part = slice(c * LANES, (c + 1) * LANES)
            copies += [
                (state_in.at[:, src, part], field.at[0:channels, c, dst, :]),
                (depth_in.at[src, part], field.at[DEPTH, c, dst, :]),
                (rotation_in.at[src, part], field.at[ROT, c, dst, :]),
                (diffusivity_in.at[:, src, part], field.at[DIFF:fields, c, dst, :]),
            ]
        copies.append((mask_in.at[src, :], mask.at[src, :]))
        return [pltpu.make_async_copy(a, b, in_sem.at[index]) for a, b in copies]

    def loaded(index, row, count):
        part = field.at[:, 0:slots, pl.ds(pl.multiple_of(row + TILE, TILE), count), :]
        pltpu.make_async_copy(part, part, in_sem.at[index]).wait()

    load_first = loads(0, first_row, first_rows)
    load_other = loads(1, other_row, other_rows) if other_rows else []
    load_region = pltpu.make_async_copy(region_in, region, in_sem.at[2])
    load_target = pltpu.make_async_copy(target_in, target, in_sem.at[3])
    for load in load_first + load_other + [load_region, load_target]:
        load.start()

    barrier = pltpu.get_barrier_semaphore()

    def greet(device):
        pl.semaphore_signal(barrier, inc=1, device_id=device, device_id_type=MESH)

    @pl.when(me == 0)
    def _():
        greet(to_member(1))
        for a, b in peers:
            greet(at(a, b, 1))

    @pl.when(me > 0)
    def _():
        for a, b in peers:
            greet(at(a, b))
        greet(to_member(parent))

    @pl.when(me == 1)
    def _():
        for other in range(2, members):
            greet(to_member(other))

    @pl.when(me > 1)
    def _():
        greet(to_member(lender))

    @pl.when((me > 1) & (core == 1))
    def _():
        greet(to_member(me - 3))

    @pl.when(me == 0)
    def _():
        pl.semaphore_wait(barrier, min(members - 1, 3))

    def all_here():
        @pl.when(me == 0)
        def _():
            pl.semaphore_wait(go, 1)

        @pl.when(me > 1)
        def _():
            pl.semaphore_wait(
                barrier,
                len(peers) + 1 + has_pair.astype(jnp.int32) + has_next.astype(jnp.int32)
                + has_far.astype(jnp.int32),
            )

    @pl.when(me == 1)
    def _():
        pl.semaphore_wait(barrier, 2 * len(peers) + 1 + clients)
        pl.semaphore_signal(go, inc=1, device_id=to_member(0), device_id_type=MESH)

    lane = lax.broadcasted_iota(jnp.int32, (TILE, LANES), 1)
    zero_tile = jnp.zeros((TILE, LANES), jnp.float32)
    low_lanes = lane < LANES // 2
    easterly = lax.rem(lane, 2 * MARGIN) >= MARGIN

    loaded(0, first_row, first_rows)

    def make_ocean(t, carry):
        r = pl.multiple_of(t * TILE, TILE)
        for c in range(slots):
            field[OCEAN, c, pl.ds(pl.multiple_of(r + TILE, TILE), TILE), :] = mask[
                pl.ds(r, TILE), c * LANES : (c + 1) * LANES
            ].astype(jnp.float32)
        return carry

    lax.fori_loop(first_row // TILE, first_row // TILE + first_tiles, make_ocean, 0)

    def remote(src, dst, index, device):
        return pltpu.make_async_remote_copy(
            src_ref=src, dst_ref=dst, send_sem=halo_send.at[index], recv_sem=halo_recv.at[index],
            device_id=device, device_id_type=MESH,
        )

    whole = slice(TILE, TILE + rows)
    last = slice(rows - TILE, rows)
    first = slice(0, TILE)
    above = slice(rows + TILE, rows + 2 * TILE)
    north = [
        remote(send_north, from_south, 0, at(1, 0)),
        remote(send_east.at[last], from_west.at[first], 4, at(1, 1)),
        remote(send_west.at[last], from_east.at[first], 5, at(1, -1)),
    ]
    south = [
        remote(send_south, from_north, 1, at(-1, 0)),
        remote(send_east.at[first], from_west.at[above], 6, at(-1, 1)),
        remote(send_west.at[first], from_east.at[above], 7, at(-1, -1)),
    ]
    sideways = [
        remote(send_east, from_west.at[whole], 2, at(0, 1)),
        remote(send_west, from_east.at[whole], 3, at(0, -1)),
    ]

    block = PACK_TILES if tiles % PACK_TILES == 0 else 1
    blocks = tiles // block

    def pack_block(b, carry):
        for i in range(block):
            r = pl.multiple_of((b * block + i) * TILE, TILE)
            now = pl.ds(pl.multiple_of(r + TILE, TILE), TILE)
            packed = [zero_tile] * 2
            for f in range(fields):
                g, s = divmod(f * 2 * MARGIN, LANES)
                edges = jnp.where(low_lanes, field[f, 0, now, :], field[f, slots - 1, now, :])
                here = (lane >= s) & (lane < s + 2 * MARGIN)
                packed[g] = jnp.where(here, pltpu.roll(edges, s + MARGIN, 1), packed[g])
            near, far = packed
            send_east[pl.ds(r, TILE), :] = jnp.where(easterly, pltpu.roll(far, MARGIN, 1), near)
            send_west[pl.ds(r, TILE), :] = jnp.where(easterly, near, pltpu.roll(far, LANES - MARGIN, 1))
        return carry

    def finish_loads():
        if other_rows:
            loaded(1, other_row, other_rows)
            lax.fori_loop(other_row // TILE, other_row // TILE + other_rows // TILE, make_ocean, 0)

    def pack_rows():
        for k in range(fields // 2):
            for c in range(slots):
                send_north[k, c, 0:half, :] = field[2 * k, c, rows + half : rows + TILE, :]
                send_north[k, c, half:TILE, :] = field[2 * k + 1, c, rows + half : rows + TILE, :]
                send_south[k, c, 0:half, :] = field[2 * k, c, TILE : TILE + half, :]
                send_south[k, c, half:TILE, :] = field[2 * k + 1, c, TILE : TILE + half, :]

    def send_halos():
        pack_rows()
        all_here()

        @pl.when(has_north)
        def _():
            for copy in north:
                copy.start()

        @pl.when(has_south)
        def _():
            for copy in south:
                copy.start()

        for copy in sideways:
            copy.start()

    def south_rows():
        @pl.when(has_south)
        def _():
            north[0].wait_recv()

        @pl.when(jnp.logical_not(has_south))
        def _():
            from_south[...] = jnp.zeros_like(from_south)

        for k in range(fields // 2):
            for c in range(slots):
                field[2 * k, c, half:TILE, :] = from_south[k, c, 0:half, :]
                field[2 * k + 1, c, half:TILE, :] = from_south[k, c, half:TILE, :]
                field[2 * k, c, 0:half, :] = from_south[k, c, 0:half, :]
                field[2 * k + 1, c, 0:half, :] = from_south[k, c, half:TILE, :]

    def north_rows():
        @pl.when(has_north)
        def _():
            south[0].wait_recv()

        @pl.when(jnp.logical_not(has_north))
        def _():
            from_north[...] = jnp.zeros_like(from_north)

        base = rows + TILE
        for k in range(fields // 2):
            for c in range(slots):
                field[2 * k, c, base : base + half, :] = from_north[k, c, 0:half, :]
                field[2 * k + 1, c, base : base + half, :] = from_north[k, c, half:TILE, :]
                field[2 * k, c, base + half : base + TILE, :] = from_north[k, c, 0:half, :]
                field[2 * k + 1, c, base + half : base + TILE, :] = from_north[k, c, half:TILE, :]

    def join_middle(order, back=False):
        now = pl.ds(pl.multiple_of(tall_of(order) * TILE, TILE), TILE)
        for f in range(fields):
            field[f, halo, now, :] = jnp.where(low_lanes, field[f, slots - 1, now, :], field[f, 0, now, :])

    def join_halo(order, back):
        now = pl.ds(pl.multiple_of(tall_of(order, back) * TILE, TILE), TILE)
        east, west = from_east[now, :], from_west[now, :]
        both = [
            jnp.where(easterly, east, west),
            jnp.where(easterly, pltpu.roll(east, MARGIN, 1), pltpu.roll(west, LANES - MARGIN, 1)),
        ]
        for f in range(fields):
            g, s = divmod(f * 2 * MARGIN, LANES)
            field[f, halo, now, :] = pltpu.roll(both[g], LANES - s - MARGIN, 1)

    class Ring:
        def __init__(self, ring, todo):
            self.todo = todo
            size = len(ring)
            place = {c: i for i, c in enumerate(ring)}
            self.east = {c: ring[(place[c] + 1) % size] for c in todo}
            self.west = {c: ring[(place[c] - 1) % size] for c in todo}
            self.used = sorted(set(todo) | set(self.east.values()) | set(self.west.values()))

        def sides(self, q):
            to_east = {c: pltpu.roll(q[c], LANES - 1, 1) for c in {*self.todo, *self.east.values()}}
            to_west = {c: pltpu.roll(q[c], 1, 1) for c in {*self.todo, *self.west.values()}}
            e = {c: jnp.where(lane == LANES - 1, to_east[self.east[c]], to_east[c]) for c in self.todo}
            w = {c: jnp.where(lane == 0, to_west[self.west[c]], to_west[c]) for c in self.todo}
            return e, w

    def surface_rows(src, dst, ring, r):
        now, above_r, below_r = pl.ds(r, TILE), pl.ds(r + 1, TILE), pl.ds(r - 1, TILE)

        def add_up(base, c, where):
            total = src[base, c, where, :]
            for k in range(1, LEV):
                total = total + src[base + k, c, where, :]
            return total

        e, w = ring.sides({c: add_up(1, c, now) for c in ring.used})
        for c in ring.todo:
            n, s = add_up(1 + LEV, c, above_r), add_up(1 + LEV, c, below_r)
            divergence = (e[c] - w[c]) + (n - s)
            dst[c, now, :] = field[OCEAN, c, now, :] * (
                src[0, c, now, :] - (divergence_gain / LEV) * field[DEPTH, c, now, :] * divergence
            )

    def update_rows(src, surface, ring, r, write):
        now, above_r, below_r = pl.ds(r, TILE), pl.ds(r + 1, TILE), pl.ds(r - 1, TILE)
        h = {c: surface[c, now, :] for c in ring.used}
        e, w = ring.sides(h)
        slope_east, slope_north = {}, {}
        for c in ring.todo:
            slope_east[c] = pressure_gain * (e[c] - w[c])
            slope_north[c] = pressure_gain * (surface[c, above_r, :] - surface[c, below_r, :])
            write(0, c, h[c])
        for k in range(LEV):
            iu, iv, ic = 1 + k, 1 + LEV + k, 1 + 2 * LEV + k
            u = {c: src[iu, c, now, :] for c in ring.used}
            v = {c: src[iv, c, now, :] for c in ring.used}
            t = {c: src[ic, c, now, :] for c in ring.used}
            ue, uw = ring.sides(u)
            ve, vw = ring.sides(v)
            te, tw = ring.sides(t)
            for c in ring.todo:
                ocean = field[OCEAN, c, now, :]
                rotation = field[ROT, c, now, :]
                mixing = field[DIFF + k, c, now, :]
                tn, ts = src[ic, c, above_r, :], src[ic, c, below_r, :]
                heat_east, heat_north = te[c] - tw[c], tn - ts
                around_u = (ue[c] + uw[c]) + (src[iu, c, above_r, :] + src[iu, c, below_r, :])
                around_v = (ve[c] + vw[c]) + (src[iv, c, above_r, :] + src[iv, c, below_r, :])
                around_t = (te[c] + tw[c]) + (tn + ts)
                new_u = ocean * (
                    u[c] + rotation * v[c] - slope_east[c] - buoyancy_gain * heat_east
                    + mixing * (around_u - 4.0 * u[c])
                )
                new_v = ocean * (
                    v[c] - rotation * u[c] - slope_north[c] - buoyancy_gain * heat_north
                    + mixing * (around_v - 4.0 * v[c])
                )
                new_t = ocean * (
                    t[c] + mixing * (around_t - 4.0 * t[c])
                    - advection_gain * (new_u * heat_east + new_v * heat_north)
                )
                write(iu, c, new_u)
                write(iv, c, new_v)
                write(ic, c, new_t)

    def run_pass(join, one, two, own, own_slots, at_order, leave, back=False):
        step = jnp.where(down ^ back, -1, 1)

        def body(i, carry):
            j = i - 1
            at_order(j)
            join(j + 2, back)
            r = jnp.where(down ^ back, rows - TILE * j, TILE + TILE * j)
            surface_rows(field, surface_one, one, r + 3 * step)
            r_one = r + 2 * step

            def middle_write(channel, c, new):
                middle[channel, c, pl.ds(r_one, TILE), :] = new

            update_rows(field, surface_one, one, r_one, middle_write)
            surface_rows(middle, surface_two, one, r + step)

            @pl.when(j >= 0)
            def _():
                order = jnp.where(back, tiles - 1 - j, j)
                t = tile_of(order)

                def last_write(channel, c, new):
                    own[t, channel, own_slots[c]] = new

                update_rows(
                    middle, surface_two, two, pl.multiple_of(r, TILE), last_write
                )
                leave(order, t)

            return carry

        lax.fori_loop(0, tiles + 1, body, 0)

    def pair_copy(ref, kind, t):
        return pltpu.make_async_remote_copy(
            src_ref=ref.at[t], dst_ref=ref.at[t],
            send_sem=pair_send.at[kind], recv_sem=take_recv.at[kind, t],
            device_id=to_member(me + 1), device_id_type=MESH,
        )

    def next_copy(ref, kind, t):
        return pltpu.make_async_remote_copy(
            src_ref=ref.at[t], dst_ref=ref.at[t],
            send_sem=next_send.at[kind], recv_sem=take_recv.at[kind, t],
            device_id=to_member(me + 2), device_id_type=MESH,
        )

    last_tile = tile_of(tiles - 1)

    def last_copy(begin, end, send, recv, other):
        part = control_rim.at[last_tile, begin:end]
        return pltpu.make_async_remote_copy(
            src_ref=part, dst_ref=part, send_sem=send, recv_sem=recv,
            device_id=to_member(other), device_id_type=MESH,
        )

    first_half = [0, split]
    second_half = [split, channels]

    def last_first(send, other):
        return last_copy(*first_half, send, take_recv.at[1, last_tile], other)

    def last_second(send, other):
        return last_copy(*second_half, send, last_recv, other)

    def send_second():
        @pl.when(has_next)
        def _():
            last_second(next_send.at[1], me + 2).start()

        @pl.when(has_far)
        def _():
            last_second(far_send, me + 3).start()

    def lend_copy(own, lent, kind, early, which, order):
        return pltpu.make_async_remote_copy(
            src_ref=own.at[tile_of(order)], dst_ref=lent.at[which, order - early],
            send_sem=lend_send.at[kind], recv_sem=lend_recv.at[kind, which],
            device_id=to_member(lender), device_id_type=MESH,
        )

    def lend_whole(own, lent, kind, early, which):
        return pltpu.make_async_remote_copy(
            src_ref=own.at[0 : tiles - early], dst_ref=lent.at[which, 0 : tiles - early],
            send_sem=lend_send.at[kind], recv_sem=lend_recv.at[kind, which],
            device_id=to_member(lender), device_id_type=MESH,
        )

    def leave_mid(order, t):
        @pl.when(me == 0)
        def _():
            for k in range(channels):
                for n in range(len(mids)):
                    control_mid[t, k, n] = own_mid[t, k, n]
            pair_copy(control_mid, 0, t).start()

            @pl.when(has_next & (order < mids_cut))
            def _():
                next_copy(control_mid, 0, t).start()

        @pl.when((me > 1) & (order >= mids_cut))
        def _():
            lend_copy(own_mid, lent_mid, 0, mids_early, client, order).start()

    def leave_rim(order, t):
        @pl.when(me == 0)
        def _():
            for k in range(channels):
                for n in range(len(rims)):
                    control_rim[t, k, n] = own_rim[t, k, n]
            pair_copy(control_rim, 1, t).start()

            @pl.when(has_next & (order == rims_early))
            def _():
                def body(late, carry):
                    next_copy(control_mid, 0, tile_of(late)).start()
                    return carry

                lax.fori_loop(mids_cut, tiles, body, 0)

            @pl.when(has_next & (order < tiles - 1))
            def _():
                next_copy(control_rim, 1, t).start()

            @pl.when(order == tiles - 1)
            def _():
                @pl.when(has_next)
                def _():
                    last_first(next_send.at[1], me + 2).start()

                send_second()

        @pl.when((me > 1) & (order >= rims_early))
        def _():
            lend_copy(own_rim, lent_rim, 1, rims_early, client, order).start()

    def start_rows():
        @pl.when(down)
        def _():
            north_rows()

        @pl.when(jnp.logical_not(down))
        def _():
            south_rows()

    def end_rows():
        @pl.when(down)
        def _():
            south_rows()

        @pl.when(jnp.logical_not(down))
        def _():
            north_rows()

    load_at = min(first_tiles - 1, tiles - 1)
    per = -(-blocks // PACK_STEPS)
    pack_at = max(load_at, PACK_AT)
    send_at = pack_at + PACK_STEPS
    ahead = lats > 2 or send_at > tiles - 2

    def events_mid(j):
        if not ahead:
            @pl.when(j == load_at)
            def _():
                finish_loads()

            @pl.when((j >= pack_at) & (j < send_at))
            def _():
                begin = (j - pack_at) * per
                lax.fori_loop(begin, jnp.minimum(begin + per, blocks), pack_block, 0)

            @pl.when(j == send_at)
            def _():
                send_halos()

        @pl.when(j == tiles - 1)
        def _():
            end_rows()

    if ahead:
        finish_loads()
        lax.fori_loop(0, blocks, pack_block, 0)
        send_halos()
    start_rows()
    join_middle(0)
    ring_mid = mids + [halo]
    run_pass(
        join_middle, Ring(ring_mid, ring_mid), Ring(ring_mid, mids),
        own_mid, {c: n for n, c in enumerate(mids)}, events_mid, leave_mid,
    )

    for copy in sideways:
        copy.wait_recv()

    @pl.when(has_north)
    def _():
        for copy in south[1:]:
            copy.wait_recv()

    @pl.when(has_south)
    def _():
        for copy in north[1:]:
            copy.wait_recv()

    @pl.when(jnp.logical_not(has_north))
    def _():
        from_east[above, :] = zero_tile
        from_west[above, :] = zero_tile

    @pl.when(jnp.logical_not(has_south))
    def _():
        from_east[first, :] = zero_tile
        from_west[first, :] = zero_tile

    back = me > 1
    join_halo(0, back)
    ring_all = list(range(slots)) + [halo]
    run_pass(
        join_halo, Ring(ring_all, [slots - 1, halo, 0]), Ring(ring_all, rims),
        own_rim, {c: n for n, c in enumerate(rims)}, lambda j: None, leave_rim, back,
    )

    def clear(ref):
        for k in range(regions):
            ref[k] = zero_tile

    def ids_at(t, c):
        return region[pl.ds(pl.multiple_of(t * TILE, TILE), TILE), c * LANES : (c + 1) * LANES]

    def ocean_at(t, c):
        return field[OCEAN, c, pl.ds(pl.multiple_of(t * TILE + TILE, TILE), TILE), :]

    def add_regions(ref, items):
        for k in range(regions):
            total = ref[k]
            for ids, amount in items:
                total = total + jnp.where(ids == k, amount, 0.0)
            ref[k] = total

    def compare(ref, mine, its, t, part):
        items = []
        for n, c in enumerate(part):
            total = None
            for k in range(channels):
                d = mine(k, n) - its(k, n)
                total = d * d if total is None else total + d * d
            items.append((ids_at(t, c), ocean_at(t, c) * total))
        add_regions(ref, items)

    def share(which):
        for p, (a, b) in enumerate(peers):
            pltpu.make_async_remote_copy(
                src_ref=gathered.at[which, 0], dst_ref=gathered.at[which, p + 1],
                send_sem=sum_send.at[which], recv_sem=sum_recv.at[which],
                device_id=at(a, b), device_id_type=MESH,
            ).start()

    def collect(which):
        others = gathered.at[which, 1 : len(peers) + 1]
        pltpu.make_async_remote_copy(
            src_ref=others, dst_ref=others, send_sem=sum_send.at[which], recv_sem=sum_recv.at[which],
            device_id=at(*peers[0]), device_id_type=MESH,
        ).wait()
        total = gathered[which, 0]
        for p in range(len(peers)):
            total = total + gathered[which, p + 1]
        return jnp.sum(total, axis=1, keepdims=True)

    load_region.wait()
    clear(squares)
    clear(counts)

    def count(t, carry):
        add_regions(counts, [(ids_at(t, c), ocean_at(t, c)) for c in range(slots)])
        return carry

    lax.fori_loop(0, tiles, count, 0)
    gathered[0, 0] = jnp.sum(counts[...], axis=1)
    share(0)

    kinds = [
        (0, own_mid, control_mid, lent_mid, mids, mids_early),
        (1, own_rim, control_rim, lent_rim, rims, rims_early),
    ]

    def take(kind, order):
        _, own, control, _, part, _ = kinds[kind]
        t = tile_of(order)

        @pl.when(even)
        def _():
            next_copy(control, kind, t).wait_recv()

            @pl.when(has_pair)
            def _():
                pair_copy(control, kind, t).start()

            @pl.when(has_next)
            def _():
                next_copy(control, kind, t).start()

        @pl.when(jnp.logical_not(even))
        def _():
            pair_copy(control, kind, t).wait_recv()

    def weigh(kind, order):
        _, own, control, _, part, _ = kinds[kind]
        t = tile_of(order)
        compare(squares, lambda k, n: own[t, k, n], lambda k, n: control[t, k, n], t, part)

    def loop(begin, end, *actions):
        def body(order, carry):
            for action in actions:
                action(order)
            return carry

        lax.fori_loop(begin, end, body, 0)

    @pl.when(me > 0)
    def _():
        late_mids = jnp.where(me == 1, tiles, mids_cut)
        late_rims = jnp.where(me == 1, tiles, rims_early)
        loop(0, mids_cut, lambda o: take(0, o), lambda o: weigh(0, o))
        loop(0, late_rims, lambda o: take(1, o), lambda o: weigh(1, o))
        loop(mids_cut, late_mids, lambda o: take(0, o), lambda o: weigh(0, o))

    def loan_copy(other, which):
        return pltpu.make_async_remote_copy(
            src_ref=loan_out.at[which], dst_ref=loan,
            send_sem=loan_send.at[which], recv_sem=loan_recv,
            device_id=to_member(other), device_id_type=MESH,
        )

    def lend(which, other):
        clear(lent_squares)
        for kind, own, control, lent, part, early in kinds:
            if early == tiles:
                continue

            def body(order, carry):
                t = tile_of(order)
                compare(
                    lent_squares,
                    lambda k, n: lent[which, order - early, k, n],
                    lambda k, n: control[t, k, n], t, part,
                )
                return carry

            @pl.when(late_here | (kind == 1))
            def _():
                lend_whole(own, lent, kind, early, which).wait_recv()
                lax.fori_loop(early, tiles, body, 0)

        loan_out[which] = jnp.sum(lent_squares[...], axis=1)
        loan_copy(other, which).start()

    gathered[1, 0] = jnp.sum(squares[...], axis=1)

    @pl.when(me == 1)
    def _():
        for which in range(clients):
            lend(which, which + 2)

    @pl.when(me > 1)
    def _():
        loan_copy(me, 0).wait_recv()
        gathered[1, 0] = gathered[1, 0] + loan[...]

    share(1)
    taken = min(rims_early + TAKE_FIRST, tiles - 1)

    @pl.when(me > 1)
    def _():
        loop(mids_cut, tiles, lambda o: take(0, o))
        loop(rims_early, taken, lambda o: take(1, o))

    count_sum = collect(0)
    square_sum = collect(1)
    growth = jnp.sqrt(square_sum / (count_sum * channels) + epsilon)
    growth_wide = jnp.broadcast_to(growth, (regions, LANES))
    growth_out[...] = growth_wide
    load_target.wait()
    for k in range(regions):
        value[k] = jnp.broadcast_to(target[k] / growth_wide[k : k + 1, :], (TILE, LANES))

    def make_factor(b, carry):
        for i in range(block):
            t = b * block + i
            for c in range(slots):
                ids = ids_at(t, c)
                total = zero_tile
                for k in range(regions):
                    total = jnp.where(ids == k, value[k], total)
                factor[t, c] = total
        return carry

    lax.fori_loop(0, blocks, make_factor, 0)

    def breed(kind, order):
        _, own, control, _, part, _ = kinds[kind]
        t = tile_of(order)
        now = pl.ds(pl.multiple_of(t * TILE, TILE), TILE)
        for n, c in enumerate(part):
            scale = factor[t, c]
            for k in range(channels):
                base = control[t, k, n]
                bred[k, now, c * LANES : (c + 1) * LANES] = base + scale * (own[t, k, n] - base)

    def take_late(kind, order):
        @pl.when(me > 1)
        def _():
            take(kind, order)

    loop(0, tiles, lambda o: breed(0, o))
    loop(0, rims_early, lambda o: breed(1, o))
    loop(rims_early, taken, lambda o: breed(1, o))
    loop(taken, tiles - 1, lambda o: take_late(1, o), lambda o: breed(1, o))

    @pl.when(me > 1)
    def _():
        last_first(half_send, me).wait_recv()

        @pl.when(has_pair)
        def _():
            last_first(half_send, me + 1).start()

        @pl.when(has_next)
        def _():
            last_first(next_send.at[1], me + 2).start()

        last_second(far_send, me).wait_recv()
        send_second()

    breed(1, tiles - 1)

    for copy in sideways:
        copy.wait_send()

    @pl.when(has_north)
    def _():
        for copy in north:
            copy.wait_send()

    @pl.when(has_south)
    def _():
        for copy in south:
            copy.wait_send()

    for kind, own, control, lent, part, early in kinds:
        def whole_control(send, other, part=control):
            return pltpu.make_async_remote_copy(
                src_ref=part, dst_ref=part, send_sem=send.at[kind], recv_sem=take_recv.at[kind, 0],
                device_id=to_member(other), device_id_type=MESH,
            )

        @pl.when(me == 0)
        def _():
            whole_control(pair_send, 1).wait_send()

        @pl.when(has_pair & (me > 1))
        def _():
            if kind == 0:
                whole_control(pair_send, me + 1).wait_send()
            else:
                whole_control(pair_send, me + 1, control.at[0 : tiles - 1]).wait_send()
                last_first(half_send, me + 1).wait_send()

        @pl.when(has_next)
        def _():
            whole_control(next_send, me + 2).wait_send()

    @pl.when(has_far)
    def _():
        last_second(far_send, me + 3).wait_send()

    @pl.when(me == 1)
    def _():
        for which in range(clients):
            loan_copy(which + 2, which).wait_send()

    @pl.when(me > 1)
    def _():
        for kind, own, control, lent, part, early in kinds:
            if early < tiles:
                @pl.when(late_here | (kind == 1))
                def _():
                    lend_whole(own, lent, kind, early, client).wait_send()


def write_kernel(bred_in, growth_in, bred, growth, out_sem):
    copy = pltpu.make_async_copy(bred_in, bred, out_sem)
    copy.start()
    shape = growth_in.shape
    diagonal = lax.broadcasted_iota(jnp.int32, shape, 0) == lax.broadcasted_iota(jnp.int32, shape, 1)
    line = jnp.sum(jnp.where(diagonal, growth_in[...], 0.0), axis=0, keepdims=True)
    growth[...] = line[:, 0 : growth.shape[1]]
    copy.wait()


def per_device(
    sizes, member_state, column_depth, rotation, diffusivity, ocean_mask, region_id, target_rms
):
    members, lons, lats = sizes
    _, channels, rows, columns = member_state.shape
    regions = target_rms.shape[0]
    fields = channels + 3 + LEV
    tall = rows + 2 * TILE
    tiles = rows // TILE
    slots = columns // LANES
    group = lons * lats
    clients = max(members - 2, 1)
    late_mids = max(tiles - MIDS_EARLY, 1)
    late_rims = max(tiles - RIMS_EARLY, 1)
    f32 = jnp.float32
    anywhere = pl.BlockSpec(memory_space=pl.ANY)
    resident = pl.BlockSpec(memory_space=pltpu.VMEM)
    piece_mid = (channels, slots - 2, TILE, LANES)
    piece_rim = (channels, 2, TILE, LANES)
    bred, growth_wide = pl.pallas_call(
        functools.partial(cycle_kernel, sizes),
        out_shape=(
            pltpu.VMEM((channels, rows, columns), f32),
            pltpu.VMEM((regions, LANES), f32),
        ),
        in_specs=[anywhere] * 7,
        out_specs=(resident,) * 2,
        scratch_shapes=[
            pltpu.VMEM((fields, slots + 1, tall, LANES), f32),
            pltpu.VMEM((channels, slots + 1, tall, LANES), f32),
            pltpu.VMEM((slots + 1, tall, LANES), f32),
            pltpu.VMEM((slots + 1, tall, LANES), f32),
            pltpu.VMEM((tiles,) + piece_mid, f32),
            pltpu.VMEM((tiles,) + piece_rim, f32),
            pltpu.VMEM((tiles,) + piece_mid, f32),
            pltpu.VMEM((tiles,) + piece_rim, f32),
            pltpu.VMEM((clients, late_mids) + piece_mid, f32),
            pltpu.VMEM((clients, late_rims) + piece_rim, f32),
            pltpu.VMEM((rows, LANES), f32),
            pltpu.VMEM((rows, LANES), f32),
            pltpu.VMEM((tall, LANES), f32),
            pltpu.VMEM((tall, LANES), f32),
            pltpu.VMEM((fields // 2, slots, TILE, LANES), f32),
            pltpu.VMEM((fields // 2, slots, TILE, LANES), f32),
            pltpu.VMEM((fields // 2, slots, TILE, LANES), f32),
            pltpu.VMEM((fields // 2, slots, TILE, LANES), f32),
            pltpu.VMEM((rows, columns), jnp.int32),
            pltpu.VMEM((rows, columns), jnp.int32),
            pltpu.VMEM((regions, TILE, LANES), f32),
            pltpu.VMEM((regions, TILE, LANES), f32),
            pltpu.VMEM((regions, TILE, LANES), f32),
            pltpu.VMEM((2, group, regions, LANES), f32),
            pltpu.VMEM((clients, regions, LANES), f32),
            pltpu.VMEM((regions, LANES), f32),
            pltpu.VMEM((regions, TILE, LANES), f32),
            pltpu.VMEM((tiles, slots, TILE, LANES), f32),
            pltpu.SMEM((regions,), f32),
            pltpu.SemaphoreType.DMA((4,)),
            pltpu.SemaphoreType.DMA((8,)),
            pltpu.SemaphoreType.DMA((8,)),
            pltpu.SemaphoreType.DMA((2,)),
            pltpu.SemaphoreType.DMA((2,)),
            pltpu.SemaphoreType.DMA((2, tiles)),
            pltpu.SemaphoreType.DMA((2,)),
            pltpu.SemaphoreType.DMA((2, clients)),
            pltpu.SemaphoreType.DMA((clients,)),
            pltpu.SemaphoreType.DMA,
            pltpu.SemaphoreType.DMA((2,)),
            pltpu.SemaphoreType.DMA((2,)),
            pltpu.SemaphoreType.REGULAR,
            pltpu.SemaphoreType.DMA,
            pltpu.SemaphoreType.DMA,
            pltpu.SemaphoreType.DMA,
        ],
        compiler_params=pltpu.CompilerParams(
            collective_id=0, has_side_effects=True, vmem_limit_bytes=KERNEL_BYTES
        ),
    )(
        member_state.reshape(channels, rows, columns),
        column_depth, rotation, diffusivity, ocean_mask, region_id, target_rms,
    )
    bred, growth = pl.pallas_call(
        write_kernel,
        out_shape=(
            jax.ShapeDtypeStruct((channels, rows, columns), f32),
            jax.ShapeDtypeStruct((1, regions), f32),
        ),
        in_specs=[resident, resident],
        out_specs=(anywhere, resident),
        scratch_shapes=[pltpu.SemaphoreType.DMA],
        compiler_params=pltpu.CompilerParams(vmem_limit_bytes=WRITE_BYTES),
    )(bred, growth_wide)
    return (bred[None], growth)


def solution(mesh):
    sizes = (mesh.shape["member"], mesh.shape["lon"], mesh.shape["lat"])
    return jax.shard_map(
        functools.partial(per_device, sizes),
        mesh=mesh,
        in_specs=(
            P("member", None, "lat", "lon"),
            P("lat", "lon"),
            P("lat", "lon"),
            P(None, "lat", "lon"),
            P("lat", "lon"),
            P("lat", "lon"),
            P(),
        ),
        out_specs=(P("member", None, "lat", "lon"), P("member", None)),
        check_vma=False,
    )
```

```python
import functools

import jax
import jax.numpy as jnp
from jax import lax
from jax.experimental import pallas as pl
from jax.experimental.pallas import tpu as pltpu
from jax.sharding import PartitionSpec as P

LEV = 5
STEPS = 2
MARGIN = 2 * STEPS
TILE = 8
LANES = 128
FIRST_ROWS = 4
PACK_AT = 4
PACK_STEPS = 2
PACK_TILES = 4
TAKE_FIRST = 2
MIDS_EARLY = 15
RIMS_EARLY = 11
KERNEL_BYTES = 56 * 2**20
WRITE_BYTES = 16 * 2**20

divergence_gain = 0.25
pressure_gain = 0.25
buoyancy_gain = 0.1
advection_gain = 0.05
epsilon = 1e-06

MESH = pl.DeviceIdType.MESH


def cycle_kernel(
    sizes,
    state_in, depth_in, rotation_in, diffusivity_in, mask_in, region_in, target_in,
    bred, growth_out,
    field, middle, surface_one, surface_two,
    own_mid, own_rim, control_mid, control_rim, lent_mid, lent_rim,
    send_east, send_west, from_east, from_west, send_north, send_south, from_north, from_south,
    mask, region, squares, lent_squares, counts, gathered, loan_out, loan, value, factor, target,
    in_sem, halo_send, halo_recv, pair_send, next_send, take_recv,
    lend_send, lend_recv, loan_send, loan_recv, sum_send, sum_recv, go,
    half_send, far_send, last_recv,
):
    members, lons, lats = sizes
    channels, rows, columns = state_in.shape
    regions = squares.shape[0]
    fields = field.shape[0]
    slots = columns // LANES
    halo = slots
    tiles = rows // TILE
    tall = rows + 2 * TILE
    clients = members - 2
    DEPTH, ROT, OCEAN, DIFF = channels, channels + 1, channels + 2, channels + 3
    mids = list(range(1, slots - 1))
    rims = [0, slots - 1]
    half = TILE // 2
    first_tiles = min(FIRST_ROWS, tiles)
    mids_early = min(MIDS_EARLY, tiles)
    rims_early = min(RIMS_EARLY, tiles - 1)
    split = channels // 2

    me = lax.axis_index("member")
    lon = lax.axis_index("lon")
    lat = lax.axis_index("lat")
    core = lax.rem(me, 2)
    client = me - 2

    down = 2 * lat >= lats
    has_north = lat < lats - 1
    has_south = lat > 0

    def tile_of(order):
        return jnp.where(down, tiles - 1 - order, order)

    def tall_of(order, back=False):
        return jnp.where(down ^ back, tiles + 1 - order, order)

    def at(dlat, dlon, member=None):
        return {
            "member": me if member is None else member,
            "lon": lax.rem(lon + dlon + lons, lons),
            "lat": lax.rem(lat + dlat + lats, lats),
        }

    def to_member(other):
        return {"member": other, "lon": lon, "lat": lat}

    even = core == 0
    has_pair = even & (me + 1 < members)
    has_next = even & (me + 2 < members)
    has_far = even & (me + 3 < members)
    late_here = 2 * lon >= lons
    mids_cut = jnp.where(late_here, mids_early, tiles)
    parent = jnp.where(even, me - 2, me - 1)
    lender = 1
    peers = [(a, b) for a in range(lats) for b in range(lons) if (a, b) != (0, 0)]
    peers.sort(key=lambda p: -(p[0] + min(p[1], lons - p[1]) + p[1]))

    first_rows = first_tiles * TILE
    other_rows = rows - first_rows
    first_row = pl.multiple_of(jnp.where(down, rows - first_rows, 0), TILE)
    other_row = pl.multiple_of(jnp.where(down, 0, first_rows), TILE)

    def loads(index, row, count):
        src = pl.ds(row, count)
        dst = pl.ds(pl.multiple_of(row + TILE, TILE), count)
        copies = []
        for c in range(slots):
            part = slice(c * LANES, (c + 1) * LANES)
            copies += [
                (state_in.at[:, src, part], field.at[0:channels, c, dst, :]),
                (depth_in.at[src, part], field.at[DEPTH, c, dst, :]),
                (rotation_in.at[src, part], field.at[ROT, c, dst, :]),
                (diffusivity_in.at[:, src, part], field.at[DIFF:fields, c, dst, :]),
            ]
        copies.append((mask_in.at[src, :], mask.at[src, :]))
        return [pltpu.make_async_copy(a, b, in_sem.at[index]) for a, b in copies]

    def loaded(index, row, count):
        part = field.at[:, 0:slots, pl.ds(pl.multiple_of(row + TILE, TILE), count), :]
        pltpu.make_async_copy(part, part, in_sem.at[index]).wait()

    load_first = loads(0, first_row, first_rows)
    load_other = loads(1, other_row, other_rows) if other_rows else []
    load_region = pltpu.make_async_copy(region_in, region, in_sem.at[2])
    load_target = pltpu.make_async_copy(target_in, target, in_sem.at[3])
    for load in load_first + load_other + [load_region, load_target]:
        load.start()

    barrier = pltpu.get_barrier_semaphore()

    def greet(device):
        pl.semaphore_signal(barrier, inc=1, device_id=device, device_id_type=MESH)

    @pl.when(me == 0)
    def _():
        greet(to_member(1))
        for a, b in peers:
            greet(at(a, b, 1))

    @pl.when(me > 0)
    def _():
        for a, b in peers:
            greet(at(a, b))
        greet(to_member(parent))

    @pl.when(me == 1)
    def _():
        for other in range(2, members):
            greet(to_member(other))

    @pl.when(me > 1)
    def _():
        greet(to_member(lender))

    @pl.when((me > 1) & (core == 1))
    def _():
        greet(to_member(me - 3))

    @pl.when(me == 0)
    def _():
        pl.semaphore_wait(barrier, min(members - 1, 3))

    def all_here():
        @pl.when(me == 0)
        def _():
            pl.semaphore_wait(go, 1)

        @pl.when(me > 1)
        def _():
            pl.semaphore_wait(
                barrier,
                len(peers) + 1 + has_pair.astype(jnp.int32) + has_next.astype(jnp.int32)
                + has_far.astype(jnp.int32),
            )

    @pl.when(me == 1)
    def _():
        pl.semaphore_wait(barrier, 2 * len(peers) + 1 + clients)
        pl.semaphore_signal(go, inc=1, device_id=to_member(0), device_id_type=MESH)

    lane = lax.broadcasted_iota(jnp.int32, (TILE, LANES), 1)
    zero_tile = jnp.zeros((TILE, LANES), jnp.float32)
    low_lanes = lane < LANES // 2
    easterly = lax.rem(lane, 2 * MARGIN) >= MARGIN

    loaded(0, first_row, first_rows)

    def make_ocean(t, carry):
        r = pl.multiple_of(t * TILE, TILE)
        for c in range(slots):
            field[OCEAN, c, pl.ds(pl.multiple_of(r + TILE, TILE), TILE), :] = mask[
                pl.ds(r, TILE), c * LANES : (c + 1) * LANES
            ].astype(jnp.float32)
        return carry

    lax.fori_loop(first_row // TILE, first_row // TILE + first_tiles, make_ocean, 0)

    def remote(src, dst, index, device):
        return pltpu.make_async_remote_copy(
            src_ref=src, dst_ref=dst, send_sem=halo_send.at[index], recv_sem=halo_recv.at[index],
            device_id=device, device_id_type=MESH,
        )

    whole = slice(TILE, TILE + rows)
    last = slice(rows - TILE, rows)
    first = slice(0, TILE)
    above = slice(rows + TILE, rows + 2 * TILE)
    north = [
        remote(send_north, from_south, 0, at(1, 0)),
        remote(send_east.at[last], from_west.at[first], 4, at(1, 1)),
        remote(send_west.at[last], from_east.at[first], 5, at(1, -1)),
    ]
    south = [
        remote(send_south, from_north, 1, at(-1, 0)),
        remote(send_east.at[first], from_west.at[above], 6, at(-1, 1)),
        remote(send_west.at[first], from_east.at[above], 7, at(-1, -1)),
    ]
    sideways = [
        remote(send_east, from_west.at[whole], 2, at(0, 1)),
        remote(send_west, from_east.at[whole], 3, at(0, -1)),
    ]

    block = PACK_TILES if tiles % PACK_TILES == 0 else 1
    blocks = tiles // block

    def pack_block(b, carry):
        for i in range(block):
            r = pl.multiple_of((b * block + i) * TILE, TILE)
            now = pl.ds(pl.multiple_of(r + TILE, TILE), TILE)
            packed = [zero_tile] * 2
            for f in range(fields):
                g, s = divmod(f * 2 * MARGIN, LANES)
                edges = jnp.where(low_lanes, field[f, 0, now, :], field[f, slots - 1, now, :])
                here = (lane >= s) & (lane < s + 2 * MARGIN)
                packed[g] = jnp.where(here, pltpu.roll(edges, s + MARGIN, 1), packed[g])
            near, far = packed
            send_east[pl.ds(r, TILE), :] = jnp.where(easterly, pltpu.roll(far, MARGIN, 1), near)
            send_west[pl.ds(r, TILE), :] = jnp.where(easterly, near, pltpu.roll(far, LANES - MARGIN, 1))
        return carry

    def finish_loads():
        if other_rows:
            loaded(1, other_row, other_rows)
            lax.fori_loop(other_row // TILE, other_row // TILE + other_rows // TILE, make_ocean, 0)

    def pack_rows():
        for k in range(fields // 2):
            for c in range(slots):
                send_north[k, c, 0:half, :] = field[2 * k, c, rows + half : rows + TILE, :]
                send_north[k, c, half:TILE, :] = field[2 * k + 1, c, rows + half : rows + TILE, :]
                send_south[k, c, 0:half, :] = field[2 * k, c, TILE : TILE + half, :]
                send_south[k, c, half:TILE, :] = field[2 * k + 1, c, TILE : TILE + half, :]

    def send_halos():
        pack_rows()
        all_here()

        @pl.when(has_north)
        def _():
            for copy in north:
                copy.start()

        @pl.when(has_south)
        def _():
            for copy in south:
                copy.start()

        for copy in sideways:
            copy.start()

    def south_rows():
        @pl.when(has_south)
        def _():
            north[0].wait_recv()

        @pl.when(jnp.logical_not(has_south))
        def _():
            from_south[...] = jnp.zeros_like(from_south)

        for k in range(fields // 2):
            for c in range(slots):
                field[2 * k, c, half:TILE, :] = from_south[k, c, 0:half, :]
                field[2 * k + 1, c, half:TILE, :] = from_south[k, c, half:TILE, :]
                field[2 * k, c, 0:half, :] = from_south[k, c, 0:half, :]
                field[2 * k + 1, c, 0:half, :] = from_south[k, c, half:TILE, :]

    def north_rows():
        @pl.when(has_north)
        def _():
            south[0].wait_recv()

        @pl.when(jnp.logical_not(has_north))
        def _():
            from_north[...] = jnp.zeros_like(from_north)

        base = rows + TILE
        for k in range(fields // 2):
            for c in range(slots):
                field[2 * k, c, base : base + half, :] = from_north[k, c, 0:half, :]
                field[2 * k + 1, c, base : base + half, :] = from_north[k, c, half:TILE, :]
                field[2 * k, c, base + half : base + TILE, :] = from_north[k, c, 0:half, :]
                field[2 * k + 1, c, base + half : base + TILE, :] = from_north[k, c, half:TILE, :]

    def join_middle(order, back=False):
        now = pl.ds(pl.multiple_of(tall_of(order) * TILE, TILE), TILE)
        for f in range(fields):
            field[f, halo, now, :] = jnp.where(low_lanes, field[f, slots - 1, now, :], field[f, 0, now, :])

    def join_halo(order, back):
        now = pl.ds(pl.multiple_of(tall_of(order, back) * TILE, TILE), TILE)
        east, west = from_east[now, :], from_west[now, :]
        both = [
            jnp.where(easterly, east, west),
            jnp.where(easterly, pltpu.roll(east, MARGIN, 1), pltpu.roll(west, LANES - MARGIN, 1)),
        ]
        for f in range(fields):
            g, s = divmod(f * 2 * MARGIN, LANES)
            field[f, halo, now, :] = pltpu.roll(both[g], LANES - s - MARGIN, 1)

    class Ring:
        def __init__(self, ring, todo):
            self.todo = todo
            size = len(ring)
            place = {c: i for i, c in enumerate(ring)}
            self.east = {c: ring[(place[c] + 1) % size] for c in todo}
            self.west = {c: ring[(place[c] - 1) % size] for c in todo}
            self.used = sorted(set(todo) | set(self.east.values()) | set(self.west.values()))

        def sides(self, q):
            to_east = {c: pltpu.roll(q[c], LANES - 1, 1) for c in {*self.todo, *self.east.values()}}
            to_west = {c: pltpu.roll(q[c], 1, 1) for c in {*self.todo, *self.west.values()}}
            e = {c: jnp.where(lane == LANES - 1, to_east[self.east[c]], to_east[c]) for c in self.todo}
            w = {c: jnp.where(lane == 0, to_west[self.west[c]], to_west[c]) for c in self.todo}
            return e, w

    def surface_rows(src, dst, ring, r):
        now, above_r, below_r = pl.ds(r, TILE), pl.ds(r + 1, TILE), pl.ds(r - 1, TILE)

        def add_up(base, c, where):
            total = src[base, c, where, :]
            for k in range(1, LEV):
                total = total + src[base + k, c, where, :]
            return total

        e, w = ring.sides({c: add_up(1, c, now) for c in ring.used})
        for c in ring.todo:
            n, s = add_up(1 + LEV, c, above_r), add_up(1 + LEV, c, below_r)
            divergence = (e[c] - w[c]) + (n - s)
            dst[c, now, :] = field[OCEAN, c, now, :] * (
                src[0, c, now, :] - (divergence_gain / LEV) * field[DEPTH, c, now, :] * divergence
            )

    def update_rows(src, surface, ring, r, write):
        now, above_r, below_r = pl.ds(r, TILE), pl.ds(r + 1, TILE), pl.ds(r - 1, TILE)
        h = {c: surface[c, now, :] for c in ring.used}
        e, w = ring.sides(h)
        slope_east, slope_north = {}, {}
        for c in ring.todo:
            slope_east[c] = pressure_gain * (e[c] - w[c])
            slope_north[c] = pressure_gain * (surface[c, above_r, :] - surface[c, below_r, :])
            write(0, c, h[c])
        for k in range(LEV):
            iu, iv, ic = 1 + k, 1 + LEV + k, 1 + 2 * LEV + k
            u = {c: src[iu, c, now, :] for c in ring.used}
            v = {c: src[iv, c, now, :] for c in ring.used}
            t = {c: src[ic, c, now, :] for c in ring.used}
            ue, uw = ring.sides(u)
            ve, vw = ring.sides(v)
            te, tw = ring.sides(t)
            for c in ring.todo:
                ocean = field[OCEAN, c, now, :]
                rotation = field[ROT, c, now, :]
                mixing = field[DIFF + k, c, now, :]
                tn, ts = src[ic, c, above_r, :], src[ic, c, below_r, :]
                heat_east, heat_north = te[c] - tw[c], tn - ts
                around_u = (ue[c] + uw[c]) + (src[iu, c, above_r, :] + src[iu, c, below_r, :])
                around_v = (ve[c] + vw[c]) + (src[iv, c, above_r, :] + src[iv, c, below_r, :])
                around_t = (te[c] + tw[c]) + (tn + ts)
                new_u = ocean * (
                    u[c] + rotation * v[c] - slope_east[c] - buoyancy_gain * heat_east
                    + mixing * (around_u - 4.0 * u[c])
                )
                new_v = ocean * (
                    v[c] - rotation * u[c] - slope_north[c] - buoyancy_gain * heat_north
                    + mixing * (around_v - 4.0 * v[c])
                )
                new_t = ocean * (
                    t[c] + mixing * (around_t - 4.0 * t[c])
                    - advection_gain * (new_u * heat_east + new_v * heat_north)
                )
                write(iu, c, new_u)
                write(iv, c, new_v)
                write(ic, c, new_t)

    def run_pass(join, one, two, own, own_slots, at_order, leave, back=False):
        step = jnp.where(down ^ back, -1, 1)

        def body(i, carry):
            j = i - 1
            at_order(j)
            join(j + 2, back)
            r = jnp.where(down ^ back, rows - TILE * j, TILE + TILE * j)
            surface_rows(field, surface_one, one, r + 3 * step)
            r_one = r + 2 * step

            def middle_write(channel, c, new):
                middle[channel, c, pl.ds(r_one, TILE), :] = new

            update_rows(field, surface_one, one, r_one, middle_write)
            surface_rows(middle, surface_two, one, r + step)

            @pl.when(j >= 0)
            def _():
                order = jnp.where(back, tiles - 1 - j, j)
                t = tile_of(order)

                def last_write(channel, c, new):
                    own[t, channel, own_slots[c]] = new

                update_rows(
                    middle, surface_two, two, pl.multiple_of(r, TILE), last_write
                )
                leave(order, t)

            return carry

        lax.fori_loop(0, tiles + 1, body, 0)

    def pair_copy(ref, kind, t):
        return pltpu.make_async_remote_copy(
            src_ref=ref.at[t], dst_ref=ref.at[t],
            send_sem=pair_send.at[kind], recv_sem=take_recv.at[kind, t],
            device_id=to_member(me + 1), device_id_type=MESH,
        )

    def next_copy(ref, kind, t):
        return pltpu.make_async_remote_copy(
            src_ref=ref.at[t], dst_ref=ref.at[t],
            send_sem=next_send.at[kind], recv_sem=take_recv.at[kind, t],
            device_id=to_member(me + 2), device_id_type=MESH,
        )

    last_tile = tile_of(tiles - 1)

    def last_copy(begin, end, send, recv, other):
        part = control_rim.at[last_tile, begin:end]
        return pltpu.make_async_remote_copy(
            src_ref=part, dst_ref=part, send_sem=send, recv_sem=recv,
            device_id=to_member(other), device_id_type=MESH,
        )

    first_half = [0, split]
    second_half = [split, channels]

    def last_first(send, other):
        return last_copy(*first_half, send, take_recv.at[1, last_tile], other)

    def last_second(send, other):
        return last_copy(*second_half, send, last_recv, other)

    def send_second():
        @pl.when(has_next)
        def _():
            last_second(next_send.at[1], me + 2).start()

        @pl.when(has_far)
        def _():
            last_second(far_send, me + 3).start()

    def lend_copy(own, lent, kind, early, which, order):
        return pltpu.make_async_remote_copy(
            src_ref=own.at[tile_of(order)], dst_ref=lent.at[which, order - early],
            send_sem=lend_send.at[kind], recv_sem=lend_recv.at[kind, which],
            device_id=to_member(lender), device_id_type=MESH,
        )

    def lend_whole(own, lent, kind, early, which):
        return pltpu.make_async_remote_copy(
            src_ref=own.at[0 : tiles - early], dst_ref=lent.at[which, 0 : tiles - early],
            send_sem=lend_send.at[kind], recv_sem=lend_recv.at[kind, which],
            device_id=to_member(lender), device_id_type=MESH,
        )

    def leave_mid(order, t):
        @pl.when(me == 0)
        def _():
            for k in range(channels):
                for n in range(len(mids)):
                    control_mid[t, k, n] = own_mid[t, k, n]
            pair_copy(control_mid, 0, t).start()

            @pl.when(has_next & (order < mids_cut))
            def _():
                next_copy(control_mid, 0, t).start()

        @pl.when((me > 1) & (order >= mids_cut))
        def _():
            lend_copy(own_mid, lent_mid, 0, mids_early, client, order).start()

    def leave_rim(order, t):
        @pl.when(me == 0)
        def _():
            for k in range(channels):
                for n in range(len(rims)):
                    control_rim[t, k, n] = own_rim[t, k, n]
            pair_copy(control_rim, 1, t).start()

            @pl.when(has_next & (order == rims_early))
            def _():
                def body(late, carry):
                    next_copy(control_mid, 0, tile_of(late)).start()
                    return carry

                lax.fori_loop(mids_cut, tiles, body, 0)

            @pl.when(has_next & (order < tiles - 1))
            def _():
                next_copy(control_rim, 1, t).start()

            @pl.when(order == tiles - 1)
            def _():
                @pl.when(has_next)
                def _():
                    last_first(next_send.at[1], me + 2).start()

                send_second()

        @pl.when((me > 1) & (order >= rims_early))
        def _():
            lend_copy(own_rim, lent_rim, 1, rims_early, client, order).start()

    def start_rows():
        @pl.when(down)
        def _():
            north_rows()

        @pl.when(jnp.logical_not(down))
        def _():
            south_rows()

    def end_rows():
        @pl.when(down)
        def _():
            south_rows()

        @pl.when(jnp.logical_not(down))
        def _():
            north_rows()

    load_at = min(first_tiles - 1, tiles - 1)
    per = -(-blocks // PACK_STEPS)
    pack_at = max(load_at, PACK_AT)
    send_at = pack_at + PACK_STEPS
    ahead = lats > 2 or send_at > tiles - 2

    def events_mid(j):
        if not ahead:
            @pl.when(j == load_at)
            def _():
                finish_loads()

            @pl.when((j >= pack_at) & (j < send_at))
            def _():
                begin = (j - pack_at) * per
                lax.fori_loop(begin, jnp.minimum(begin + per, blocks), pack_block, 0)

            @pl.when(j == send_at)
            def _():
                send_halos()

        @pl.when(j == tiles - 1)
        def _():
            end_rows()

    if ahead:
        finish_loads()
        lax.fori_loop(0, blocks, pack_block, 0)
        send_halos()
    start_rows()
    join_middle(0)
    ring_mid = mids + [halo]
    run_pass(
        join_middle, Ring(ring_mid, ring_mid), Ring(ring_mid, mids),
        own_mid, {c: n for n, c in enumerate(mids)}, events_mid, leave_mid,
    )

    for copy in sideways:
        copy.wait_recv()

    @pl.when(has_north)
    def _():
        for copy in south[1:]:
            copy.wait_recv()

    @pl.when(has_south)
    def _():
        for copy in north[1:]:
            copy.wait_recv()

    @pl.when(jnp.logical_not(has_north))
    def _():
        from_east[above, :] = zero_tile
        from_west[above, :] = zero_tile

    @pl.when(jnp.logical_not(has_south))
    def _():
        from_east[first, :] = zero_tile
        from_west[first, :] = zero_tile

    back = me > 1
    join_halo(0, back)
    ring_all = list(range(slots)) + [halo]
    run_pass(
        join_halo, Ring(ring_all, [slots - 1, halo, 0]), Ring(ring_all, rims),
        own_rim, {c: n for n, c in enumerate(rims)}, lambda j: None, leave_rim, back,
    )

    def clear(ref):
        for k in range(regions):
            ref[k] = zero_tile

    def ids_at(t, c):
        return region[pl.ds(pl.multiple_of(t * TILE, TILE), TILE), c * LANES : (c + 1) * LANES]

    def ocean_at(t, c):
        return field[OCEAN, c, pl.ds(pl.multiple_of(t * TILE + TILE, TILE), TILE), :]

    def add_regions(ref, items):
        for k in range(regions):
            total = ref[k]
            for ids, amount in items:
                total = total + jnp.where(ids == k, amount, 0.0)
            ref[k] = total

    def compare(ref, mine, its, t, part):
        items = []
        for n, c in enumerate(part):
            total = None
            for k in range(channels):
                d = mine(k, n) - its(k, n)
                total = d * d if total is None else total + d * d
            items.append((ids_at(t, c), ocean_at(t, c) * total))
        add_regions(ref, items)

    def share(which):
        for p, (a, b) in enumerate(peers):
            pltpu.make_async_remote_copy(
                src_ref=gathered.at[which, 0], dst_ref=gathered.at[which, p + 1],
                send_sem=sum_send.at[which], recv_sem=sum_recv.at[which],
                device_id=at(a, b), device_id_type=MESH,
            ).start()

    def collect(which):
        others = gathered.at[which, 1 : len(peers) + 1]
        pltpu.make_async_remote_copy(
            src_ref=others, dst_ref=others, send_sem=sum_send.at[which], recv_sem=sum_recv.at[which],
            device_id=at(*peers[0]), device_id_type=MESH,
        ).wait()
        total = gathered[which, 0]
        for p in range(len(peers)):
            total = total + gathered[which, p + 1]
        return jnp.sum(total, axis=1, keepdims=True)

    load_region.wait()
    clear(squares)
    clear(counts)

    def count(t, carry):
        add_regions(counts, [(ids_at(t, c), ocean_at(t, c)) for c in range(slots)])
        return carry

    lax.fori_loop(0, tiles, count, 0)
    gathered[0, 0] = jnp.sum(counts[...], axis=1)
    share(0)

    kinds = [
        (0, own_mid, control_mid, lent_mid, mids, mids_early),
        (1, own_rim, control_rim, lent_rim, rims, rims_early),
    ]

    def take(kind, order):
        _, own, control, _, part, _ = kinds[kind]
        t = tile_of(order)

        @pl.when(even)
        def _():
            next_copy(control, kind, t).wait_recv()

            @pl.when(has_pair)
            def _():
                pair_copy(control, kind, t).start()

            @pl.when(has_next)
            def _():
                next_copy(control, kind, t).start()

        @pl.when(jnp.logical_not(even))
        def _():
            pair_copy(control, kind, t).wait_recv()

    def weigh(kind, order):
        _, own, control, _, part, _ = kinds[kind]
        t = tile_of(order)
        compare(squares, lambda k, n: own[t, k, n], lambda k, n: control[t, k, n], t, part)

    def loop(begin, end, *actions):
        def body(order, carry):
            for action in actions:
                action(order)
            return carry

        lax.fori_loop(begin, end, body, 0)

    @pl.when(me > 0)
    def _():
        late_mids = jnp.where(me == 1, tiles, mids_cut)
        late_rims = jnp.where(me == 1, tiles, rims_early)
        loop(0, mids_cut, lambda o: take(0, o), lambda o: weigh(0, o))
        loop(0, late_rims, lambda o: take(1, o), lambda o: weigh(1, o))
        loop(mids_cut, late_mids, lambda o: take(0, o), lambda o: weigh(0, o))

    def loan_copy(other, which):
        return pltpu.make_async_remote_copy(
            src_ref=loan_out.at[which], dst_ref=loan,
            send_sem=loan_send.at[which], recv_sem=loan_recv,
            device_id=to_member(other), device_id_type=MESH,
        )

    def lend(which, other):
        clear(lent_squares)
        for kind, own, control, lent, part, early in kinds:
            if early == tiles:
                continue

            def body(order, carry):
                t = tile_of(order)
                compare(
                    lent_squares,
                    lambda k, n: lent[which, order - early, k, n],
                    lambda k, n: control[t, k, n], t, part,
                )
                return carry

            @pl.when(late_here | (kind == 1))
            def _():
                lend_whole(own, lent, kind, early, which).wait_recv()
                lax.fori_loop(early, tiles, body, 0)

        loan_out[which] = jnp.sum(lent_squares[...], axis=1)
        loan_copy(other, which).start()

    gathered[1, 0] = jnp.sum(squares[...], axis=1)

    @pl.when(me == 1)
    def _():
        for which in range(clients):
            lend(which, which + 2)

    @pl.when(me > 1)
    def _():
        loan_copy(me, 0).wait_recv()
        gathered[1, 0] = gathered[1, 0] + loan[...]

    share(1)
    taken = min(rims_early + TAKE_FIRST, tiles - 1)

    @pl.when(me > 1)
    def _():
        loop(mids_cut, tiles, lambda o: take(0, o))
        loop(rims_early, taken, lambda o: take(1, o))

    count_sum = collect(0)
    square_sum = collect(1)
    growth = jnp.sqrt(square_sum / (count_sum * channels) + epsilon)
    growth_wide = jnp.broadcast_to(growth, (regions, LANES))
    growth_out[...] = growth_wide
    load_target.wait()
    for k in range(regions):
        value[k] = jnp.broadcast_to(target[k] / growth_wide[k : k + 1, :], (TILE, LANES))

    def make_factor(b, carry):
        for i in range(block):
            t = b * block + i
            for c in range(slots):
                ids = ids_at(t, c)
                total = zero_tile
                for k in range(regions):
                    total = jnp.where(ids == k, value[k], total)
                factor[t, c] = total
        return carry

    lax.fori_loop(0, blocks, make_factor, 0)

    def breed(kind, order):
        _, own, control, _, part, _ = kinds[kind]
        t = tile_of(order)
        now = pl.ds(pl.multiple_of(t * TILE, TILE), TILE)
        for n, c in enumerate(part):
            scale = factor[t, c]
            for k in range(channels):
                base = control[t, k, n]
                bred[k, now, c * LANES : (c + 1) * LANES] = base + scale * (own[t, k, n] - base)

    def take_late(kind, order):
        @pl.when(me > 1)
        def _():
            take(kind, order)

    def breed_block(b, carry):
        for i in range(block):
            breed(0, b * block + i)
        return carry

    lax.fori_loop(0, blocks, breed_block, 0)
    loop(0, rims_early, lambda o: breed(1, o))
    loop(rims_early, taken, lambda o: breed(1, o))
    loop(taken, tiles - 1, lambda o: take_late(1, o), lambda o: breed(1, o))

    @pl.when(me > 1)
    def _():
        last_first(half_send, me).wait_recv()

        @pl.when(has_pair)
        def _():
            last_first(half_send, me + 1).start()

        @pl.when(has_next)
        def _():
            last_first(next_send.at[1], me + 2).start()

        last_second(far_send, me).wait_recv()
        send_second()

    breed(1, tiles - 1)

    for copy in sideways:
        copy.wait_send()

    @pl.when(has_north)
    def _():
        for copy in north:
            copy.wait_send()

    @pl.when(has_south)
    def _():
        for copy in south:
            copy.wait_send()

    for kind, own, control, lent, part, early in kinds:
        def whole_control(send, other, part=control):
            return pltpu.make_async_remote_copy(
                src_ref=part, dst_ref=part, send_sem=send.at[kind], recv_sem=take_recv.at[kind, 0],
                device_id=to_member(other), device_id_type=MESH,
            )

        @pl.when(me == 0)
        def _():
            whole_control(pair_send, 1).wait_send()

        @pl.when(has_pair & (me > 1))
        def _():
            if kind == 0:
                whole_control(pair_send, me + 1).wait_send()
            else:
                whole_control(pair_send, me + 1, control.at[0 : tiles - 1]).wait_send()
                last_first(half_send, me + 1).wait_send()

        @pl.when(has_next)
        def _():
            whole_control(next_send, me + 2).wait_send()

    @pl.when(has_far)
    def _():
        last_second(far_send, me + 3).wait_send()

    @pl.when(me == 1)
    def _():
        for which in range(clients):
            loan_copy(which + 2, which).wait_send()

    @pl.when(me > 1)
    def _():
        for kind, own, control, lent, part, early in kinds:
            if early < tiles:
                @pl.when(late_here | (kind == 1))
                def _():
                    lend_whole(own, lent, kind, early, client).wait_send()


def write_kernel(bred_in, growth_in, bred, growth, out_sem):
    copy = pltpu.make_async_copy(bred_in, bred, out_sem)
    copy.start()
    shape = growth_in.shape
    diagonal = lax.broadcasted_iota(jnp.int32, shape, 0) == lax.broadcasted_iota(jnp.int32, shape, 1)
    line = jnp.sum(jnp.where(diagonal, growth_in[...], 0.0), axis=0, keepdims=True)
    growth[...] = line[:, 0 : growth.shape[1]]
    copy.wait()


def per_device(
    sizes, member_state, column_depth, rotation, diffusivity, ocean_mask, region_id, target_rms
):
    members, lons, lats = sizes
    _, channels, rows, columns = member_state.shape
    regions = target_rms.shape[0]
    fields = channels + 3 + LEV
    tall = rows + 2 * TILE
    tiles = rows // TILE
    slots = columns // LANES
    group = lons * lats
    clients = max(members - 2, 1)
    late_mids = max(tiles - MIDS_EARLY, 1)
    late_rims = max(tiles - RIMS_EARLY, 1)
    f32 = jnp.float32
    anywhere = pl.BlockSpec(memory_space=pl.ANY)
    resident = pl.BlockSpec(memory_space=pltpu.VMEM)
    piece_mid = (channels, slots - 2, TILE, LANES)
    piece_rim = (channels, 2, TILE, LANES)
    bred, growth_wide = pl.pallas_call(
        functools.partial(cycle_kernel, sizes),
        out_shape=(
            pltpu.VMEM((channels, rows, columns), f32),
            pltpu.VMEM((regions, LANES), f32),
        ),
        in_specs=[anywhere] * 7,
        out_specs=(resident,) * 2,
        scratch_shapes=[
            pltpu.VMEM((fields, slots + 1, tall, LANES), f32),
            pltpu.VMEM((channels, slots + 1, tall, LANES), f32),
            pltpu.VMEM((slots + 1, tall, LANES), f32),
            pltpu.VMEM((slots + 1, tall, LANES), f32),
            pltpu.VMEM((tiles,) + piece_mid, f32),
            pltpu.VMEM((tiles,) + piece_rim, f32),
            pltpu.VMEM((tiles,) + piece_mid, f32),
            pltpu.VMEM((tiles,) + piece_rim, f32),
            pltpu.VMEM((clients, late_mids) + piece_mid, f32),
            pltpu.VMEM((clients, late_rims) + piece_rim, f32),
            pltpu.VMEM((rows, LANES), f32),
            pltpu.VMEM((rows, LANES), f32),
            pltpu.VMEM((tall, LANES), f32),
            pltpu.VMEM((tall, LANES), f32),
            pltpu.VMEM((fields // 2, slots, TILE, LANES), f32),
            pltpu.VMEM((fields // 2, slots, TILE, LANES), f32),
            pltpu.VMEM((fields // 2, slots, TILE, LANES), f32),
            pltpu.VMEM((fields // 2, slots, TILE, LANES), f32),
            pltpu.VMEM((rows, columns), jnp.int32),
            pltpu.VMEM((rows, columns), jnp.int32),
            pltpu.VMEM((regions, TILE, LANES), f32),
            pltpu.VMEM((regions, TILE, LANES), f32),
            pltpu.VMEM((regions, TILE, LANES), f32),
            pltpu.VMEM((2, group, regions, LANES), f32),
            pltpu.VMEM((clients, regions, LANES), f32),
            pltpu.VMEM((regions, LANES), f32),
            pltpu.VMEM((regions, TILE, LANES), f32),
            pltpu.VMEM((tiles, slots, TILE, LANES), f32),
            pltpu.SMEM((regions,), f32),
            pltpu.SemaphoreType.DMA((4,)),
            pltpu.SemaphoreType.DMA((8,)),
            pltpu.SemaphoreType.DMA((8,)),
            pltpu.SemaphoreType.DMA((2,)),
            pltpu.SemaphoreType.DMA((2,)),
            pltpu.SemaphoreType.DMA((2, tiles)),
            pltpu.SemaphoreType.DMA((2,)),
            pltpu.SemaphoreType.DMA((2, clients)),
            pltpu.SemaphoreType.DMA((clients,)),
            pltpu.SemaphoreType.DMA,
            pltpu.SemaphoreType.DMA((2,)),
            pltpu.SemaphoreType.DMA((2,)),
            pltpu.SemaphoreType.REGULAR,
            pltpu.SemaphoreType.DMA,
            pltpu.SemaphoreType.DMA,
            pltpu.SemaphoreType.DMA,
        ],
        compiler_params=pltpu.CompilerParams(
            collective_id=0, has_side_effects=True, vmem_limit_bytes=KERNEL_BYTES
        ),
    )(
        member_state.reshape(channels, rows, columns),
        column_depth, rotation, diffusivity, ocean_mask, region_id, target_rms,
    )
    bred, growth = pl.pallas_call(
        write_kernel,
        out_shape=(
            jax.ShapeDtypeStruct((channels, rows, columns), f32),
            jax.ShapeDtypeStruct((1, regions), f32),
        ),
        in_specs=[resident, resident],
        out_specs=(anywhere, resident),
        scratch_shapes=[pltpu.SemaphoreType.DMA],
        compiler_params=pltpu.CompilerParams(vmem_limit_bytes=WRITE_BYTES),
    )(bred, growth_wide)
    return (bred[None], growth)


def solution(mesh):
    sizes = (mesh.shape["member"], mesh.shape["lon"], mesh.shape["lat"])
    return jax.shard_map(
        functools.partial(per_device, sizes),
        mesh=mesh,
        in_specs=(
            P("member", None, "lat", "lon"),
            P("lat", "lon"),
            P("lat", "lon"),
            P(None, "lat", "lon"),
            P("lat", "lon"),
            P("lat", "lon"),
            P(),
        ),
        out_specs=(P("member", None, "lat", "lon"), P("member", None)),
        check_vma=False,
    )
```
